256 devices in a mesh: dp: 4 (over x_lo, core), ctx: 64 (over x_hi, z, y).
Axes of the slice: x: 4 (x_hi: 2, x_lo: 2; x = x_hi * 2 + x_lo), y: 4, z: 8, core: 2. Of those that a mesh axis runs over, the one named last changes fastest.
Arguments:
- inputs: bfloat16 [4, 8192, 2048], P('dp', 'ctx'), may hold values from -6 to 6
- b_proj: bfloat16 [4, 8192, 64], P('dp', 'ctx'), may hold values from -0.75 to 0.75
- c_proj: bfloat16 [4, 8192, 64], P('dp', 'ctx'), may hold values from -6 to 6
- step_sizes: float32 [4, 32, 8192], P('dp', None, 'ctx'), may hold values from 0.0001 to 0.37
- a_log: float32 [32], replicated, may hold values from -8 to -1.7
- skip_gain: float32 [32], replicated, may hold values from 0.5 to 1.5
- doc_lengths: int32 [4, 16], P('dp'), may hold values from 1 to 2048, 8192 in all within a row
- grad_out: bfloat16 [4, 8192, 2048], P('dp', 'ctx'), may hold values from -6 to 6
Outputs:
- input_grads: bfloat16 [4, 8192, 2048], P('dp', 'ctx')
- b_gradient: bfloat16 [4, 8192, 64], P('dp', 'ctx')
- c_gradient: bfloat16 [4, 8192, 64], P('dp', 'ctx')
- step_grads: float32 [4, 32, 8192], P('dp', None, 'ctx')
- alog_grads: float32 [32], replicated
- skip_grads: float32 [32], replicated
The draws below stay inside these ranges and needn't reach their ends.
Inputs may be any that keep to these rules, and one draw needn't show every extreme that they name: `doc_lengths`: each row holds the 16 document lengths of one packed sequence, in order, summing to 8192; the longest is exactly 2048.
All inputs are finite; a program needn't handle non-finite values.
Results may differ from the reference program's by a relative error of at most 0.0012.
Values sent between devices are 32-bit elements; how exact they have to be, the bound alone decides.
A program may use at most 256 MiB of HBM per device.

```python
import math
import jax
import jax.numpy as jnp
import numpy as np
from jax import lax

H = 32
P_SIZE = 64
N = 64
GROUP = 128
DOCS = 16
LENGTH = 8192
BATCH = 4
MOST_DOC = 2048


def head_rates(key):
    base_key = jax.random.fold_in(key, 101)
    slow_share = 0.5
    chooser = jax.random.uniform(jax.random.fold_in(base_key, 1), (H,), jnp.float32)
    slow_rates = jnp.exp(jax.random.uniform(jax.random.fold_in(base_key, 2), (H,), jnp.float32, jnp.log(0.25), jnp.log(2.0))) / MOST_DOC
    fast_rates = jnp.exp(jax.random.uniform(jax.random.fold_in(base_key, 3), (H,), jnp.float32, jnp.log(1.0 / 50.0), jnp.log(1.0 / 30.0)))
    return jnp.where(chooser < slow_share, slow_rates, fast_rates)


def draw_a_log(key, part):
    return 0.5 * jnp.log(head_rates(key))


def draw_step_sizes(key, part):
    head_rate = head_rates(key)
    roughness = jnp.exp(jax.random.uniform(jax.random.fold_in(key, 202), (BATCH, H, LENGTH), jnp.float32, -0.6931, 0.6931))
    return jnp.sqrt(head_rate)[None, :, None] * roughness


def block_scale(rng, dims, cuts, low, largest):
    gain, own = 1.0, jax.random.fold_in(rng, 6)
    for position, blocks in cuts:
        heights = jnp.exp(jax.random.uniform(jax.random.fold_in(own, position), (blocks,), jnp.float32, low / len(cuts), largest / len(cuts)))
        gain = gain * jnp.repeat(heights, dims[position] // blocks).reshape([-1 if axis == position else 1 for axis in range(len(dims))])
    return gain


def length_profile(count, total, bound, lean):
    weights = [(1 << 20) // math.isqrt(grade ** lean) + 1 for grade in range(2, count + 1)]
    rest, given = total - bound - (count - 1), [1] * (count - 1)
    while rest > 0:
        free = [i for i in range(count - 1) if given[i] < bound]
        pool, left = sum([weights[i] for i in free]), rest
        for i in free:
            addition = min(bound - given[i], max(1, left * weights[i] // pool), rest)
            given[i] = given[i] + addition
            rest = rest - addition
    return np.array([bound] + given)


def uneven(key, count, total, most, slope):
    if count == 2:
        one = jax.random.randint(key, (), max(1, total - most), min(most, total - 1) + 1)
        return jnp.stack([one, total - one])
    sizes = jnp.asarray(length_profile(count, total, most, slope), jnp.int32)
    pairs = (count - 1) // 2
    giver, sink = sizes[1:1 + 2 * pairs:2], sizes[2:2 + 2 * pairs:2]
    margin = jnp.minimum(giver - 1, most - sink)
    passed = jax.random.randint(jax.random.fold_in(key, 1), (pairs,), 0, 1 << 20) % (margin + 1)
    sizes = sizes.at[1:1 + 2 * pairs:2].set(giver - passed).at[2:2 + 2 * pairs:2].set(sink + passed)
    return sizes[jax.random.permutation(jax.random.fold_in(key, 2), count)]


def normal_values(own_key, extent, deviation, reach, split=(), kind=jnp.bfloat16):
    entries = deviation * jax.random.normal(own_key, extent, jnp.float32)
    if split:
        entries = entries * block_scale(own_key, extent, split, -0.22, 0.18)
    return jnp.clip(entries, -reach, reach).astype(kind)


def setup_inputs(seed: int = 0) -> dict:
    keys = jax.random.split(jax.random.key(seed), 9)
    inputs = normal_values(keys[0], (BATCH, LENGTH, H * P_SIZE), 1.0, 6.0, ((0, 4), (1, 64)))
    b_proj = normal_values(keys[1], (BATCH, LENGTH, N), N ** -0.5, 0.75, ((0, 4), (1, 64)))
    c_proj = normal_values(keys[2], (BATCH, LENGTH, N), 1.0, 6.0, ((0, 4), (1, 64)))
    step_sizes = draw_step_sizes(jax.random.fold_in(keys[8], 71), 0)
    a_log = draw_a_log(jax.random.fold_in(keys[8], 71), 0)
    skip_gain = jnp.clip(jax.random.uniform(keys[5], (H,), jnp.float32, 0.5, 1.5), 0.5, 1.5)
    doc_lengths = jax.vmap(lambda own: uneven(own, DOCS, LENGTH, MOST_DOC, 2))(jax.random.split(keys[6], BATCH)).reshape((BATCH, DOCS)).astype(jnp.int32)
    grad_out = normal_values(keys[7], (BATCH, LENGTH, H * P_SIZE), 1.0, 6.0, ((0, 4), (1, 64)))
    return {"inputs": inputs, "b_proj": b_proj, "c_proj": c_proj, "step_sizes": step_sizes, "a_log": a_log, "skip_gain": skip_gain, "doc_lengths": doc_lengths, "grad_out": grad_out}


very_negative = -1e+30
highest = lax.Precision.HIGHEST

def segment_ids(lengths, offset, row_count):
    starts = jnp.cumsum(lengths) - lengths
    places = offset + jnp.arange(row_count, dtype=jnp.int32)
    return lax.optimization_barrier(jnp.sum((starts[None, :] <= places[:, None]).astype(jnp.int32), axis=1)) - 1

def decay_logs(deltas, rate_log):
    return deltas * (-jnp.exp(rate_log))[:, None]

def intra_group(values, bvectors, cvectors, deltas, rate_log, segment):
    cumulated = jnp.cumsum(decay_logs(deltas, rate_log), axis=1)
    spread = cumulated[:, :, None] - cumulated[:, None, :]
    places = jnp.arange(segment.shape[0])
    allowed = (places[:, None] >= places[None, :]) & (segment[:, None] == segment[None, :])
    kernel = jnp.exp(jnp.where(allowed[None], spread, very_negative))
    scores = jnp.dot(cvectors, bvectors.T, precision=highest)
    weights = kernel * scores[None] * deltas[:, None, :]
    return jnp.einsum('hts,shp->thp', weights, values, precision=highest)

def group_cross(values, bvectors, cvectors, deltas, rate_log, segment, before, incoming):
    cumulated = jnp.cumsum(decay_logs(deltas, rate_log), axis=1)
    living = (segment == before).astype(cumulated.dtype)
    carried = jnp.exp(cumulated) * living[None, :]
    readout = jnp.einsum('tn,hpn->thp', cvectors, incoming, precision=highest) * jnp.transpose(carried)[:, :, None]
    ending = (segment == segment[-1]).astype(cumulated.dtype)
    keeping = jnp.exp(cumulated[:, -1:] - cumulated) * deltas * ending[None, :]
    weighted = values * jnp.transpose(keeping)[:, :, None]
    fresh_part = jnp.einsum('shp,sn->hpn', weighted, bvectors, precision=highest)
    return (readout, carried[:, -1][:, None, None] * incoming + fresh_part)

def intra_run(values, bvectors, cvectors, deltas, rate_log, segment):
    row_count = values.shape[0]
    group_count = row_count // GROUP
    pieces = (values.reshape(group_count, GROUP, values.shape[1], values.shape[2]), bvectors.reshape(group_count, GROUP, bvectors.shape[1]), cvectors.reshape(group_count, GROUP, cvectors.shape[1]), jnp.transpose(deltas.reshape(deltas.shape[0], group_count, GROUP), (1, 0, 2)), segment.reshape(group_count, GROUP))

    def within(pieces_now):
        return intra_group(pieces_now[0], pieces_now[1], pieces_now[2], pieces_now[3], rate_log, pieces_now[4])
    outcome = lax.map(jax.checkpoint(within), pieces)
    return outcome.reshape(row_count, values.shape[1], values.shape[2])

def cross_run(values, bvectors, cvectors, deltas, rate_log, segment, before, incoming):
    row_count = values.shape[0]
    group_count = row_count // GROUP
    befores = jnp.concatenate([jnp.reshape(before, (1,)).astype(jnp.int32), segment[GROUP - 1::GROUP][:-1].astype(jnp.int32)])
    pieces = (values.reshape(group_count, GROUP, values.shape[1], values.shape[2]), bvectors.reshape(group_count, GROUP, bvectors.shape[1]), cvectors.reshape(group_count, GROUP, cvectors.shape[1]), jnp.transpose(deltas.reshape(deltas.shape[0], group_count, GROUP), (1, 0, 2)), segment.reshape(group_count, GROUP), befores)

    def advance(carried_state, pieces_now):
        readout, next_state = group_cross(pieces_now[0], pieces_now[1], pieces_now[2], pieces_now[3], rate_log, pieces_now[4], pieces_now[5], carried_state)
        return (next_state, readout)
    ending_state, readout = lax.scan(jax.checkpoint(advance), incoming, pieces)
    return (readout.reshape(row_count, values.shape[1], values.shape[2]), ending_state)

def reference(inputs, b_proj, c_proj, step_sizes, a_log, skip_gain, doc_lengths, grad_out):

    def one_sequence(pieces):
        row_count = pieces[0].shape[0]
        values = pieces[0].astype(jnp.float32).reshape(row_count, H, P_SIZE)
        bvectors = pieces[1].astype(jnp.float32)
        cvectors = pieces[2].astype(jnp.float32)
        deltas = pieces[3]
        segment = segment_ids(pieces[4], jnp.int32(0), row_count)
        upstream = pieces[5].astype(jnp.float32).reshape(row_count, H, P_SIZE)
        nothing = jnp.zeros((H, P_SIZE, N), jnp.float32)
        opening = jnp.int32(-1)

        def forward(value_in, bvec_in, cvec_in, delta_in, rate_in, skip_in):
            readout, ending_state = cross_run(value_in, bvec_in, cvec_in, delta_in, rate_in, segment, opening, nothing)
            return intra_run(value_in, bvec_in, cvec_in, delta_in, rate_in, segment) + readout + skip_in[None, :, None] * value_in
        outcome, pullback = jax.vjp(forward, values, bvectors, cvectors, deltas, a_log, skip_gain)
        grads = pullback(upstream)
        return (grads[0].reshape(row_count, H * P_SIZE), grads[1], grads[2], grads[3], grads[4], grads[5])
    gradients = lax.map(one_sequence, (inputs, b_proj, c_proj, step_sizes, doc_lengths, grad_out))
    return (gradients[0].astype(jnp.bfloat16), gradients[1].astype(jnp.bfloat16), gradients[2].astype(jnp.bfloat16), gradients[3], lax.optimization_barrier(jnp.sum(gradients[4], axis=0)), lax.optimization_barrier(jnp.sum(gradients[5], axis=0)))
```

```python
import functools

import jax
import jax.numpy as jnp
from jax import lax
from jax.experimental import pallas as pl
from jax.experimental.pallas import tpu as pltpu
from jax.sharding import PartitionSpec as P

MESH = pl.DeviceIdType.MESH
f32, bf16 = jnp.float32, jnp.bfloat16

MOST_DOC = 2048
RING = 4
CHUNKS = 2


def nn(a, b):
    return lax.dot_general(a, b, (((1,), (0,)), ((), ())), preferred_element_type=f32)


def nt(a, b):
    return lax.dot_general(a, b, (((1,), (1,)), ((), ())), preferred_element_type=f32)


def split(v, count):
    pieces = []
    for i in range(count):
        piece = v.astype(bf16)
        pieces.append(piece)
        if i + 1 < count:
            v = v - piece.astype(f32)
    return pieces


def kernel(
    dims,
    x_ref, g_ref, b_ref, c_ref, dt_ref, alog_ref, skip_ref, len_ref,
    dx_ref, db_ref, dc_ref, dstep_ref, dalog_ref, dskip_ref,
    xh, gh, bd, z1, z2, rowv, vecs, sa, ra, sb, rb, sc, rc, ar,
    sa_send, sa_recv, sb_send, sb_recv, sc_send, sc_recv, ar_send, ar_recv,
):
    n_dp, n_ctx, n_z, T, H, D, N, DOCS = dims
    n_x = n_ctx // (n_z * RING)
    groups = n_ctx // RING
    rounds = -(-MOST_DOC // (RING * T))
    W = H * D // (RING * CHUNKS)
    Q = H * D // RING
    dp, me = lax.axis_index("dp"), lax.axis_index("ctx")
    y, group = me % RING, me // RING
    z, xhi = group % n_z, group // n_z

    y_peers = [(d, (y + d) % RING) for d in (2, 1, 3)]
    ahead = ((group + 1) % groups) * RING + y
    behind = ((group + groups - 1) % groups) * RING + y
    z_peers = [(xhi * n_z + (z + d) % n_z) * RING + y for d in range(1, n_z)]
    fold = dp * n_x + xhi
    f_peers = []
    for d in range(1, n_dp * n_x):
        other = (fold + d) % (n_dp * n_x)
        f_peers.append((other // n_x, ((other % n_x) * n_z + z) * RING + y))

    barrier = pltpu.get_barrier_semaphore()
    greeted = [(dp, group * RING + q) for _, q in y_peers]
    greeted += [(dp, ahead), (dp, behind)]
    greeted += [(dp, p) for p in z_peers]
    greeted += f_peers
    for target in greeted:
        pl.semaphore_signal(barrier, inc=1, device_id=target, device_id_type=MESH)

    offset = me * T
    starts, total = [], jnp.int32(0)
    for d in range(DOCS):
        starts.append(total)
        total = total + len_ref[0, d]
    rows = lax.broadcasted_iota(jnp.int32, (T, T), 0)
    cols = lax.broadcasted_iota(jnp.int32, (T, T), 1)
    lane8 = lax.broadcasted_iota(jnp.int32, (8, T), 1)
    seg_r = jnp.zeros((T, T), jnp.int32)
    seg_c = jnp.zeros((8, T), jnp.int32)
    before, last = jnp.int32(0), jnp.int32(0)
    for s in starts:
        seg_r = seg_r + jnp.where(rows + offset >= s, 1, 0)
        seg_c = seg_c + jnp.where(lane8 + offset >= s, 1, 0)
        before = before + jnp.where(s <= offset - 1, 1, 0)
        last = last + jnp.where(s <= offset + T - 1, 1, 0)
    seg_c = seg_c[0:1, :]
    same = seg_r == seg_c
    allowed = jnp.logical_and(rows >= cols, same)
    allowed_t = jnp.logical_and(cols >= rows, same)
    living_col = jnp.where(seg_r == before, 1.0, 0.0)[:, :N]
    ending_col = jnp.where(seg_r == last, 1.0, 0.0)[:, :N]
    living_row = jnp.where(seg_c == before, 1.0, 0.0)
    ending_row = jnp.where(seg_c == last, 1.0, 0.0)
    through_flag = jnp.where(last == before, 1.0, 0.0)

    tril = jnp.where(rows >= cols, 1.0, 0.0).astype(bf16)
    eye = jnp.where(rows == cols, 1.0, 0.0).astype(bf16)
    dt = dt_ref[...]
    cum_dt, dt_t = jnp.zeros((T, H), f32), jnp.zeros((T, H), f32)
    for piece in split(dt, 3):
        cum_dt = cum_dt + nt(tril, piece)
        dt_t = dt_t + nt(eye, piece)
    rate = -jnp.exp(alog_ref[...])
    cum = cum_dt * rate
    alpha = jnp.exp(cum)
    beta = jnp.exp(-cum) * dt_t
    spread = jnp.concatenate(
        [
            jnp.concatenate(split(alpha, 3), axis=1),
            jnp.concatenate(split(beta, 3), axis=1),
        ],
        axis=0,
    )
    skip3 = jnp.concatenate(split(jnp.broadcast_to(skip_ref[...], (16, H)), 3), axis=1)

    def one_hot(start, width, copies):
        heads = lax.broadcasted_iota(jnp.int32, (copies * H, width), 0) % H
        lanes = lax.broadcasted_iota(jnp.int32, (copies * H, width), 1) + start
        return jnp.where(lanes // D == heads, 1.0, 0.0).astype(bf16)

    bb, cc = b_ref[...], c_ref[...]
    b32, c32 = bb.astype(f32), cc.astype(f32)
    eye_n = eye[:N, :N]
    eb_t = (nt(eye_n, bb) * ending_row).astype(bf16)
    lc_t = (nt(eye_n, cc) * living_row).astype(bf16)
    eb_t = jnp.concatenate([eb_t, eb_t], axis=1)
    lc_t = jnp.concatenate([lc_t, lc_t], axis=1)
    eb = (b32 * ending_col).astype(bf16)
    lc = (c32 * living_col).astype(bf16)
    eb = jnp.concatenate([eb, eb], axis=1)
    lc = jnp.concatenate([lc, lc], axis=1)

    sent = []
    vecs[...] = jnp.zeros_like(vecs)
    for k in range(CHUNKS):
        for q in range(RING):
            lo = q * Q + k * W
            at = slice(lo, lo + W)
            hot = one_hot(lo, W, 3)
            wide = nn(spread, hot)
            alpha_w, beta_w = wide[:T], wide[T:]
            rowv[0:8, at] = nn(skip3, hot)[0:8]
            last_alpha = jnp.broadcast_to(alpha_w[T - 1 : T], (8, W))
            rowv[8:16, at] = last_alpha
            g = g_ref[:, at].astype(f32)
            x = x_ref[:, at].astype(f32)
            vecs[1:2, at] = jnp.sum(g * x, axis=0, keepdims=True)
            g_hi, g_lo = split(g * alpha_w, 2)
            x_hi, x_lo = split(x * beta_w, 2)
            gh[0:T, at], gh[T : 2 * T, at] = g_hi, g_lo
            xh[0:T, at], xh[T : 2 * T, at] = x_hi, x_lo
            bd[:, at] = beta_w
            sa[q, k, 0:N, :] = nn(eb_t, xh[:, at]) * last_alpha[0:1]
            sa[q, k, N : 2 * N, :] = nn(lc_t, gh[:, at])
            sa[q, k, 2 * N : 2 * N + 8, :] = last_alpha * through_flag
        if k == 0:
            pl.semaphore_wait(barrier, len(greeted))
        for _, q in y_peers:
            copy = pltpu.make_async_remote_copy(
                src_ref=sa.at[q, k],
                dst_ref=ra.at[y, k],
                send_sem=sa_send.at[q, k],
                recv_sem=sa_recv.at[y, k],
                device_id=(dp, group * RING + q),
                device_id_type=MESH,
            )
            copy.start()
            sent.append(copy)
        ra[y, k] = sa[y, k]

    s_hi, s_lo = split(jnp.where(allowed, nt(cc, bb), 0.0), 2)
    t_hi, t_lo = split(jnp.where(allowed_t, nt(bb, cc), 0.0), 2)
    s_hi = jnp.concatenate([s_hi, s_hi], axis=1)
    t_hi = jnp.concatenate([t_hi, t_hi], axis=1)
    step = 512
    both = jnp.zeros((T, 2 * T), f32)
    rest = jnp.zeros((T, T), f32)
    for lo in range(0, H * D, step):
        at = slice(lo, lo + step)
        xp, gp = xh[:, at], gh[:, at]
        z2[:, at] = nn(s_hi, xp) + nn(s_lo, xp[:T])
        z1[:, at] = nn(t_hi, gp) + nn(t_lo, gp[:T])
        both = both + nt(gp[:T], xp)
        rest = rest + nt(gp[T:], xp[:T])
    ds = jnp.where(allowed, both[:, :T] + both[:, T:] + rest, 0.0)
    dc = jnp.zeros((T, N), f32)
    for piece in split(ds, 2):
        dc = dc + nn(piece, bb)
    db = jnp.zeros((T, N), f32)
    for piece in split(ds.T, 2):
        db = db + nn(piece, cc)

    def arrived(refs, sem, index):
        pltpu.make_async_remote_copy(
            src_ref=refs, dst_ref=refs, send_sem=sem.at[index], recv_sem=sem.at[index],
            device_id=(dp, me), device_id_type=MESH,
        ).wait_recv()

    def through(r, k):
        return ra[r, k, 2 * N : 2 * N + 1, :]

    def own(r, k):
        return ra[r, k, 0:N, :]

    def pulled(r, k):
        return ra[r, k, N : 2 * N, :]

    def pass_on(r, k, up, down):
        sb[r, 0, k], sb[r, 1, k] = up, down
        for side, target in ((0, ahead), (1, behind)):
            copy = pltpu.make_async_remote_copy(
                src_ref=sb.at[r, side, k],
                dst_ref=rb.at[r, side, k],
                send_sem=sb_send.at[r, side, k],
                recv_sem=sb_recv.at[r, side, k],
                device_id=(dp, target),
                device_id_type=MESH,
            )
            copy.start()
            sent.append(copy)

    group_through, up_total, down_total = {}, {}, {}

    def event(k, r):
        if r == 0:
            for _, q in y_peers:
                arrived(ra.at[q, k], sa_recv, (q, k))
            up, down = own(0, k), pulled(RING - 1, k)
            for i in range(1, RING):
                up = own(i, k) + through(i, k) * up
                j = RING - 1 - i
                down = pulled(j, k) + through(j, k) * down
            g = through(0, k)
            for i in range(1, RING):
                g = g * through(i, k)
            group_through[k] = g
            pass_on(0, k, up, down)
            return
        for side in (0, 1):
            arrived(rb.at[r - 1, side, k], sb_recv, (r - 1, side, k))
        up, down = rb[r - 1, 0, k], rb[r - 1, 1, k]
        if r < rounds:
            pass_on(
                r, k,
                sb[0, 0, k] + group_through[k] * up,
                sb[0, 1, k] + group_through[k] * down,
            )
            return
        for i in range(RING):
            j = RING - 1 - i
            sc[i, k, 0:N, :] = up
            sc[j, k, N : 2 * N, :] = down
            if i + 1 < RING:
                up = own(i, k) + through(i, k) * up
                down = pulled(j, k) + through(j, k) * down
        for _, q in y_peers:
            copy = pltpu.make_async_remote_copy(
                src_ref=sc.at[q, k],
                dst_ref=rc.at[y, k],
                send_sem=sc_send.at[q, k],
                recv_sem=sc_recv.at[y, k],
                device_id=(dp, group * RING + q),
                device_id_type=MESH,
            )
            copy.start()
            sent.append(copy)
        rc[y, k] = sc[y, k]

    for wave in range(CHUNKS + rounds):
        for k in range(CHUNKS):
            if 0 <= wave - k <= rounds:
                event(k, wave - k)

    col_q, row_q = jnp.zeros((H, 2 * T), f32), jnp.zeros((H, 2 * T), f32)
    acc_c, acc_b = jnp.zeros((2 * T, 2 * N), f32), jnp.zeros((2 * T, 2 * N), f32)
    for k in range(CHUNKS):
        for _, q in y_peers:
            arrived(rc.at[q, k], sc_recv, (q, k))
        for q in range(RING):
            lo = q * Q + k * W
            at = slice(lo, lo + W)
            hot = one_hot(lo, W, 1)
            state, later = rc[q, k, 0:N, :], rc[q, k, N : 2 * N, :]
            last_alpha = rowv[8:9, at]
            vecs[0:1, at] = jnp.sum(
                later * (sa[q, k, 0:N, :] + last_alpha * through_flag * state),
                axis=0, keepdims=True,
            )
            hh = jnp.concatenate(split(state, 2), axis=0)
            fh = jnp.concatenate(split(later * last_alpha, 2), axis=0)
            z1_w = z1[:, at] + nn(eb, fh)
            z2_w = z2[:, at] + nn(lc, hh)
            gp, xp = gh[:, at], xh[:, at]
            p1 = z1_w * (xp[:T].astype(f32) + xp[T:].astype(f32))
            p2 = z2_w * (gp[:T].astype(f32) + gp[T:].astype(f32))
            dx_ref[:, at] = (bd[:, at] * z1_w + rowv[0:1, at] * g_ref[:, at].astype(f32)).astype(bf16)
            col_q = col_q + nt(hot, jnp.concatenate(split(p1, 2), axis=0))
            row_q = row_q + nt(hot, jnp.concatenate(split(p2, 2), axis=0))
            acc_c = acc_c + nt(gp, hh)
            acc_b = acc_b + nt(xp, fh)

    acc_c = acc_c[:T] + acc_c[T:]
    acc_b = acc_b[:T] + acc_b[T:]
    dc_ref[...] = (dc + living_col * (acc_c[:, :N] + acc_c[:, N:])).astype(bf16)
    db_ref[...] = (db + ending_col * (acc_b[:, :N] + acc_b[:, N:])).astype(bf16)

    hot = one_hot(0, H * D, 1)
    sums = jnp.zeros((H, 8), f32)
    for piece in split(vecs[...], 3):
        sums = sums + nt(hot, piece)
    col_q = col_q[:, :T] + col_q[:, T:]
    row_q = row_q[:, :T] + row_q[:, T:]
    d_log = jnp.zeros((H, T), f32) + sums[:, 0:1]
    for piece in split(row_q - col_q, 3):
        d_log = d_log + nn(piece, tril)
    head_r = lax.broadcasted_iota(jnp.int32, (H, H), 0)
    head_c = lax.broadcasted_iota(jnp.int32, (H, H), 1)
    rate_c = jnp.sum(jnp.where(head_r == head_c, jnp.broadcast_to(rate, (H, H)), 0.0), axis=1, keepdims=True)
    d_dt = d_log * rate_c
    dstep_ref[...] = col_q / dt + d_dt
    dalog = jnp.sum(d_dt * dt, axis=1, keepdims=True)
    on_diagonal = rows[:H] == cols[:H]
    alog_row = jnp.sum(jnp.where(on_diagonal, dalog, 0.0), axis=0, keepdims=True)
    skip_row = jnp.sum(jnp.where(on_diagonal, sums[:, 1:2], 0.0), axis=0, keepdims=True)
    row8 = lax.broadcasted_iota(jnp.int32, (8, T), 0)
    part = jnp.where(row8 == 0, alog_row, jnp.where(row8 == 1, skip_row, 0.0))

    stages = (
        (y, RING, [(dp, group * RING + (y + d) % RING) for d in range(1, RING)]),
        (z, n_z, [(dp, p) for p in z_peers]),
        (fold, n_dp * n_x, f_peers),
    )
    for s, (mine, count, peers) in enumerate(stages):
        ar[s, mine] = part
        for d, target in enumerate(peers, 1):
            copy = pltpu.make_async_remote_copy(
                src_ref=ar.at[s, mine],
                dst_ref=ar.at[s, mine],
                send_sem=ar_send.at[s, d],
                recv_sem=ar_recv.at[s, mine],
                device_id=target,
                device_id_type=MESH,
            )
            copy.start()
            sent.append(copy)
        for d in range(1, count):
            other = (mine + d) % count
            arrived(ar.at[s, other], ar_recv, (s, other))
        part = ar[s, 0]
        for i in range(1, count):
            part = part + ar[s, i]
    dalog_ref[...] = part[0:1, :H]
    dskip_ref[...] = part[1:2, :H]
    for copy in sent:
        copy.wait_send()


def per_device(n_dp, n_ctx, n_z, inputs, b_proj, c_proj, step_sizes, a_log, skip_gain, doc_lengths, grad_out):
    T, H, N = inputs.shape[1], a_log.shape[0], b_proj.shape[2]
    D = inputs.shape[2] // H
    HD = H * D
    K, W = CHUNKS, HD // (RING * CHUNKS)
    rounds = -(-MOST_DOC // (RING * T))
    n_x = n_ctx // (n_z * RING)
    slots = max(RING, n_z, n_dp * n_x)
    dims = (n_dp, n_ctx, n_z, T, H, D, N, doc_lengths.shape[1])
    vmem = pl.BlockSpec(memory_space=pltpu.VMEM)
    dma = pltpu.SemaphoreType.DMA
    dx, db, dc, dstep, dalog, dskip = pl.pallas_call(
        functools.partial(kernel, dims),
        out_shape=(
            jax.ShapeDtypeStruct((T, HD), bf16),
            jax.ShapeDtypeStruct((T, N), bf16),
            jax.ShapeDtypeStruct((T, N), bf16),
            jax.ShapeDtypeStruct((H, T), f32),
            jax.ShapeDtypeStruct((1, H), f32),
            jax.ShapeDtypeStruct((1, H), f32),
        ),
        in_specs=[vmem] * 7 + [pl.BlockSpec(memory_space=pltpu.SMEM)],
        out_specs=(vmem,) * 6,
        scratch_shapes=[
            pltpu.VMEM((2 * T, HD), bf16),
            pltpu.VMEM((2 * T, HD), bf16),
            pltpu.VMEM((T, HD), f32),
            pltpu.VMEM((T, HD), f32),
            pltpu.VMEM((T, HD), f32),
            pltpu.VMEM((16, HD), f32),
            pltpu.VMEM((8, HD), f32),
            pltpu.VMEM((RING, K, 2 * N + 8, W), f32),
            pltpu.VMEM((RING, K, 2 * N + 8, W), f32),
            pltpu.VMEM((rounds, 2, K, N, W), f32),
            pltpu.VMEM((rounds, 2, K, N, W), f32),
            pltpu.VMEM((RING, K, 2 * N, W), f32),
            pltpu.VMEM((RING, K, 2 * N, W), f32),
            pltpu.VMEM((3, slots, 8, 128), f32),
            dma((RING, K)),
            dma((RING, K)),
            dma((rounds, 2, K)),
            dma((rounds, 2, K)),
            dma((RING, K)),
            dma((RING, K)),
            dma((3, slots)),
            dma((3, slots)),
        ],
        compiler_params=pltpu.CompilerParams(
            collective_id=0, has_side_effects=True, vmem_limit_bytes=40 << 20
        ),
        name="ssd_backward",
    )(
        inputs[0], grad_out[0], b_proj[0], c_proj[0], step_sizes[0],
        a_log[None], skip_gain[None], doc_lengths,
    )
    return dx[None], db[None], dc[None], dstep[None], dalog[0], dskip[0]


def solution(mesh):
    tokens, heads = P("dp", "ctx", None), P("dp", None, "ctx")
    n_dp, n_ctx = mesh.shape["dp"], mesh.shape["ctx"]
    n_z = min(8, n_ctx // RING)
    return jax.shard_map(
        functools.partial(per_device, n_dp, n_ctx, n_z),
        mesh=mesh,
        in_specs=(tokens, tokens, tokens, heads, P(), P(), P("dp", None), tokens),
        out_specs=(tokens, tokens, tokens, heads, P(), P()),
        check_vma=False,
    )
```

```python
import functools

import jax
import jax.numpy as jnp
from jax import lax
from jax.experimental import pallas as pl
from jax.experimental.pallas import tpu as pltpu
from jax.sharding import PartitionSpec as P

MESH = pl.DeviceIdType.MESH
f32, bf16 = jnp.float32, jnp.bfloat16

MOST_DOC = 2048
RING = 4
CHUNKS = 4
ORDER = (
    ("total", 0), ("total", 1), ("pair", 0), ("total", 2), ("pair", 1), ("total", 3), ("pair", 2), ("give", 0),
    ("pair", 3), ("give", 1), ("give", 2), ("finish", 0), ("give", 3), ("finish", 1), ("finish", 2), ("finish", 3),
)


def nn(a, b):
    return lax.dot_general(a, b, (((1,), (0,)), ((), ())), preferred_element_type=f32)


def nt(a, b):
    return lax.dot_general(a, b, (((1,), (1,)), ((), ())), preferred_element_type=f32)


def split(v, count):
    pieces = []
    for i in range(count):
        piece = v.astype(bf16)
        pieces.append(piece)
        if i + 1 < count:
            v = v - piece.astype(f32)
    return pieces


def kernel(
    dims,
    x_hbm, g_hbm, bt_hbm, ct_hbm, dt_hbm, alog_hbm, skip_hbm, len_hbm,
    dx_hbm, db_hbm, dc_hbm, dstep_hbm, dalog_hbm, dskip_hbm,
    dx_ref, db_ref, dc_ref, dstep_ref, dalog_ref, dskip_ref,
    x_ref, g_ref, bt_ref, ct_ref, dt_ref, alog_ref, skip_ref, len_ref,
    xh, gh, bd, z1, z2, rowv, vecs, sa, ra, s1, r1, s2, r2, r3, sc, rc, ar,
    load, store, sa_send, sa_recv, s1_send, r1_recv, s2_send, r2_recv, s3_send, r3_recv, sc_send, sc_recv, ar_send, ar_recv,
):
    n_dp, n_ctx, n_z, T, H, D, N, DOCS = dims
    n_x = n_ctx // (n_z * RING)
    groups = n_ctx // RING
    W = H * D // (RING * CHUNKS)
    C = RING * W
    dp, me = lax.axis_index("dp"), lax.axis_index("ctx")
    y, group = me % RING, me // RING
    z, xhi = group % n_z, group // n_z

    y_peers = [(d, (y + d) % RING) for d in (2, 1, 3)]
    z_near = [(dp, ((group + d) % groups) * RING + y) for d in (1, groups - 1)]
    z_far = [(dp, ((group + d + groups) % groups) * RING + y) for d in (3, -3)]
    z_peers = [(dp, (xhi * n_z + (z + d) % n_z) * RING + y) for d in range(1, n_z)]
    fold = dp * n_x + xhi
    f_peers = []
    for d in range(1, n_dp * n_x):
        other = (fold + d) % (n_dp * n_x)
        f_peers.append((other // n_x, ((other % n_x) * n_z + z) * RING + y))

    barrier = pltpu.get_barrier_semaphore()
    greeted = [(dp, group * RING + q) for _, q in y_peers]
    greeted += z_near + z_far + z_peers + f_peers
    for target in greeted:
        pl.semaphore_signal(barrier, inc=1, device_id=target, device_id_type=MESH)

    pairs = [(len_hbm, len_ref), (dt_hbm, dt_ref), (alog_hbm, alog_ref), (bt_hbm, bt_ref), (ct_hbm, ct_ref), (skip_hbm, skip_ref)]
    small = len(pairs)
    for k in range(CHUNKS):
        at = slice(k * C, (k + 1) * C)
        pairs += [(g_hbm.at[:, at], g_ref.at[:, at]), (x_hbm.at[:, at], x_ref.at[:, at])]
    loads = [pltpu.make_async_copy(a, b, load.at[i]) for i, (a, b) in enumerate(pairs)]
    for copy in loads:
        copy.start()

    rows = lax.broadcasted_iota(jnp.int32, (T, T), 0)
    cols = lax.broadcasted_iota(jnp.int32, (T, T), 1)
    tril = jnp.where(rows >= cols, 1.0, 0.0).astype(bf16)
    eye = jnp.where(rows == cols, 1.0, 0.0).astype(bf16)
    head_r = lax.broadcasted_iota(jnp.int32, (H, H), 0)
    head_c = lax.broadcasted_iota(jnp.int32, (H, H), 1)

    def one_hot(k, copies):
        heads = lax.broadcasted_iota(jnp.int32, (copies * H, C), 0) % H
        lanes = lax.broadcasted_iota(jnp.int32, (copies * H, C), 1) + k * C
        return jnp.where(lanes // D == heads, 1.0, 0.0).astype(bf16)

    for copy in loads[:small]:
        copy.wait()

    offset = me * T
    lengths = len_ref[...]
    doc_r = lax.broadcasted_iota(jnp.int32, (DOCS, DOCS), 0)
    doc_c = lax.broadcasted_iota(jnp.int32, (DOCS, DOCS), 1)
    length_col = jnp.sum(jnp.where(doc_r == doc_c, lengths, 0), axis=1, keepdims=True)
    start_col = jnp.sum(jnp.where(doc_c < doc_r, lengths, 0), axis=1, keepdims=True)
    start_row = jnp.sum(jnp.where(doc_r < doc_c, length_col, 0), axis=0, keepdims=True)
    place_row = lax.broadcasted_iota(jnp.int32, (DOCS, T), 1) + offset
    place_col = lax.broadcasted_iota(jnp.int32, (T, DOCS), 0) + offset
    seg_row = jnp.sum(jnp.where(start_col <= place_row, 1.0, 0.0), axis=0, keepdims=True)
    seg_col = jnp.sum(jnp.where(start_row <= place_col, 1.0, 0.0), axis=1, keepdims=True)
    before = jnp.sum(jnp.where(start_row <= offset - 1, 1.0, 0.0), axis=1, keepdims=True)
    last = jnp.sum(jnp.where(start_row <= offset + T - 1, 1.0, 0.0), axis=1, keepdims=True)
    same = seg_col == seg_row
    allowed = jnp.logical_and(rows >= cols, same)
    allowed_t = jnp.logical_and(cols >= rows, same)
    living_col = jnp.where(seg_col == before, 1.0, 0.0)
    ending_col = jnp.where(seg_col == last, 1.0, 0.0)
    living_row = jnp.where(seg_row == before, 1.0, 0.0)
    ending_row = jnp.where(seg_row == last, 1.0, 0.0)
    through_flag = jnp.where(last == before, 1.0, 0.0)

    dt = dt_ref[...]
    cum_dt, dt_t, cum_row = jnp.zeros((T, H), f32), jnp.zeros((T, H), f32), jnp.zeros((H, T), f32)
    for piece in split(dt, 3):
        cum_dt = cum_dt + nt(tril, piece)
        dt_t = dt_t + nt(eye, piece)
        cum_row = cum_row + nt(piece, tril)
    rate = -jnp.exp(alog_ref[...])
    cum = cum_dt * rate
    alpha = jnp.exp(cum)
    beta = jnp.exp(-cum) * dt_t
    spread = jnp.concatenate(
        [
            jnp.concatenate(split(alpha, 3), axis=1),
            jnp.concatenate(split(beta, 3), axis=1),
        ],
        axis=0,
    )
    skip3 = jnp.concatenate(split(jnp.broadcast_to(skip_ref[...], (16, H)), 3), axis=1)

    bt, ct = bt_ref[...], ct_ref[...]
    b32, c32 = nt(eye, bt), nt(eye, ct)
    bb, cc = b32.astype(bf16), c32.astype(bf16)
    eb_t = (bt.astype(f32) * ending_row).astype(bf16)
    lc_t = (ct.astype(f32) * living_row).astype(bf16)
    eb_t = jnp.concatenate([eb_t, eb_t], axis=1)
    lc_t = jnp.concatenate([lc_t, lc_t], axis=1)
    eb = (b32 * ending_col).astype(bf16)
    lc = (c32 * living_col).astype(bf16)
    eb = jnp.concatenate([eb, eb], axis=1)
    lc = jnp.concatenate([lc, lc], axis=1)

    sent = []

    def send(src, dst, ssem, rsem, target):
        copy = pltpu.make_async_remote_copy(
            src_ref=src, dst_ref=dst, send_sem=ssem, recv_sem=rsem, device_id=target, device_id_type=MESH
        )
        copy.start()
        sent.append(copy)

    stored = []

    def store_out(src, dst):
        copy = pltpu.make_async_copy(src, dst, store.at[len(stored)])
        copy.start()
        stored.append(copy)

    def arrived(ref, sem):
        pltpu.make_async_remote_copy(
            src_ref=ref, dst_ref=ref, send_sem=sem, recv_sem=sem, device_id=(dp, me), device_id_type=MESH
        ).wait_recv()

    for k in range(CHUNKS):
        at = slice(k * C, (k + 1) * C)
        hot = one_hot(k, 3)
        wide = nn(spread, hot)
        alpha_w, beta_w = wide[:T], wide[T:]
        for copy in loads[small + 2 * k : small + 2 * k + 2]:
            copy.wait()
        g = g_ref[:, at].astype(f32)
        x = x_ref[:, at].astype(f32)
        g_hi, g_lo = split(g * alpha_w, 2)
        x_hi, x_lo = split(x * beta_w, 2)
        gh[0:T, at], gh[T : 2 * T, at] = g_hi, g_lo
        xh[0:T, at], xh[T : 2 * T, at] = x_hi, x_lo
        last_alpha = alpha_w[T - 1 : T]
        states = nn(eb_t, xh[:, at]) * last_alpha
        backs = nn(lc_t, gh[:, at])
        through = jnp.broadcast_to(last_alpha * through_flag, (8, C))
        for q in range(RING):
            part = slice(q * W, (q + 1) * W)
            sa[q, k, 0:N, :] = states[:, part]
            sa[q, k, N : 2 * N, :] = backs[:, part]
            sa[q, k, 2 * N : 2 * N + 8, :] = through[:, part]
        if k == 0:
            pl.semaphore_wait(barrier, len(greeted))
        for _, q in y_peers:
            send(sa.at[q, k], ra.at[y, k], sa_send.at[q, k], sa_recv.at[y, k], (dp, group * RING + q))
        ra[y, k] = sa[y, k]
        rowv[0:8, at] = nn(skip3, hot)[0:8]
        rowv[8:16, at] = jnp.broadcast_to(last_alpha, (8, C))
        vecs[:, at] = jnp.broadcast_to(jnp.sum(g * x, axis=0, keepdims=True), (8, C))
        bd[:, at] = beta_w

    s_hi, s_lo = split(jnp.where(allowed, nn(cc, bt), 0.0), 2)
    t_hi, t_lo = split(jnp.where(allowed_t, nn(bb, ct), 0.0), 2)
    s_hi = jnp.concatenate([s_hi, s_hi], axis=1)
    t_hi = jnp.concatenate([t_hi, t_hi], axis=1)
    both = jnp.zeros((T, 2 * T), f32)
    rest = jnp.zeros((T, T), f32)
    for k in range(CHUNKS):
        at = slice(k * C, (k + 1) * C)
        xp, gp = xh[:, at], gh[:, at]
        z2[:, at] = nn(s_hi, xp) + nn(s_lo, xp[:T])
        z1[:, at] = nn(t_hi, gp) + nn(t_lo, gp[:T])
        both = both + nt(gp[:T], xp)
        rest = rest + nt(gp[T:], xp[:T])
    ds = jnp.where(allowed, both[:, :T] + both[:, T:] + rest, 0.0)
    dc, db = jnp.zeros((N, T), f32), jnp.zeros((N, T), f32)
    for piece in split(ds, 2):
        dc = dc + nt(bt, piece)
        db = db + nn(ct, piece)

    def through_of(r, k):
        return ra[r, k, 2 * N : 2 * N + 1, :]

    def own(r, k):
        return ra[r, k, 0:N, :]

    def pulled(r, k):
        return ra[r, k, N : 2 * N, :]

    def total(k):
        for _, q in y_peers:
            arrived(ra.at[q, k], sa_recv.at[q, k])
        up, down = own(0, k), pulled(RING - 1, k)
        across = through_of(0, k)
        for i in range(1, RING):
            j = RING - 1 - i
            up = own(i, k) + through_of(i, k) * up
            down = pulled(j, k) + through_of(j, k) * down
            across = across * through_of(i, k)
        for side, value in ((0, up), (1, down)):
            s1[k, side, 0:N, :] = value
            s1[k, side, N : N + 8, :] = jnp.broadcast_to(across, (8, W))
            send(s1.at[k, side], r1.at[k, side], s1_send.at[k, side], r1_recv.at[k, side], z_near[side])

    def pair(k):
        for side in (0, 1):
            arrived(r1.at[k, side], r1_recv.at[k, side])
            across = s1[k, side, N : N + 8, :]
            s2[k, side, 0:N, :] = s1[k, side, 0:N, :] + across[0:1] * r1[k, side, 0:N, :]
            s2[k, side, N : N + 8, :] = across * r1[k, side, N : N + 8, :]
            send(
                s2.at[k, side, 0:N, :], r3.at[k, side], s3_send.at[k, side], r3_recv.at[k, side], z_far[side]
            )
            send(s2.at[k, side], r2.at[k, side], s2_send.at[k, side], r2_recv.at[k, side], z_near[side])

    def give(k):
        enters = []
        for side in (0, 1):
            arrived(r2.at[k, side], r2_recv.at[k, side])
            arrived(r3.at[k, side], r3_recv.at[k, side])
            enters.append(r2[k, side, 0:N, :] + r2[k, side, N : N + 1, :] * r3[k, side])
        up, down = enters
        for i in range(RING):
            j = RING - 1 - i
            sc[i, k, 0:N, :] = up
            sc[j, k, N : 2 * N, :] = down
            if i + 1 < RING:
                up = own(i, k) + through_of(i, k) * up
                down = pulled(j, k) + through_of(j, k) * down
        for _, q in y_peers:
            send(sc.at[q, k], rc.at[y, k], sc_send.at[q, k], sc_recv.at[y, k], (dp, group * RING + q))
        rc[y, k] = sc[y, k]

    sums = [jnp.zeros((H, 2 * T), f32), jnp.zeros((H, 2 * T), f32), jnp.zeros((2 * N, 2 * T), f32), jnp.zeros((2 * N, 2 * T), f32), jnp.zeros((H, 8), f32)]

    def finish(k):
        at = slice(k * C, (k + 1) * C)
        for _, q in y_peers:
            arrived(rc.at[q, k], sc_recv.at[q, k])
        hot = one_hot(k, 1)
        state = jnp.concatenate([rc[q, k, 0:N, :] for q in range(RING)], axis=1)
        later = jnp.concatenate([rc[q, k, N : 2 * N, :] for q in range(RING)], axis=1)
        mine = jnp.concatenate([sa[q, k, 0:N, :] for q in range(RING)], axis=1)
        last_alpha = rowv[8:9, at]
        leaving = jnp.sum(later * (mine + last_alpha * through_flag * state), axis=0, keepdims=True)
        first_row = lax.broadcasted_iota(jnp.int32, (8, C), 0) == 0
        vec = jnp.where(first_row, leaving, vecs[:, at])
        hh = jnp.concatenate(split(state, 2), axis=0)
        fh = jnp.concatenate(split(later * last_alpha, 2), axis=0)
        z1_w = z1[:, at] + nn(eb, fh)
        z2_w = z2[:, at] + nn(lc, hh)
        gp, xp = gh[:, at], xh[:, at]
        p1 = z1_w * (xp[:T].astype(f32) + xp[T:].astype(f32))
        p2 = z2_w * (gp[:T].astype(f32) + gp[T:].astype(f32))
        dx_ref[:, at] = (bd[:, at] * z1_w + rowv[0:1, at] * g_ref[:, at].astype(f32)).astype(bf16)
        store_out(dx_ref.at[:, at], dx_hbm.at[:, at])
        sums[0] = sums[0] + nt(hot, jnp.concatenate(split(p1, 2), axis=0))
        sums[1] = sums[1] + nt(hot, jnp.concatenate(split(p2, 2), axis=0))
        sums[2] = sums[2] + nt(hh, gp)
        sums[3] = sums[3] + nt(fh, xp)
        for piece in split(vec, 3):
            sums[4] = sums[4] + nt(hot, piece)

    steps = {"total": total, "pair": pair, "give": give, "finish": finish}
    for name, k in ORDER:
        steps[name](k)

    col_q = sums[0][:, :T] + sums[0][:, T:]
    row_q = sums[1][:, :T] + sums[1][:, T:]
    d_cum = row_q - col_q
    d_end, d_skip = sums[4][:, 0:1], sums[4][:, 1:2]
    rate_c = jnp.sum(jnp.where(head_r == head_c, jnp.broadcast_to(rate, (H, H)), 0.0), axis=1, keepdims=True)
    at_end = cols[:H] == T - 1
    d_alog = rate_c * jnp.sum((d_cum + jnp.where(at_end, d_end, 0.0)) * cum_row, axis=1, keepdims=True)
    diagonal = rows[:H] == cols[:H]
    alog_row = jnp.sum(jnp.where(diagonal, d_alog, 0.0), axis=0, keepdims=True)
    skip_row = jnp.sum(jnp.where(diagonal, d_skip, 0.0), axis=0, keepdims=True)
    row8 = lax.broadcasted_iota(jnp.int32, (8, T), 0)
    part = jnp.where(row8 == 0, alog_row, jnp.where(row8 == 1, skip_row, 0.0))

    stages = (
        (y, RING, [(dp, group * RING + (y + d) % RING) for d in range(1, RING)]),
        (z, n_z, z_peers),
        (fold, n_dp * n_x, f_peers),
    )
    for s, (mine, count, peers) in enumerate(stages):
        ar[s, mine] = part
        for d, target in enumerate(peers, 1):
            send(ar.at[s, mine], ar.at[s, mine], ar_send.at[s, d], ar_recv.at[s, mine], target)
        if s == 0:
            acc = sums[2][:N] + sums[2][N:]
            dc_ref[...] = (dc + living_row * (acc[:, :T] + acc[:, T:])).astype(bf16)
            acc = sums[3][:N] + sums[3][N:]
            db_ref[...] = (db + ending_row * (acc[:, :T] + acc[:, T:])).astype(bf16)
            d_log = jnp.zeros((H, T), f32) + d_end
            for piece in split(d_cum, 3):
                d_log = d_log + nn(piece, tril)
            dstep_ref[...] = col_q / dt + d_log * rate_c
            for src, dst in ((dc_ref, dc_hbm), (db_ref, db_hbm), (dstep_ref, dstep_hbm)):
                store_out(src, dst)
        for d in range(1, count):
            other = (mine + d) % count
            arrived(ar.at[s, other], ar_recv.at[s, other])
        part = ar[s, 0]
        for i in range(1, count):
            part = part + ar[s, i]
    dalog_ref[...] = part[0:1, :H]
    dskip_ref[...] = part[1:2, :H]
    store_out(dalog_ref, dalog_hbm)
    store_out(dskip_ref, dskip_hbm)
    for copy in sent:
        copy.wait_send()
    for copy in stored:
        copy.wait()


def write_out(count, *refs):
    sem = refs[-1]
    copies = [pltpu.make_async_copy(refs[i], refs[count + i], sem.at[i]) for i in range(count)]
    for copy in copies:
        copy.start()
    for copy in copies:
        copy.wait()


def per_device(n_dp, n_ctx, n_z, inputs, b_proj, c_proj, step_sizes, a_log, skip_gain, doc_lengths, grad_out):
    T, H, N = inputs.shape[1], a_log.shape[0], b_proj.shape[2]
    D, DOCS = inputs.shape[2] // H, doc_lengths.shape[1]
    HD = H * D
    K, W = CHUNKS, HD // (RING * CHUNKS)
    assert 4 * RING * T >= MOST_DOC
    n_x = n_ctx // (n_z * RING)
    slots = max(RING, n_z, n_dp * n_x)
    dims = (n_dp, n_ctx, n_z, T, H, D, N, DOCS)
    hbm = pl.BlockSpec(memory_space=pltpu.HBM)
    dma = pltpu.SemaphoreType.DMA
    outs = (
        jax.ShapeDtypeStruct((T, HD), bf16),
        jax.ShapeDtypeStruct((N, T), bf16),
        jax.ShapeDtypeStruct((N, T), bf16),
        jax.ShapeDtypeStruct((H, T), f32),
        jax.ShapeDtypeStruct((1, H), f32),
        jax.ShapeDtypeStruct((1, H), f32),
    )
    results = pl.pallas_call(
        functools.partial(kernel, dims),
        out_shape=outs,
        in_specs=[hbm] * 8,
        out_specs=(hbm,) * 6,
        scratch_shapes=[
            *(pltpu.VMEM(o.shape, o.dtype) for o in outs),
            pltpu.VMEM((T, HD), bf16),
            pltpu.VMEM((T, HD), bf16),
            pltpu.VMEM((N, T), bf16),
            pltpu.VMEM((N, T), bf16),
            pltpu.VMEM((H, T), f32),
            pltpu.VMEM((1, H), f32),
            pltpu.VMEM((1, H), f32),
            pltpu.VMEM((1, DOCS), jnp.int32),
            pltpu.VMEM((2 * T, HD), bf16),
            pltpu.VMEM((2 * T, HD), bf16),
            pltpu.VMEM((T, HD), f32),
            pltpu.VMEM((T, HD), f32),
            pltpu.VMEM((T, HD), f32),
            pltpu.VMEM((16, HD), f32),
            pltpu.VMEM((8, HD), f32),
            pltpu.VMEM((RING, K, 2 * N + 8, W), f32),
            pltpu.VMEM((RING, K, 2 * N + 8, W), f32),
            pltpu.VMEM((K, 2, N + 8, W), f32),
            pltpu.VMEM((K, 2, N + 8, W), f32),
            pltpu.VMEM((K, 2, N + 8, W), f32),
            pltpu.VMEM((K, 2, N + 8, W), f32),
            pltpu.VMEM((K, 2, N, W), f32),
            pltpu.VMEM((RING, K, 2 * N, W), f32),
            pltpu.VMEM((RING, K, 2 * N, W), f32),
            pltpu.VMEM((3, slots, 8, 128), f32),
            dma((6 + 2 * K,)),
            dma((5 + K,)),
            dma((RING, K)),
            dma((RING, K)),
            dma((K, 2)),
            dma((K, 2)),
            dma((K, 2)),
            dma((K, 2)),
            dma((K, 2)),
            dma((K, 2)),
            dma((RING, K)),
            dma((RING, K)),
            dma((3, slots)),
            dma((3, slots)),
        ],
        compiler_params=pltpu.CompilerParams(
            collective_id=0, has_side_effects=True, vmem_limit_bytes=60 << 20
        ),
        name="ssd_backward",
    )(
        inputs[0], grad_out[0], b_proj[0].T, c_proj[0].T, step_sizes[0],
        a_log[None], skip_gain[None], doc_lengths,
    )
    dx, db, dc, dstep, dalog, dskip = pl.pallas_call(
        functools.partial(write_out, len(outs)),
        out_shape=outs,
        in_specs=[hbm] * 6,
        out_specs=(hbm,) * 6,
        scratch_shapes=[dma((len(outs),))],
        name="write_out",
    )(*results)
    return dx[None], db.T[None], dc.T[None], dstep[None], dalog[0], dskip[0]


def solution(mesh):
    tokens, heads = P("dp", "ctx", None), P("dp", None, "ctx")
    n_dp, n_ctx = mesh.shape["dp"], mesh.shape["ctx"]
    n_z = min(8, n_ctx // RING)
    return jax.shard_map(
        functools.partial(per_device, n_dp, n_ctx, n_z),
        mesh=mesh,
        in_specs=(tokens, tokens, tokens, heads, P(), P(), P("dp", None), tokens),
        out_specs=(tokens, tokens, tokens, heads, P(), P()),
        check_vma=False,
    )
```

```python
import functools

import jax
import jax.numpy as jnp
from jax import lax
from jax.experimental import pallas as pl
from jax.experimental.pallas import tpu as pltpu
from jax.sharding import PartitionSpec as P

MESH = pl.DeviceIdType.MESH
f32, bf16 = jnp.float32, jnp.bfloat16

MOST_DOC = 2048
RING = 4
CHUNKS = 4
ORDER = (
    ("total", 0), ("total", 1), ("pair", 0), ("total", 2), ("pair", 1), ("total", 3), ("pair", 2), ("give", 0),
    ("pair", 3), ("give", 1), ("give", 2), ("finish", 0), ("give", 3), ("finish", 1), ("finish", 2), ("finish", 3),
)


def nn(a, b):
    return lax.dot_general(a, b, (((1,), (0,)), ((), ())), preferred_element_type=f32)


def nt(a, b):
    return lax.dot_general(a, b, (((1,), (1,)), ((), ())), preferred_element_type=f32)


def split(v, count):
    pieces = []
    for i in range(count):
        piece = v.astype(bf16)
        pieces.append(piece)
        if i + 1 < count:
            v = v - piece.astype(f32)
    return pieces


def kernel(
    dims,
    x_hbm, g_hbm, bt_hbm, ct_hbm, dt_hbm, alog_hbm, skip_hbm, len_hbm,
    dx_hbm, db_hbm, dc_hbm, dstep_hbm, dalog_hbm, dskip_hbm,
    dx_ref, db_ref, dc_ref, dstep_ref, dalog_ref, dskip_ref,
    x_ref, g_ref, bt_ref, ct_ref, dt_ref, alog_ref, skip_ref, len_ref,
    xh, gh, bd, z1, z2, rowv, vecs, sa, ra, s1, r1, s2, r2, r3, sc, rc, ar,
    load, store, sa_send, sa_recv, s1_send, r1_recv, s2_send, r2_recv, s3_send, r3_recv, sc_send, sc_recv, ar_send, ar_recv,
):
    n_dp, n_ctx, n_z, T, H, D, N, DOCS = dims
    n_x = n_ctx // (n_z * RING)
    groups = n_ctx // RING
    W = H * D // (RING * CHUNKS)
    C = RING * W
    dp, me = lax.axis_index("dp"), lax.axis_index("ctx")
    y, group = me % RING, me // RING
    z, xhi = group % n_z, group // n_z

    y_peers = [(d, (y + d) % RING) for d in (2, 1, 3)]
    z_near = [(dp, ((group + d) % groups) * RING + y) for d in (1, groups - 1)]
    z_far = [(dp, ((group + d + groups) % groups) * RING + y) for d in (3, -3)]
    z_peers = [(dp, (xhi * n_z + (z + d) % n_z) * RING + y) for d in range(1, n_z)]
    fold = dp * n_x + xhi
    f_peers = []
    for d in range(1, n_dp * n_x):
        other = (fold + d) % (n_dp * n_x)
        f_peers.append((other // n_x, ((other % n_x) * n_z + z) * RING + y))

    barrier = pltpu.get_barrier_semaphore()
    greeted = [(dp, group * RING + q) for _, q in y_peers]
    greeted += z_near + z_far + z_peers + f_peers
    for target in greeted:
        pl.semaphore_signal(barrier, inc=1, device_id=target, device_id_type=MESH)

    pairs = [(len_hbm, len_ref), (dt_hbm, dt_ref), (alog_hbm, alog_ref), (bt_hbm, bt_ref), (ct_hbm, ct_ref), (skip_hbm, skip_ref)]
    small = len(pairs)
    for k in range(CHUNKS):
        at = slice(k * C, (k + 1) * C)
        pairs += [(g_hbm.at[:, at], g_ref.at[:, at]), (x_hbm.at[:, at], x_ref.at[:, at])]
    loads = [pltpu.make_async_copy(a, b, load.at[i]) for i, (a, b) in enumerate(pairs)]
    for copy in loads:
        copy.start()

    rows = lax.broadcasted_iota(jnp.int32, (T, T), 0)
    cols = lax.broadcasted_iota(jnp.int32, (T, T), 1)
    tril = jnp.where(rows >= cols, 1.0, 0.0).astype(bf16)
    eye = jnp.where(rows == cols, 1.0, 0.0).astype(bf16)
    head_r = lax.broadcasted_iota(jnp.int32, (H, H), 0)
    head_c = lax.broadcasted_iota(jnp.int32, (H, H), 1)

    def one_hot(k, copies):
        heads = lax.broadcasted_iota(jnp.int32, (copies * H, C), 0) % H
        lanes = lax.broadcasted_iota(jnp.int32, (copies * H, C), 1) + k * C
        return jnp.where(lanes // D == heads, 1.0, 0.0).astype(bf16)

    for copy in loads[:small]:
        copy.wait()

    offset = me * T
    lengths = len_ref[...]
    doc_r = lax.broadcasted_iota(jnp.int32, (DOCS, DOCS), 0)
    doc_c = lax.broadcasted_iota(jnp.int32, (DOCS, DOCS), 1)
    length_col = jnp.sum(jnp.where(doc_r == doc_c, lengths, 0), axis=1, keepdims=True)
    start_col = jnp.sum(jnp.where(doc_c < doc_r, lengths, 0), axis=1, keepdims=True)
    start_row = jnp.sum(jnp.where(doc_r < doc_c, length_col, 0), axis=0, keepdims=True)
    place_row = lax.broadcasted_iota(jnp.int32, (DOCS, T), 1) + offset
    place_col = lax.broadcasted_iota(jnp.int32, (T, DOCS), 0) + offset
    seg_row = jnp.sum(jnp.where(start_col <= place_row, 1.0, 0.0), axis=0, keepdims=True)
    seg_col = jnp.sum(jnp.where(start_row <= place_col, 1.0, 0.0), axis=1, keepdims=True)
    before = jnp.sum(jnp.where(start_row <= offset - 1, 1.0, 0.0), axis=1, keepdims=True)
    last = jnp.sum(jnp.where(start_row <= offset + T - 1, 1.0, 0.0), axis=1, keepdims=True)
    same = seg_col == seg_row
    allowed = jnp.logical_and(rows >= cols, same)
    allowed_t = jnp.logical_and(cols >= rows, same)
    living_col = jnp.where(seg_col == before, 1.0, 0.0)
    ending_col = jnp.where(seg_col == last, 1.0, 0.0)
    living_row = jnp.where(seg_row == before, 1.0, 0.0)
    ending_row = jnp.where(seg_row == last, 1.0, 0.0)
    through_flag = jnp.where(last == before, 1.0, 0.0)

    dt = dt_ref[...]
    cum_dt, dt_t, cum_row = jnp.zeros((T, H), f32), jnp.zeros((T, H), f32), jnp.zeros((H, T), f32)
    for piece in split(dt, 3):
        cum_dt = cum_dt + nt(tril, piece)
        dt_t = dt_t + nt(eye, piece)
        cum_row = cum_row + nt(piece, tril)
    rate = -jnp.exp(alog_ref[...])
    cum = cum_dt * rate
    alpha = jnp.exp(cum)
    beta = jnp.exp(-cum) * dt_t
    spread = jnp.concatenate(
        [
            jnp.concatenate(split(alpha, 3), axis=1),
            jnp.concatenate(split(beta, 3), axis=1),
        ],
        axis=0,
    )
    skip3 = jnp.concatenate(split(jnp.broadcast_to(skip_ref[...], (16, H)), 3), axis=1)

    bt, ct = bt_ref[...], ct_ref[...]
    b32, c32 = nt(eye, bt), nt(eye, ct)
    bb, cc = b32.astype(bf16), c32.astype(bf16)
    eb_t = (bt.astype(f32) * ending_row).astype(bf16)
    lc_t = (ct.astype(f32) * living_row).astype(bf16)
    eb_t = jnp.concatenate([eb_t, eb_t], axis=1)
    lc_t = jnp.concatenate([lc_t, lc_t], axis=1)
    eb = (b32 * ending_col).astype(bf16)
    lc = (c32 * living_col).astype(bf16)
    eb = jnp.concatenate([eb, eb], axis=1)
    lc = jnp.concatenate([lc, lc], axis=1)

    sent = []

    def send(src, dst, ssem, rsem, target):
        copy = pltpu.make_async_remote_copy(
            src_ref=src, dst_ref=dst, send_sem=ssem, recv_sem=rsem, device_id=target, device_id_type=MESH
        )
        copy.start()
        sent.append(copy)

    stored = []

    def store_out(src, dst):
        copy = pltpu.make_async_copy(src, dst, store.at[len(stored)])
        copy.start()
        stored.append(copy)

    def arrived(ref, sem):
        pltpu.make_async_remote_copy(
            src_ref=ref, dst_ref=ref, send_sem=sem, recv_sem=sem, device_id=(dp, me), device_id_type=MESH
        ).wait_recv()

    for k in range(CHUNKS):
        at = slice(k * C, (k + 1) * C)
        hot = one_hot(k, 3)
        wide = nn(spread, hot)
        alpha_w, beta_w = wide[:T], wide[T:]
        for copy in loads[small + 2 * k : small + 2 * k + 2]:
            copy.wait()
        g = g_ref[:, at].astype(f32)
        x = x_ref[:, at].astype(f32)
        g_hi, g_lo = split(g * alpha_w, 2)
        x_hi, x_lo = split(x * beta_w, 2)
        gh[0:T, at], gh[T : 2 * T, at] = g_hi, g_lo
        xh[0:T, at], xh[T : 2 * T, at] = x_hi, x_lo
        last_alpha = alpha_w[T - 1 : T]
        states = nn(eb_t, xh[:, at]) * last_alpha
        backs = nn(lc_t, gh[:, at])
        through = jnp.broadcast_to(last_alpha * through_flag, (8, C))
        for q in range(RING):
            part = slice(q * W, (q + 1) * W)
            sa[q, k, 0:N, :] = states[:, part]
            sa[q, k, N : 2 * N, :] = backs[:, part]
            sa[q, k, 2 * N : 2 * N + 8, :] = through[:, part]
        if k == 0:
            pl.semaphore_wait(barrier, len(greeted))
        for _, q in y_peers:
            send(sa.at[q, k], ra.at[y, k], sa_send.at[q, k], sa_recv.at[y, k], (dp, group * RING + q))
        ra[y, k] = sa[y, k]
        rowv[0:8, at] = nn(skip3, hot)[0:8]
        rowv[8:16, at] = jnp.broadcast_to(last_alpha, (8, C))
        vecs[:, at] = jnp.broadcast_to(jnp.sum(g * x, axis=0, keepdims=True), (8, C))
        bd[:, at] = beta_w

    s_hi, s_lo = split(jnp.where(allowed, nn(cc, bt), 0.0), 2)
    t_hi, t_lo = split(jnp.where(allowed_t, nn(bb, ct), 0.0), 2)
    s_hi = jnp.concatenate([s_hi, s_hi], axis=1)
    t_hi = jnp.concatenate([t_hi, t_hi], axis=1)
    both = jnp.zeros((T, 2 * T), f32)
    rest = jnp.zeros((T, T), f32)
    for k in range(CHUNKS):
        at = slice(k * C, (k + 1) * C)
        xp, gp = xh[:, at], gh[:, at]
        z2[:, at] = nn(s_hi, xp) + nn(s_lo, xp[:T])
        z1[:, at] = nn(t_hi, gp) + nn(t_lo, gp[:T])
        both = both + nt(gp[:T], xp)
        rest = rest + nt(gp[T:], xp[:T])
    ds = jnp.where(allowed, both[:, :T] + both[:, T:] + rest, 0.0)
    dc, db = jnp.zeros((N, T), f32), jnp.zeros((N, T), f32)
    for piece in split(ds, 2):
        dc = dc + nt(bt, piece)
        db = db + nn(ct, piece)

    def through_of(r, k):
        return ra[r, k, 2 * N : 2 * N + 1, :]

    def own(r, k):
        return ra[r, k, 0:N, :]

    def pulled(r, k):
        return ra[r, k, N : 2 * N, :]

    def total(k):
        for _, q in y_peers:
            arrived(ra.at[q, k], sa_recv.at[q, k])
        up, down = own(0, k), pulled(RING - 1, k)
        across = through_of(0, k)
        for i in range(1, RING):
            j = RING - 1 - i
            up = own(i, k) + through_of(i, k) * up
            down = pulled(j, k) + through_of(j, k) * down
            across = across * through_of(i, k)
        for side, value in ((0, up), (1, down)):
            s1[k, side, 0:N, :] = value
            s1[k, side, N : N + 8, :] = jnp.broadcast_to(across, (8, W))
            send(s1.at[k, side], r1.at[k, side], s1_send.at[k, side], r1_recv.at[k, side], z_near[side])

    def pair(k):
        for side in (0, 1):
            arrived(r1.at[k, side], r1_recv.at[k, side])
            across = s1[k, side, N : N + 8, :]
            s2[k, side, 0:N, :] = s1[k, side, 0:N, :] + across[0:1] * r1[k, side, 0:N, :]
            s2[k, side, N : N + 8, :] = across * r1[k, side, N : N + 8, :]
            send(
                s2.at[k, side, 0:N, :], r3.at[k, side], s3_send.at[k, side], r3_recv.at[k, side], z_far[side]
            )
            send(s2.at[k, side], r2.at[k, side], s2_send.at[k, side], r2_recv.at[k, side], z_near[side])

    def give(k):
        enters = []
        for side in (0, 1):
            arrived(r2.at[k, side], r2_recv.at[k, side])
            arrived(r3.at[k, side], r3_recv.at[k, side])
            enters.append(r2[k, side, 0:N, :] + r2[k, side, N : N + 1, :] * r3[k, side])
        up, down = enters
        for i in range(RING):
            j = RING - 1 - i
            sc[i, k, 0:N, :] = up
            sc[j, k, N : 2 * N, :] = down
            if i + 1 < RING:
                up = own(i, k) + through_of(i, k) * up
                down = pulled(j, k) + through_of(j, k) * down
        for _, q in y_peers:
            send(sc.at[q, k], rc.at[y, k], sc_send.at[q, k], sc_recv.at[y, k], (dp, group * RING + q))
        rc[y, k] = sc[y, k]

    sums = [jnp.zeros((H, 2 * T), f32), jnp.zeros((H, 2 * T), f32), jnp.zeros((2 * N, 2 * T), f32), jnp.zeros((2 * N, 2 * T), f32), jnp.zeros((H, 8), f32)]

    def finish(k):
        at = slice(k * C, (k + 1) * C)
        for _, q in y_peers:
            arrived(rc.at[q, k], sc_recv.at[q, k])
        hot = one_hot(k, 1)
        state = jnp.concatenate([rc[q, k, 0:N, :] for q in range(RING)], axis=1)
        later = jnp.concatenate([rc[q, k, N : 2 * N, :] for q in range(RING)], axis=1)
        mine = jnp.concatenate([sa[q, k, 0:N, :] for q in range(RING)], axis=1)
        last_alpha = rowv[8:9, at]
        leaving = jnp.sum(later * (mine + last_alpha * through_flag * state), axis=0, keepdims=True)
        first_row = lax.broadcasted_iota(jnp.int32, (8, C), 0) == 0
        vec = jnp.where(first_row, leaving, vecs[:, at])
        hh = jnp.concatenate(split(state, 2), axis=0)
        fh = jnp.concatenate(split(later * last_alpha, 2), axis=0)
        z1_w = z1[:, at] + nn(eb, fh)
        z2_w = z2[:, at] + nn(lc, hh)
        gp, xp = gh[:, at], xh[:, at]
        p1 = z1_w * (xp[:T].astype(f32) + xp[T:].astype(f32))
        p2 = z2_w * (gp[:T].astype(f32) + gp[T:].astype(f32))
        dx_ref[:, at] = (bd[:, at] * z1_w + rowv[0:1, at] * g_ref[:, at].astype(f32)).astype(bf16)
        store_out(dx_ref.at[:, at], dx_hbm.at[:, at])
        sums[0] = sums[0] + nt(hot, jnp.concatenate(split(p1, 2), axis=0))
        sums[1] = sums[1] + nt(hot, jnp.concatenate(split(p2, 2), axis=0))
        sums[2] = sums[2] + nt(hh, gp)
        sums[3] = sums[3] + nt(fh, xp)
        for piece in split(vec, 3):
            sums[4] = sums[4] + nt(hot, piece)

    steps = {"total": total, "pair": pair, "give": give, "finish": finish}
    for name, k in ORDER:
        steps[name](k)

    col_q = sums[0][:, :T] + sums[0][:, T:]
    row_q = sums[1][:, :T] + sums[1][:, T:]
    d_cum = row_q - col_q
    d_end, d_skip = sums[4][:, 0:1], sums[4][:, 1:2]
    rate_c = jnp.sum(jnp.where(head_r == head_c, jnp.broadcast_to(rate, (H, H)), 0.0), axis=1, keepdims=True)
    at_end = cols[:H] == T - 1
    d_alog = rate_c * jnp.sum((d_cum + jnp.where(at_end, d_end, 0.0)) * cum_row, axis=1, keepdims=True)
    diagonal = rows[:H] == cols[:H]
    alog_row = jnp.sum(jnp.where(diagonal, d_alog, 0.0), axis=0, keepdims=True)
    skip_row = jnp.sum(jnp.where(diagonal, d_skip, 0.0), axis=0, keepdims=True)
    row8 = lax.broadcasted_iota(jnp.int32, (8, T), 0)
    part = jnp.where(row8 == 0, alog_row, jnp.where(row8 == 1, skip_row, 0.0))

    stages = (
        (y, RING, [(dp, group * RING + (y + d) % RING) for d in range(1, RING)]),
        (z, n_z, z_peers),
        (fold, n_dp * n_x, f_peers),
    )
    for s, (mine, count, peers) in enumerate(stages):
        ar[s, mine] = part
        for d, target in enumerate(peers, 1):
            send(ar.at[s, mine], ar.at[s, mine], ar_send.at[s, d], ar_recv.at[s, mine], target)
        if s == 0:
            acc = sums[2][:N] + sums[2][N:]
            dc_ref[...] = (dc + living_row * (acc[:, :T] + acc[:, T:])).astype(bf16)
            acc = sums[3][:N] + sums[3][N:]
            db_ref[...] = (db + ending_row * (acc[:, :T] + acc[:, T:])).astype(bf16)
            d_log = jnp.zeros((H, T), f32) + d_end
            for piece in split(d_cum, 3):
                d_log = d_log + nn(piece, tril)
            dstep_ref[...] = col_q / dt + d_log * rate_c
            for src, dst in ((dc_ref, dc_hbm), (db_ref, db_hbm), (dstep_ref, dstep_hbm)):
                store_out(src, dst)
        for d in range(1, count):
            other = (mine + d) % count
            arrived(ar.at[s, other], ar_recv.at[s, other])
        part = ar[s, 0]
        for i in range(1, count):
            part = part + ar[s, i]
    dalog_ref[...] = part[0:1, :H]
    dskip_ref[...] = part[1:2, :H]
    store_out(dalog_ref, dalog_hbm)
    store_out(dskip_ref, dskip_hbm)
    for copy in sent:
        copy.wait_send()
    for copy in stored:
        copy.wait()


def write_out(plan, *refs):
    count = len(refs) // 3
    sources, targets, places, loaded, stored = refs[:count], refs[count : 2 * count], refs[2 * count : 3 * count], *refs[-2:]
    copies = []
    for n, (i, at) in enumerate(plan):
        load = pltpu.make_async_copy(sources[i].at[:, at], places[i].at[:, at], loaded.at[n])
        copies.append((load, pltpu.make_async_copy(places[i].at[:, at], targets[i].at[:, at], stored.at[n])))
        load.start()
    for load, store in copies:
        load.wait()
        store.start()
    for _, store in copies:
        store.wait()


def per_device(n_dp, n_ctx, n_z, inputs, b_proj, c_proj, step_sizes, a_log, skip_gain, doc_lengths, grad_out):
    T, H, N = inputs.shape[1], a_log.shape[0], b_proj.shape[2]
    D, DOCS = inputs.shape[2] // H, doc_lengths.shape[1]
    HD = H * D
    K, W = CHUNKS, HD // (RING * CHUNKS)
    assert 4 * RING * T >= MOST_DOC
    n_x = n_ctx // (n_z * RING)
    slots = max(RING, n_z, n_dp * n_x)
    dims = (n_dp, n_ctx, n_z, T, H, D, N, DOCS)
    hbm = pl.BlockSpec(memory_space=pltpu.HBM)
    dma = pltpu.SemaphoreType.DMA
    outs = (
        jax.ShapeDtypeStruct((T, HD), bf16),
        jax.ShapeDtypeStruct((N, T), bf16),
        jax.ShapeDtypeStruct((N, T), bf16),
        jax.ShapeDtypeStruct((H, T), f32),
        jax.ShapeDtypeStruct((1, H), f32),
        jax.ShapeDtypeStruct((1, H), f32),
    )
    results = pl.pallas_call(
        functools.partial(kernel, dims),
        out_shape=outs,
        in_specs=[hbm] * 8,
        out_specs=(hbm,) * 6,
        scratch_shapes=[
            *(pltpu.VMEM(o.shape, o.dtype) for o in outs),
            pltpu.VMEM((T, HD), bf16),
            pltpu.VMEM((T, HD), bf16),
            pltpu.VMEM((N, T), bf16),
            pltpu.VMEM((N, T), bf16),
            pltpu.VMEM((H, T), f32),
            pltpu.VMEM((1, H), f32),
            pltpu.VMEM((1, H), f32),
            pltpu.VMEM((1, DOCS), jnp.int32),
            pltpu.VMEM((2 * T, HD), bf16),
            pltpu.VMEM((2 * T, HD), bf16),
            pltpu.VMEM((T, HD), f32),
            pltpu.VMEM((T, HD), f32),
            pltpu.VMEM((T, HD), f32),
            pltpu.VMEM((16, HD), f32),
            pltpu.VMEM((8, HD), f32),
            pltpu.VMEM((RING, K, 2 * N + 8, W), f32),
            pltpu.VMEM((RING, K, 2 * N + 8, W), f32),
            pltpu.VMEM((K, 2, N + 8, W), f32),
            pltpu.VMEM((K, 2, N + 8, W), f32),
            pltpu.VMEM((K, 2, N + 8, W), f32),
            pltpu.VMEM((K, 2, N + 8, W), f32),
            pltpu.VMEM((K, 2, N, W), f32),
            pltpu.VMEM((RING, K, 2 * N, W), f32),
            pltpu.VMEM((RING, K, 2 * N, W), f32),
            pltpu.VMEM((3, slots, 8, 128), f32),
            dma((6 + 2 * K,)),
            dma((5 + K,)),
            dma((RING, K)),
            dma((RING, K)),
            dma((K, 2)),
            dma((K, 2)),
            dma((K, 2)),
            dma((K, 2)),
            dma((K, 2)),
            dma((K, 2)),
            dma((RING, K)),
            dma((RING, K)),
            dma((3, slots)),
            dma((3, slots)),
        ],
        compiler_params=pltpu.CompilerParams(
            collective_id=0, has_side_effects=True, vmem_limit_bytes=60 << 20
        ),
        name="ssd_backward",
    )(
        inputs[0], grad_out[0], b_proj[0].T, c_proj[0].T, step_sizes[0],
        a_log[None], skip_gain[None], doc_lengths,
    )
    plan = [(0, slice(lo, lo + 512)) for lo in range(0, HD, 512)] + [(i, slice(None)) for i in range(1, len(outs))]
    dx, db, dc, dstep, dalog, dskip = pl.pallas_call(
        functools.partial(write_out, plan),
        out_shape=outs,
        in_specs=[hbm] * 6,
        out_specs=(hbm,) * 6,
        scratch_shapes=[*(pltpu.VMEM(o.shape, o.dtype) for o in outs), dma((len(plan),)), dma((len(plan),))],
        compiler_params=pltpu.CompilerParams(vmem_limit_bytes=60 << 20),
        name="write_out",
    )(*results)
    return dx[None], db.T[None], dc.T[None], dstep[None], dalog[0], dskip[0]


def solution(mesh):
    tokens, heads = P("dp", "ctx", None), P("dp", None, "ctx")
    n_dp, n_ctx = mesh.shape["dp"], mesh.shape["ctx"]
    n_z = min(8, n_ctx // RING)
    return jax.shard_map(
        functools.partial(per_device, n_dp, n_ctx, n_z),
        mesh=mesh,
        in_specs=(tokens, tokens, tokens, heads, P(), P(), P("dp", None), tokens),
        out_specs=(tokens, tokens, tokens, heads, P(), P()),
        check_vma=False,
    )
```

```python
import functools

import jax
import jax.numpy as jnp
from jax import lax
from jax.experimental import pallas as pl
from jax.experimental.pallas import tpu as pltpu
from jax.sharding import PartitionSpec as P

MESH = pl.DeviceIdType.MESH
f32, bf16 = jnp.float32, jnp.bfloat16

MOST_DOC = 2048
RING = 4
CHUNKS = 4
ORDER = (
    ("total", 0), ("total", 1), ("pair", 0), ("total", 2), ("pair", 1), ("total", 3), ("pair", 2), ("give", 0),
    ("pair", 3), ("give", 1), ("give", 2), ("finish", 0), ("give", 3), ("finish", 1), ("finish", 2), ("finish", 3),
)


def nn(a, b):
    return lax.dot_general(a, b, (((1,), (0,)), ((), ())), preferred_element_type=f32)


def nt(a, b):
    return lax.dot_general(a, b, (((1,), (1,)), ((), ())), preferred_element_type=f32)


def split(v, count):
    pieces = []
    for i in range(count):
        piece = v.astype(bf16)
        pieces.append(piece)
        if i + 1 < count:
            v = v - piece.astype(f32)
    return pieces


def kernel(
    dims,
    x_hbm, g_hbm, bt_hbm, ct_hbm, dt_hbm, alog_hbm, skip_hbm, len_hbm,
    dx_hbm, db_hbm, dc_hbm, dstep_hbm, dalog_hbm, dskip_hbm,
    dx_ref, db_ref, dc_ref, dstep_ref, dalog_ref, dskip_ref,
    x_ref, g_ref, bt_ref, ct_ref, dt_ref, alog_ref, skip_ref, len_ref,
    xh, gh, bd, z1, z2, rowv, vecs, sa, ra, s1, r1, s2, r2, r3, sc, rc, ar,
    load, store, sa_send, sa_recv, s1_send, r1_recv, s2_send, r2_recv, s3_send, r3_recv, sc_send, sc_recv, ar_send, ar_recv, known,
):
    n_dp, n_ctx, n_z, T, H, D, N, DOCS = dims
    n_x = n_ctx // (n_z * RING)
    groups = n_ctx // RING
    W = H * D // (RING * CHUNKS)
    C = RING * W
    dp, me = lax.axis_index("dp"), lax.axis_index("ctx")
    y, group = me % RING, me // RING
    z, xhi = group % n_z, group // n_z

    y_peers = [(d, (y + d) % RING) for d in (2, 1, 3)]
    z_near = [(dp, ((group + d) % groups) * RING + y) for d in (1, groups - 1)]
    z_far = [(dp, ((group + d + groups) % groups) * RING + y) for d in (3, -3)]
    n_core = 2 - n_dp % 2
    xlo, core = dp // n_core, dp % n_core
    n_plane, n_line = RING * (n_dp // n_core) * n_x, n_z * n_core
    plane, line = (xlo * n_x + xhi) * RING + y, z * n_core + core
    plane_peers, line_peers = [], []
    for d in range(1, n_plane):
        other = (plane + d) % n_plane
        across = other // RING
        plane_peers.append(((across // n_x) * n_core + core, ((across % n_x) * n_z + z) * RING + other % RING))
    for d in range(1, n_line):
        other = (line + d) % n_line
        line_peers.append((xlo * n_core + other % n_core, (xhi * n_z + other // n_core) * RING + y))

    pairs = [(len_hbm, len_ref), (dt_hbm, dt_ref), (alog_hbm, alog_ref), (bt_hbm, bt_ref), (ct_hbm, ct_ref), (skip_hbm, skip_ref)]
    small = len(pairs)
    for k in range(CHUNKS):
        at = slice(k * C, (k + 1) * C)
        pairs += [(g_hbm.at[:, at], g_ref.at[:, at]), (x_hbm.at[:, at], x_ref.at[:, at])]
    loads = [pltpu.make_async_copy(a, b, load.at[i]) for i, (a, b) in enumerate(pairs)]
    for copy in loads[: small + 2]:
        copy.start()

    x_peers, core_peers = [], []
    for d in range(1, n_plane // RING):
        other = (plane // RING + d) % (n_plane // RING)
        x_peers.append(((other // n_x) * n_core + core, ((other % n_x) * n_z + z) * RING + y))
    for d in range(1, n_core):
        core_peers.append((xlo * n_core + (core + d) % n_core, me))
    barrier = pltpu.get_barrier_semaphore()
    greeted = [(dp, group * RING + q) for _, q in y_peers]
    greeted += z_near + z_far + x_peers + core_peers
    greeted += [(dp, (xhi * n_z + (z + d) % n_z) * RING + y) for d in range(1, n_z)]
    for target in greeted:
        pl.semaphore_signal(barrier, inc=1, device_id=target, device_id_type=MESH)
    for copy in loads[small + 2 :]:
        copy.start()

    rows = lax.broadcasted_iota(jnp.int32, (T, T), 0)
    cols = lax.broadcasted_iota(jnp.int32, (T, T), 1)
    tril = jnp.where(rows >= cols, 1.0, 0.0).astype(bf16)
    eye = jnp.where(rows == cols, 1.0, 0.0).astype(bf16)
    head_r = lax.broadcasted_iota(jnp.int32, (H, H), 0)
    head_c = lax.broadcasted_iota(jnp.int32, (H, H), 1)

    def one_hot(k, copies):
        heads = lax.broadcasted_iota(jnp.int32, (copies * H, C), 0) % H
        lanes = lax.broadcasted_iota(jnp.int32, (copies * H, C), 1) + k * C
        return jnp.where(lanes // D == heads, 1.0, 0.0).astype(bf16)

    for copy in loads[:small]:
        copy.wait()

    offset = me * T
    lengths = len_ref[...]
    doc_r = lax.broadcasted_iota(jnp.int32, (DOCS, DOCS), 0)
    doc_c = lax.broadcasted_iota(jnp.int32, (DOCS, DOCS), 1)
    length_col = jnp.sum(jnp.where(doc_r == doc_c, lengths, 0), axis=1, keepdims=True)
    start_col = jnp.sum(jnp.where(doc_c < doc_r, lengths, 0), axis=1, keepdims=True)
    start_row = jnp.sum(jnp.where(doc_r < doc_c, length_col, 0), axis=0, keepdims=True)
    place_row = lax.broadcasted_iota(jnp.int32, (DOCS, T), 1) + offset
    place_col = lax.broadcasted_iota(jnp.int32, (T, DOCS), 0) + offset
    seg_row = jnp.sum(jnp.where(start_col <= place_row, 1.0, 0.0), axis=0, keepdims=True)
    seg_col = jnp.sum(jnp.where(start_row <= place_col, 1.0, 0.0), axis=1, keepdims=True)
    before = jnp.sum(jnp.where(start_row <= offset - 1, 1.0, 0.0), axis=1, keepdims=True)
    last = jnp.sum(jnp.where(start_row <= offset + T - 1, 1.0, 0.0), axis=1, keepdims=True)
    same = seg_col == seg_row
    allowed = jnp.logical_and(rows >= cols, same)
    allowed_t = jnp.logical_and(cols >= rows, same)
    living_col = jnp.where(seg_col == before, 1.0, 0.0)
    ending_col = jnp.where(seg_col == last, 1.0, 0.0)
    living_row = jnp.where(seg_row == before, 1.0, 0.0)
    ending_row = jnp.where(seg_row == last, 1.0, 0.0)
    through_flag = jnp.where(last == before, 1.0, 0.0)

    dt = dt_ref[...]
    cum_dt, dt_t, cum_row = jnp.zeros((T, H), f32), jnp.zeros((T, H), f32), jnp.zeros((H, T), f32)
    for piece in split(dt, 3):
        cum_dt = cum_dt + nt(tril, piece)
        dt_t = dt_t + nt(eye, piece)
        cum_row = cum_row + nt(piece, tril)
    rate = -jnp.exp(alog_ref[...])
    cum = cum_dt * rate
    alpha = jnp.exp(cum)
    beta = jnp.exp(-cum) * dt_t
    spread = jnp.concatenate(
        [
            jnp.concatenate(split(alpha, 3), axis=1),
            jnp.concatenate(split(beta, 3), axis=1),
        ],
        axis=0,
    )
    skip3 = jnp.concatenate(split(jnp.broadcast_to(skip_ref[...], (16, H)), 3), axis=1)

    bt, ct = bt_ref[...], ct_ref[...]
    b32, c32 = nt(eye, bt), nt(eye, ct)
    bb, cc = b32.astype(bf16), c32.astype(bf16)
    eb_t = (bt.astype(f32) * ending_row).astype(bf16)
    lc_t = (ct.astype(f32) * living_row).astype(bf16)
    eb_t = jnp.concatenate([eb_t, eb_t], axis=1)
    lc_t = jnp.concatenate([lc_t, lc_t], axis=1)
    eb = (b32 * ending_col).astype(bf16)
    lc = (c32 * living_col).astype(bf16)
    eb = jnp.concatenate([eb, eb], axis=1)
    lc = jnp.concatenate([lc, lc], axis=1)

    sent = []

    def send(src, dst, ssem, rsem, target):
        copy = pltpu.make_async_remote_copy(
            src_ref=src, dst_ref=dst, send_sem=ssem, recv_sem=rsem, device_id=target, device_id_type=MESH
        )
        copy.start()
        sent.append(copy)

    stored = []

    def store_out(src, dst):
        copy = pltpu.make_async_copy(src, dst, store.at[len(stored)])
        copy.start()
        stored.append(copy)

    def arrived(ref, sem):
        pltpu.make_async_remote_copy(
            src_ref=ref, dst_ref=ref, send_sem=sem, recv_sem=sem, device_id=(dp, me), device_id_type=MESH
        ).wait_recv()

    s_hi, s_lo = split(jnp.where(allowed, nn(cc, bt), 0.0), 2)
    t_hi, t_lo = split(jnp.where(allowed_t, nn(bb, ct), 0.0), 2)
    s_hi = jnp.concatenate([s_hi, s_hi], axis=1)
    t_hi = jnp.concatenate([t_hi, t_hi], axis=1)
    scores = [jnp.zeros((T, 2 * T), f32), jnp.zeros((T, T), f32)]

    def states(k):
        at = slice(k * C, (k + 1) * C)
        hot = one_hot(k, 3)
        wide = nn(spread, hot)
        alpha_w, beta_w = wide[:T], wide[T:]
        for copy in loads[small + 2 * k : small + 2 * k + 2]:
            copy.wait()
        g = g_ref[:, at].astype(f32)
        x = x_ref[:, at].astype(f32)
        g_hi, g_lo = split(g * alpha_w, 2)
        x_hi, x_lo = split(x * beta_w, 2)
        gh[0:T, at], gh[T : 2 * T, at] = g_hi, g_lo
        xh[0:T, at], xh[T : 2 * T, at] = x_hi, x_lo
        last_alpha = alpha_w[T - 1 : T]
        own_states = nn(eb_t, xh[:, at]) * last_alpha
        backs = nn(lc_t, gh[:, at])
        through = jnp.broadcast_to(last_alpha * through_flag, (8, C))
        for q in range(RING):
            part = slice(q * W, (q + 1) * W)
            sa[q, k, 0:N, :] = own_states[:, part]
            sa[q, k, N : 2 * N, :] = backs[:, part]
            sa[q, k, 2 * N : 2 * N + 8, :] = through[:, part]
        if k == 0:
            pl.semaphore_wait(barrier, len(greeted))
        for _, q in y_peers:
            send(sa.at[q, k], ra.at[y, k], sa_send.at[q, k], sa_recv.at[y, k], (dp, group * RING + q))
        ra[y, k] = sa[y, k]
        rowv[0:8, at] = nn(skip3, hot)[0:8]
        rowv[8:16, at] = jnp.broadcast_to(last_alpha, (8, C))
        vecs[:, at] = jnp.broadcast_to(jnp.sum(g * x, axis=0, keepdims=True), (8, C))
        bd[:, at] = beta_w

    def within(k):
        at = slice(k * C, (k + 1) * C)
        xp, gp = xh[:, at], gh[:, at]
        z2[:, at] = nn(s_hi, xp) + nn(s_lo, xp[:T])
        z1[:, at] = nn(t_hi, gp) + nn(t_lo, gp[:T])
        scores[0] = scores[0] + nt(gp[:T], xp)
        scores[1] = scores[1] + nt(gp[T:], xp[:T])

    for k in range(CHUNKS):
        states(k)
    for target in x_peers + core_peers:
        pl.semaphore_signal(known, inc=1, device_id=target, device_id_type=MESH)
    for k in range(CHUNKS):
        within(k)
    ds = jnp.where(allowed, scores[0][:, :T] + scores[0][:, T:] + scores[1], 0.0)
    dc, db = jnp.zeros((N, T), f32), jnp.zeros((N, T), f32)
    for piece in split(ds, 2):
        dc = dc + nt(bt, piece)
        db = db + nn(ct, piece)

    def through_of(r, k):
        return ra[r, k, 2 * N : 2 * N + 1, :]

    def own(r, k):
        return ra[r, k, 0:N, :]

    def pulled(r, k):
        return ra[r, k, N : 2 * N, :]

    def total(k):
        for _, q in y_peers:
            arrived(ra.at[q, k], sa_recv.at[q, k])
        up, down = own(0, k), pulled(RING - 1, k)
        across = through_of(0, k)
        for i in range(1, RING):
            j = RING - 1 - i
            up = own(i, k) + through_of(i, k) * up
            down = pulled(j, k) + through_of(j, k) * down
            across = across * through_of(i, k)
        for side, value in ((0, up), (1, down)):
            s1[k, side, 0:N, :] = value
            s1[k, side, N : N + 8, :] = jnp.broadcast_to(across, (8, W))
            send(s1.at[k, side], r1.at[k, side], s1_send.at[k, side], r1_recv.at[k, side], z_near[side])

    def pair(k):
        for side in (0, 1):
            arrived(r1.at[k, side], r1_recv.at[k, side])
            across = s1[k, side, N : N + 8, :]
            s2[k, side, 0:N, :] = s1[k, side, 0:N, :] + across[0:1] * r1[k, side, 0:N, :]
            s2[k, side, N : N + 8, :] = across * r1[k, side, N : N + 8, :]
            send(
                s2.at[k, side, 0:N, :], r3.at[k, side], s3_send.at[k, side], r3_recv.at[k, side], z_far[side]
            )
            send(s2.at[k, side], r2.at[k, side], s2_send.at[k, side], r2_recv.at[k, side], z_near[side])

    def give(k):
        enters = []
        for side in (0, 1):
            arrived(r2.at[k, side], r2_recv.at[k, side])
            arrived(r3.at[k, side], r3_recv.at[k, side])
            enters.append(r2[k, side, 0:N, :] + r2[k, side, N : N + 1, :] * r3[k, side])
        up, down = enters
        for i in range(RING):
            j = RING - 1 - i
            sc[i, k, 0:N, :] = up
            sc[j, k, N : 2 * N, :] = down
            if i + 1 < RING:
                up = own(i, k) + through_of(i, k) * up
                down = pulled(j, k) + through_of(j, k) * down
        for _, q in y_peers:
            send(sc.at[q, k], rc.at[y, k], sc_send.at[q, k], sc_recv.at[y, k], (dp, group * RING + q))
        rc[y, k] = sc[y, k]

    sums = [jnp.zeros((H, 2 * T), f32), jnp.zeros((H, 2 * T), f32), jnp.zeros((2 * N, 2 * T), f32), jnp.zeros((2 * N, 2 * T), f32), jnp.zeros((H, 8), f32)]

    def finish(k):
        at = slice(k * C, (k + 1) * C)
        for _, q in y_peers:
            arrived(rc.at[q, k], sc_recv.at[q, k])
        hot = one_hot(k, 1)
        state = jnp.concatenate([rc[q, k, 0:N, :] for q in range(RING)], axis=1)
        later = jnp.concatenate([rc[q, k, N : 2 * N, :] for q in range(RING)], axis=1)
        mine = jnp.concatenate([sa[q, k, 0:N, :] for q in range(RING)], axis=1)
        last_alpha = rowv[8:9, at]
        leaving = jnp.sum(later * (mine + last_alpha * through_flag * state), axis=0, keepdims=True)
        first_row = lax.broadcasted_iota(jnp.int32, (8, C), 0) == 0
        vec = jnp.where(first_row, leaving, vecs[:, at])
        hh = jnp.concatenate(split(state, 2), axis=0)
        fh = jnp.concatenate(split(later * last_alpha, 2), axis=0)
        z1_w = z1[:, at] + nn(eb, fh)
        z2_w = z2[:, at] + nn(lc, hh)
        gp, xp = gh[:, at], xh[:, at]
        p1 = z1_w * (xp[:T].astype(f32) + xp[T:].astype(f32))
        p2 = z2_w * (gp[:T].astype(f32) + gp[T:].astype(f32))
        dx_ref[:, at] = (bd[:, at] * z1_w + rowv[0:1, at] * g_ref[:, at].astype(f32)).astype(bf16)
        store_out(dx_ref.at[:, at], dx_hbm.at[:, at])
        sums[0] = sums[0] + nt(hot, jnp.concatenate(split(p1, 2), axis=0))
        sums[1] = sums[1] + nt(hot, jnp.concatenate(split(p2, 2), axis=0))
        sums[2] = sums[2] + nt(hh, gp)
        sums[3] = sums[3] + nt(fh, xp)
        for piece in split(vec, 3):
            sums[4] = sums[4] + nt(hot, piece)

    steps = {"total": total, "pair": pair, "give": give, "finish": finish}
    for name, k in ORDER:
        steps[name](k)

    col_q = sums[0][:, :T] + sums[0][:, T:]
    row_q = sums[1][:, :T] + sums[1][:, T:]
    d_cum = row_q - col_q
    d_end, d_skip = sums[4][:, 0:1], sums[4][:, 1:2]
    rate_c = jnp.sum(jnp.where(head_r == head_c, jnp.broadcast_to(rate, (H, H)), 0.0), axis=1, keepdims=True)
    at_end = cols[:H] == T - 1
    d_alog = rate_c * jnp.sum((d_cum + jnp.where(at_end, d_end, 0.0)) * cum_row, axis=1, keepdims=True)
    part = jnp.where(rows[:H] == cols[:H], d_alog, jnp.where(rows[:H] + H == cols[:H], d_skip, 0.0))
    part = jnp.sum(part, axis=0, keepdims=True)

    stages = ((plane, n_plane, plane_peers), (line, n_line, line_peers))
    pl.semaphore_wait(known, len(x_peers) + len(core_peers))
    for s, (mine, count, peers) in enumerate(stages):
        ar[s, mine] = part
        for d, target in enumerate(peers, 1):
            send(ar.at[s, mine], ar.at[s, mine], ar_send.at[s, d], ar_recv.at[s, mine], target)
        if s == 0:
            acc = sums[2][:N] + sums[2][N:]
            dc_ref[...] = (dc + living_row * (acc[:, :T] + acc[:, T:])).astype(bf16)
            acc = sums[3][:N] + sums[3][N:]
            db_ref[...] = (db + ending_row * (acc[:, :T] + acc[:, T:])).astype(bf16)
            d_log = jnp.zeros((H, T), f32) + d_end
            for piece in split(d_cum, 3):
                d_log = d_log + nn(piece, tril)
            dstep_ref[...] = col_q / dt + d_log * rate_c
            for src, dst in ((dc_ref, dc_hbm), (db_ref, db_hbm), (dstep_ref, dstep_hbm)):
                store_out(src, dst)
        for d in range(1, count):
            other = (mine + d) % count
            arrived(ar.at[s, other], ar_recv.at[s, other])
        part = ar[s, 0]
        for i in range(1, count):
            part = part + ar[s, i]
    dalog_ref[...] = part[:, :H]
    dskip_ref[...] = part[:, H : 2 * H]
    store_out(dalog_ref, dalog_hbm)
    store_out(dskip_ref, dskip_hbm)
    for copy in sent:
        copy.wait_send()
    for copy in stored:
        copy.wait()


def write_out(plan, *refs):
    count = len(refs) // 3
    sources, targets, places, loaded, stored = refs[:count], refs[count : 2 * count], refs[2 * count : 3 * count], *refs[-2:]
    copies = []
    for n, (i, at) in enumerate(plan):
        load = pltpu.make_async_copy(sources[i].at[:, at], places[i].at[:, at], loaded.at[n])
        copies.append((load, pltpu.make_async_copy(places[i].at[:, at], targets[i].at[:, at], stored.at[n])))
        load.start()
    for load, store in copies:
        load.wait()
        store.start()
    for _, store in copies:
        store.wait()


def per_device(n_dp, n_ctx, n_z, inputs, b_proj, c_proj, step_sizes, a_log, skip_gain, doc_lengths, grad_out):
    T, H, N = inputs.shape[1], a_log.shape[0], b_proj.shape[2]
    D, DOCS = inputs.shape[2] // H, doc_lengths.shape[1]
    HD = H * D
    K, W = CHUNKS, HD // (RING * CHUNKS)
    assert 4 * RING * T >= MOST_DOC
    n_x = n_ctx // (n_z * RING)
    slots = max(RING * n_dp * n_x, 2 * n_z)
    dims = (n_dp, n_ctx, n_z, T, H, D, N, DOCS)
    hbm = pl.BlockSpec(memory_space=pltpu.HBM)
    dma = pltpu.SemaphoreType.DMA
    outs = (
        jax.ShapeDtypeStruct((T, HD), bf16),
        jax.ShapeDtypeStruct((N, T), bf16),
        jax.ShapeDtypeStruct((N, T), bf16),
        jax.ShapeDtypeStruct((H, T), f32),
        jax.ShapeDtypeStruct((1, H), f32),
        jax.ShapeDtypeStruct((1, H), f32),
    )
    results = pl.pallas_call(
        functools.partial(kernel, dims),
        out_shape=outs,
        in_specs=[hbm] * 8,
        out_specs=(hbm,) * 6,
        scratch_shapes=[
            *(pltpu.VMEM(o.shape, o.dtype) for o in outs),
            pltpu.VMEM((T, HD), bf16),
            pltpu.VMEM((T, HD), bf16),
            pltpu.VMEM((N, T), bf16),
            pltpu.VMEM((N, T), bf16),
            pltpu.VMEM((H, T), f32),
            pltpu.VMEM((1, H), f32),
            pltpu.VMEM((1, H), f32),
            pltpu.VMEM((1, DOCS), jnp.int32),
            pltpu.VMEM((2 * T, HD), bf16),
            pltpu.VMEM((2 * T, HD), bf16),
            pltpu.VMEM((T, HD), f32),
            pltpu.VMEM((T, HD), f32),
            pltpu.VMEM((T, HD), f32),
            pltpu.VMEM((16, HD), f32),
            pltpu.VMEM((8, HD), f32),
            pltpu.VMEM((RING, K, 2 * N + 8, W), f32),
            pltpu.VMEM((RING, K, 2 * N + 8, W), f32),
            pltpu.VMEM((K, 2, N + 8, W), f32),
            pltpu.VMEM((K, 2, N + 8, W), f32),
            pltpu.VMEM((K, 2, N + 8, W), f32),
            pltpu.VMEM((K, 2, N + 8, W), f32),
            pltpu.VMEM((K, 2, N, W), f32),
            pltpu.VMEM((RING, K, 2 * N, W), f32),
            pltpu.VMEM((RING, K, 2 * N, W), f32),
            pltpu.VMEM((2, slots, 1, 128), f32),
            dma((6 + 2 * K,)),
            dma((5 + K,)),
            dma((RING, K)),
            dma((RING, K)),
            dma((K, 2)),
            dma((K, 2)),
            dma((K, 2)),
            dma((K, 2)),
            dma((K, 2)),
            dma((K, 2)),
            dma((RING, K)),
            dma((RING, K)),
            dma((2, slots)),
            dma((2, slots)),
            pltpu.SemaphoreType.REGULAR,
        ],
        compiler_params=pltpu.CompilerParams(
            collective_id=0, has_side_effects=True, vmem_limit_bytes=60 << 20
        ),
        name="ssd_backward",
    )(
        inputs[0], grad_out[0], b_proj[0].T, c_proj[0].T, step_sizes[0],
        a_log[None], skip_gain[None], doc_lengths,
    )
    plan = [(0, slice(lo, lo + 512)) for lo in range(0, HD, 512)] + [(i, slice(None)) for i in range(1, len(outs))]
    dx, db, dc, dstep, dalog, dskip = pl.pallas_call(
        functools.partial(write_out, plan),
        out_shape=outs,
        in_specs=[hbm] * 6,
        out_specs=(hbm,) * 6,
        scratch_shapes=[*(pltpu.VMEM(o.shape, o.dtype) for o in outs), dma((len(plan),)), dma((len(plan),))],
        compiler_params=pltpu.CompilerParams(vmem_limit_bytes=60 << 20),
        name="write_out",
    )(*results)
    return dx[None], db.T[None], dc.T[None], dstep[None], dalog[0], dskip[0]


def solution(mesh):
    tokens, heads = P("dp", "ctx", None), P("dp", None, "ctx")
    n_dp, n_ctx = mesh.shape["dp"], mesh.shape["ctx"]
    n_z = min(8, n_ctx // RING)
    return jax.shard_map(
        functools.partial(per_device, n_dp, n_ctx, n_z),
        mesh=mesh,
        in_specs=(tokens, tokens, tokens, heads, P(), P(), P("dp", None), tokens),
        out_specs=(tokens, tokens, tokens, heads, P(), P()),
        check_vma=False,
    )
```

```python
import functools

import jax
import jax.numpy as jnp
from jax import lax
from jax.experimental import pallas as pl
from jax.experimental.pallas import tpu as pltpu
from jax.sharding import PartitionSpec as P

MESH = pl.DeviceIdType.MESH
f32, bf16 = jnp.float32, jnp.bfloat16

MOST_DOC = 2048
RING = 4
CHUNKS = 4
ORDER = (
    ("total", 0), ("total", 1), ("pair", 0), ("total", 2), ("pair", 1), ("total", 3), ("pair", 2), ("give", 0),
    ("pair", 3), ("give", 1), ("give", 2), ("finish", 0), ("give", 3), ("finish", 1), ("finish", 2), ("finish", 3),
)


def nn(a, b):
    return lax.dot_general(a, b, (((1,), (0,)), ((), ())), preferred_element_type=f32)


def nt(a, b):
    return lax.dot_general(a, b, (((1,), (1,)), ((), ())), preferred_element_type=f32)


def split(v, count):
    pieces = []
    for i in range(count):
        piece = v.astype(bf16)
        pieces.append(piece)
        if i + 1 < count:
            v = v - piece.astype(f32)
    return pieces


def kernel(
    dims,
    x_hbm, g_hbm, bt_hbm, ct_hbm, dt_hbm, alog_hbm, skip_hbm, len_hbm,
    dx_hbm, db_hbm, dc_hbm, dstep_hbm, dalog_hbm, dskip_hbm,
    dx_ref, db_ref, dc_ref, dstep_ref, dalog_ref, dskip_ref,
    x_ref, g_ref, bt_ref, ct_ref, dt_ref, alog_ref, skip_ref, len_ref,
    xh, gh, bd, z1, z2, rowv, vecs, sa, ra, st, rt, s1, r1, s2, r2, r3, sc, rc, ar,
    load, store, sa_send, sa_recv, s1_send, r1_recv, s2_send, r2_recv, s3_send, r3_recv, sc_send, sc_recv, st_send, rt_recv, ar_send, ar_recv, known,
):
    n_dp, n_ctx, n_z, T, H, D, N, DOCS = dims
    n_x = n_ctx // (n_z * RING)
    groups = n_ctx // RING
    W = H * D // (RING * CHUNKS)
    C = RING * W
    dp, me = lax.axis_index("dp"), lax.axis_index("ctx")
    y, group = me % RING, me // RING
    z, xhi = group % n_z, group // n_z

    y_peers = [(d, (y + d) % RING) for d in (2, 1, 3)]
    z_near = [(dp, ((group + d) % groups) * RING + y) for d in (1, groups - 1)]
    z_far = [(dp, ((group + d + groups) % groups) * RING + y) for d in (3, -3)]
    n_core = 2 - n_dp % 2
    xlo, core = dp // n_core, dp % n_core
    n_plane, n_line = RING * (n_dp // n_core) * n_x, n_z * n_core
    plane_peers, line_peers = [], []
    n_lane = n_plane // RING
    lane, n_xlo = xhi * (n_dp // n_core) + xlo, n_dp // n_core
    plane, line = lane * RING + y, z * n_core + core

    def far(step, size):
        return min(step, size - step)

    steps = [(a, b) for a in range(n_lane) for b in range(RING) if (a, b) != (0, 0)]
    for a, b in sorted(steps, key=lambda s: -far(s[0], n_lane) - far(s[1], RING)):
        other = (lane + a) % n_lane
        plane_peers.append(((other % n_xlo) * n_core + core, ((other // n_xlo) * n_z + z) * RING + (y + b) % RING))
    steps = [(a, b) for a in range(n_z) for b in range(n_core) if (a, b) != (0, 0)]
    for a, b in sorted(steps, key=lambda s: -far(s[0], n_z) - 0.5 * s[1]):
        line_peers.append((xlo * n_core + (core + b) % n_core, (xhi * n_z + (z + a) % n_z) * RING + y))

    pairs = [(len_hbm, len_ref), (dt_hbm, dt_ref), (alog_hbm, alog_ref), (bt_hbm, bt_ref), (ct_hbm, ct_ref), (skip_hbm, skip_ref)]
    small = len(pairs)
    for k in range(CHUNKS):
        at = slice(k * C, (k + 1) * C)
        pairs += [(g_hbm.at[:, at], g_ref.at[:, at]), (x_hbm.at[:, at], x_ref.at[:, at])]
    loads = [pltpu.make_async_copy(a, b, load.at[i]) for i, (a, b) in enumerate(pairs)]
    for copy in loads[: small + 2]:
        copy.start()

    x_peers, core_peers = [], []
    for a in range(1, n_lane):
        other = (lane + a) % n_lane
        x_peers.append(((other % n_xlo) * n_core + core, ((other // n_xlo) * n_z + z) * RING + y))
    for b in range(1, n_core):
        core_peers.append((xlo * n_core + (core + b) % n_core, me))
    barrier = pltpu.get_barrier_semaphore()
    greeted = [(dp, group * RING + q) for _, q in y_peers]
    greeted += z_near + z_far + x_peers + core_peers
    greeted += [(dp, (xhi * n_z + (z + d) % n_z) * RING + y) for d in range(1, n_z)]
    for target in greeted:
        pl.semaphore_signal(barrier, inc=1, device_id=target, device_id_type=MESH)
    for copy in loads[small + 2 :]:
        copy.start()

    rows = lax.broadcasted_iota(jnp.int32, (T, T), 0)
    cols = lax.broadcasted_iota(jnp.int32, (T, T), 1)
    tril = jnp.where(rows >= cols, 1.0, 0.0).astype(bf16)
    eye = jnp.where(rows == cols, 1.0, 0.0).astype(bf16)
    head_r = lax.broadcasted_iota(jnp.int32, (H, H), 0)
    head_c = lax.broadcasted_iota(jnp.int32, (H, H), 1)

    def one_hot(k, copies):
        heads = lax.broadcasted_iota(jnp.int32, (copies * H, C), 0) % H
        lanes = lax.broadcasted_iota(jnp.int32, (copies * H, C), 1) + k * C
        return jnp.where(lanes // D == heads, 1.0, 0.0).astype(bf16)

    for copy in loads[:small]:
        copy.wait()

    offset = me * T
    lengths = len_ref[...]
    doc_r = lax.broadcasted_iota(jnp.int32, (DOCS, DOCS), 0)
    doc_c = lax.broadcasted_iota(jnp.int32, (DOCS, DOCS), 1)
    length_col = jnp.sum(jnp.where(doc_r == doc_c, lengths, 0), axis=1, keepdims=True)
    start_col = jnp.sum(jnp.where(doc_c < doc_r, lengths, 0), axis=1, keepdims=True)
    start_row = jnp.sum(jnp.where(doc_r < doc_c, length_col, 0), axis=0, keepdims=True)
    place_row = lax.broadcasted_iota(jnp.int32, (DOCS, T), 1) + offset
    place_col = lax.broadcasted_iota(jnp.int32, (T, DOCS), 0) + offset
    seg_row = jnp.sum(jnp.where(start_col <= place_row, 1.0, 0.0), axis=0, keepdims=True)
    seg_col = jnp.sum(jnp.where(start_row <= place_col, 1.0, 0.0), axis=1, keepdims=True)
    before = jnp.sum(jnp.where(start_row <= offset - 1, 1.0, 0.0), axis=1, keepdims=True)
    last = jnp.sum(jnp.where(start_row <= offset + T - 1, 1.0, 0.0), axis=1, keepdims=True)
    same = seg_col == seg_row
    allowed = jnp.logical_and(rows >= cols, same)
    allowed_t = jnp.logical_and(cols >= rows, same)
    living_col = jnp.where(seg_col == before, 1.0, 0.0)
    ending_col = jnp.where(seg_col == last, 1.0, 0.0)
    living_row = jnp.where(seg_row == before, 1.0, 0.0)
    ending_row = jnp.where(seg_row == last, 1.0, 0.0)
    through_flag = jnp.where(last == before, 1.0, 0.0)

    dt = dt_ref[...]
    cum_dt, dt_t = jnp.zeros((T, H), f32), jnp.zeros((T, H), f32)
    for piece in split(dt, 3):
        cum_dt = cum_dt + nt(tril, piece)
        dt_t = dt_t + nt(eye, piece)
    rate = -jnp.exp(alog_ref[...])
    cum = cum_dt * rate
    alpha = jnp.exp(cum)
    beta = jnp.exp(-cum) * dt_t
    spread = jnp.concatenate(
        [
            jnp.concatenate(split(alpha, 3), axis=1),
            jnp.concatenate(split(beta, 3), axis=1),
        ],
        axis=0,
    )
    skip3 = jnp.concatenate(split(jnp.broadcast_to(skip_ref[...], (16, H)), 3), axis=1)

    bt, ct = bt_ref[...], ct_ref[...]
    eb_t = (bt.astype(f32) * ending_row).astype(bf16)
    lc_t = (ct.astype(f32) * living_row).astype(bf16)
    eb_t = jnp.concatenate([eb_t, eb_t], axis=1)
    lc_t = jnp.concatenate([lc_t, lc_t], axis=1)

    sent = []

    def send(src, dst, ssem, rsem, target):
        pltpu.make_async_remote_copy(
            src_ref=src, dst_ref=dst, send_sem=ssem, recv_sem=rsem, device_id=target, device_id_type=MESH
        ).start()

    def waiter(ref, sem):
        return pltpu.make_async_remote_copy(
            src_ref=ref, dst_ref=ref, send_sem=sem, recv_sem=sem, device_id=(dp, me), device_id_type=MESH
        )

    stored = []

    def store_out(src, dst):
        copy = pltpu.make_async_copy(src, dst, store.at[len(stored)])
        copy.start()
        stored.append(copy)


    per = C // D
    row_k = lax.broadcasted_iota(jnp.int32, (8, H), 0)
    head_l = lax.broadcasted_iota(jnp.int32, (8, H), 1)
    mine = jnp.where(head_l // per == row_k, alpha[T - 1 : T] * through_flag, 0.0)
    head_s = lax.broadcasted_iota(jnp.int32, (H, C), 0)
    lane_s = lax.broadcasted_iota(jnp.int32, (H, C), 1)
    spots = jnp.where(head_s % per == lane_s // D, 1.0, 0.0).astype(bf16)
    tile = jnp.zeros((8, C), f32)
    for piece in split(mine, 3):
        tile = tile + nn(piece, spots)
    for q in range(RING):
        st[q] = tile[:, q * W : (q + 1) * W]

    def states(k):
        at = slice(k * C, (k + 1) * C)
        hot = one_hot(k, 3)
        wide = nn(spread, hot)
        alpha_w, beta_w = wide[:T], wide[T:]
        for copy in loads[small + 2 * k : small + 2 * k + 2]:
            copy.wait()
        g = g_ref[:, at].astype(f32)
        x = x_ref[:, at].astype(f32)
        g_hi, g_lo = split(g * alpha_w, 2)
        x_hi, x_lo = split(x * beta_w, 2)
        gh[0:T, at], gh[T : 2 * T, at] = g_hi, g_lo
        xh[0:T, at], xh[T : 2 * T, at] = x_hi, x_lo
        last_alpha = alpha_w[T - 1 : T]
        own_states = nn(eb_t, xh[:, at]) * last_alpha
        backs = nn(lc_t, gh[:, at])
        for q in range(RING):
            part = slice(q * W, (q + 1) * W)
            sa[q, k, 0:N, :] = own_states[:, part]
            sa[q, k, N : 2 * N, :] = backs[:, part]
        if k == 0:
            pl.semaphore_wait(barrier, len(greeted))
            for _, q in y_peers:
                send(st.at[q], rt.at[y], st_send.at[0], rt_recv.at[0], (dp, group * RING + q))
            sent.append((st.at[0 : RING - 1], st_send.at[0]))
            rt[y] = st[y]
        for _, q in y_peers:
            send(sa.at[q, k], ra.at[y, k], sa_send.at[k], sa_recv.at[k], (dp, group * RING + q))
        sent.append((sa.at[0 : RING - 1, k], sa_send.at[k]))
        ra[y, k] = sa[y, k]
        rowv[0:8, at] = nn(skip3, hot)[0:8]
        rowv[8:16, at] = jnp.broadcast_to(last_alpha, (8, C))
        vecs[:, at] = jnp.broadcast_to(jnp.sum(g * x, axis=0, keepdims=True), (8, C))
        bd[:, at] = beta_w

    def within(k):
        at = slice(k * C, (k + 1) * C)
        xp, gp = xh[:, at], gh[:, at]
        z2[:, at] = nn(s_hi, xp) + nn(s_lo, xp[:T])
        z1[:, at] = nn(t_hi, gp) + nn(t_lo, gp[:T])
        scores[0] = scores[0] + nt(gp[:T], xp)
        scores[1] = scores[1] + nt(gp[T:], xp[:T])

    for k in range(CHUNKS):
        states(k)
    for target in x_peers + core_peers:
        pl.semaphore_signal(known, inc=1, device_id=target, device_id_type=MESH)
    cum_row = jnp.zeros((H, T), f32)
    for piece in split(dt, 3):
        cum_row = cum_row + nt(piece, tril)
    b32, c32 = nt(eye, bt), nt(eye, ct)
    bb, cc = b32.astype(bf16), c32.astype(bf16)
    eb = (b32 * ending_col).astype(bf16)
    lc = (c32 * living_col).astype(bf16)
    eb = jnp.concatenate([eb, eb], axis=1)
    lc = jnp.concatenate([lc, lc], axis=1)
    s_hi, s_lo = split(jnp.where(allowed, nn(cc, bt), 0.0), 2)
    t_hi, t_lo = split(jnp.where(allowed_t, nn(bb, ct), 0.0), 2)
    s_hi = jnp.concatenate([s_hi, s_hi], axis=1)
    t_hi = jnp.concatenate([t_hi, t_hi], axis=1)
    scores = [jnp.zeros((T, 2 * T), f32), jnp.zeros((T, T), f32)]
    for k in range(CHUNKS):
        within(k)
    ds = jnp.where(allowed, scores[0][:, :T] + scores[0][:, T:] + scores[1], 0.0)
    dc, db = jnp.zeros((N, T), f32), jnp.zeros((N, T), f32)
    for piece in split(ds, 2):
        dc = dc + nt(bt, piece)
        db = db + nn(ct, piece)

    def through_of(r, k):
        return rt[r, k : k + 1, :]

    def own(r, k):
        return ra[r, k, 0:N, :]

    def pulled(r, k):
        return ra[r, k, N : 2 * N, :]

    def total(k):
        if k == 0:
            waiter(rt.at[0 : RING - 1], rt_recv.at[0]).wait_recv()
        waiter(ra.at[0 : RING - 1, k], sa_recv.at[k]).wait_recv()
        up, down = own(0, k), pulled(RING - 1, k)
        across = through_of(0, k)
        for i in range(1, RING):
            j = RING - 1 - i
            up = own(i, k) + through_of(i, k) * up
            down = pulled(j, k) + through_of(j, k) * down
            across = across * through_of(i, k)
        for side, value in ((0, up), (1, down)):
            s1[k, side, 0:N, :] = value
            s1[k, side, N : N + 8, :] = jnp.broadcast_to(across, (8, W))
            send(s1.at[k, side], r1.at[k, side], s1_send.at[k], r1_recv.at[k], z_near[side])
        sent.append((s1.at[k], s1_send.at[k]))

    def pair(k):
        waiter(r1.at[k], r1_recv.at[k]).wait_recv()
        for side in (0, 1):
            across = s1[k, side, N : N + 8, :]
            s2[k, side, 0:N, :] = s1[k, side, 0:N, :] + across[0:1] * r1[k, side, 0:N, :]
            s2[k, side, N : N + 8, :] = across * r1[k, side, N : N + 8, :]
            send(s2.at[k, side, 0:N, :], r3.at[k, side], s3_send.at[k], r3_recv.at[k], z_far[side])
            send(s2.at[k, side], r2.at[k, side], s2_send.at[k], r2_recv.at[k], z_near[side])
        sent.append((r3.at[k], s3_send.at[k]))
        sent.append((s2.at[k], s2_send.at[k]))

    def give(k):
        enters = []
        waiter(r2.at[k], r2_recv.at[k]).wait_recv()
        waiter(r3.at[k], r3_recv.at[k]).wait_recv()
        for side in (0, 1):
            enters.append(r2[k, side, 0:N, :] + r2[k, side, N : N + 1, :] * r3[k, side])
        up, down = enters
        for i in range(RING):
            j = RING - 1 - i
            sc[i, k, 0:N, :] = up
            sc[j, k, N : 2 * N, :] = down
            if i + 1 < RING:
                up = own(i, k) + through_of(i, k) * up
                down = pulled(j, k) + through_of(j, k) * down
        for _, q in y_peers:
            send(sc.at[q, k], rc.at[y, k], sc_send.at[k], sc_recv.at[k], (dp, group * RING + q))
        sent.append((sc.at[0 : RING - 1, k], sc_send.at[k]))
        rc[y, k] = sc[y, k]

    sums = [jnp.zeros((H, 2 * T), f32), jnp.zeros((H, 2 * T), f32), jnp.zeros((2 * N, 2 * T), f32), jnp.zeros((2 * N, 2 * T), f32), jnp.zeros((H, 8), f32)]

    def finish(k):
        at = slice(k * C, (k + 1) * C)
        waiter(rc.at[0 : RING - 1, k], sc_recv.at[k]).wait_recv()
        hot = one_hot(k, 1)
        state = jnp.concatenate([rc[q, k, 0:N, :] for q in range(RING)], axis=1)
        later = jnp.concatenate([rc[q, k, N : 2 * N, :] for q in range(RING)], axis=1)
        mine = jnp.concatenate([sa[q, k, 0:N, :] for q in range(RING)], axis=1)
        last_alpha = rowv[8:9, at]
        leaving = jnp.sum(later * (mine + last_alpha * through_flag * state), axis=0, keepdims=True)
        first_row = lax.broadcasted_iota(jnp.int32, (8, C), 0) == 0
        vec = jnp.where(first_row, leaving, vecs[:, at])
        hh = jnp.concatenate(split(state, 2), axis=0)
        fh = jnp.concatenate(split(later * last_alpha, 2), axis=0)
        z1_w = z1[:, at] + nn(eb, fh)
        z2_w = z2[:, at] + nn(lc, hh)
        gp, xp = gh[:, at], xh[:, at]
        p1 = z1_w * (xp[:T].astype(f32) + xp[T:].astype(f32))
        p2 = z2_w * (gp[:T].astype(f32) + gp[T:].astype(f32))
        sums[0] = sums[0] + nt(hot, jnp.concatenate(split(p1, 2), axis=0))
        sums[1] = sums[1] + nt(hot, jnp.concatenate(split(p2, 2), axis=0))
        for piece in split(vec, 3):
            sums[4] = sums[4] + nt(hot, piece)

        def remainder():
            dx_ref[:, at] = (bd[:, at] * z1_w + rowv[0:1, at] * g_ref[:, at].astype(f32)).astype(bf16)
            store_out(dx_ref.at[:, at], dx_hbm.at[:, at])
            sums[2] = sums[2] + nt(hh, gp)
            sums[3] = sums[3] + nt(fh, xp)

        if k + 1 < CHUNKS:
            remainder()
        else:
            put_off.append(remainder)

    put_off = []
    steps = {"total": total, "pair": pair, "give": give, "finish": finish}
    for name, k in ORDER:
        steps[name](k)

    col_q = sums[0][:, :T] + sums[0][:, T:]
    row_q = sums[1][:, :T] + sums[1][:, T:]
    d_cum = row_q - col_q
    d_end, d_skip = sums[4][:, 0:1], sums[4][:, 1:2]
    rate_c = jnp.sum(jnp.where(head_r == head_c, jnp.broadcast_to(rate, (H, H)), 0.0), axis=1, keepdims=True)
    at_end = cols[:H] == T - 1
    d_alog = rate_c * jnp.sum((d_cum + jnp.where(at_end, d_end, 0.0)) * cum_row, axis=1, keepdims=True)
    part = jnp.where(rows[:H] == cols[:H], d_alog, jnp.where(rows[:H] + H == cols[:H], d_skip, 0.0))
    part = jnp.sum(part, axis=0, keepdims=True)

    stages = ((plane, n_plane, plane_peers), (line, n_line, line_peers))
    pl.semaphore_wait(known, len(x_peers) + len(core_peers))
    for s, (mine, count, peers) in enumerate(stages):
        ar[s, mine] = part
        for target in peers:
            send(ar.at[s, mine], ar.at[s, mine], ar_send.at[s], ar_recv.at[s], target)
        if s == 0:
            for work in put_off:
                work()
            acc = sums[2][:N] + sums[2][N:]
            dc_ref[...] = (dc + living_row * (acc[:, :T] + acc[:, T:])).astype(bf16)
            acc = sums[3][:N] + sums[3][N:]
            db_ref[...] = (db + ending_row * (acc[:, :T] + acc[:, T:])).astype(bf16)
            d_log = jnp.zeros((H, T), f32) + d_end
            for piece in split(d_cum, 3):
                d_log = d_log + nn(piece, tril)
            dstep_ref[...] = col_q / dt + d_log * rate_c
            for src, dst in ((dc_ref, dc_hbm), (db_ref, db_hbm), (dstep_ref, dstep_hbm)):
                store_out(src, dst)
            for ref, sem in sent:
                waiter(ref, sem).wait_send()
        if peers:
            waiter(ar.at[s, 0 : count - 1], ar_recv.at[s]).wait_recv()
        part = ar[s, 0]
        for i in range(1, count):
            part = part + ar[s, i]
    dalog_ref[...] = part[:, :H]
    dskip_ref[...] = part[:, H : 2 * H]
    store_out(dalog_ref, dalog_hbm)
    store_out(dskip_ref, dskip_hbm)
    for s, (mine, count, peers) in enumerate(stages):
        if peers:
            waiter(ar.at[s, 0 : count - 1], ar_send.at[s]).wait_send()
    for copy in stored:
        copy.wait()


def write_out(plan, *refs):
    count = len(refs) // 3
    sources, targets, places, loaded, stored = refs[:count], refs[count : 2 * count], refs[2 * count : 3 * count], *refs[-2:]
    copies = []
    for n, (i, at) in enumerate(plan):
        load = pltpu.make_async_copy(sources[i].at[:, at], places[i].at[:, at], loaded.at[n])
        copies.append((load, pltpu.make_async_copy(places[i].at[:, at], targets[i].at[:, at], stored.at[n])))
        load.start()
    for load, store in copies:
        load.wait()
        store.start()
    for _, store in copies:
        store.wait()


def per_device(n_dp, n_ctx, n_z, inputs, b_proj, c_proj, step_sizes, a_log, skip_gain, doc_lengths, grad_out):
    T, H, N = inputs.shape[1], a_log.shape[0], b_proj.shape[2]
    D, DOCS = inputs.shape[2] // H, doc_lengths.shape[1]
    HD = H * D
    K, W = CHUNKS, HD // (RING * CHUNKS)
    assert 4 * RING * T >= MOST_DOC
    n_x = n_ctx // (n_z * RING)
    slots = max(RING * n_dp * n_x, 2 * n_z)
    dims = (n_dp, n_ctx, n_z, T, H, D, N, DOCS)
    hbm = pl.BlockSpec(memory_space=pltpu.HBM)
    dma = pltpu.SemaphoreType.DMA
    outs = (
        jax.ShapeDtypeStruct((T, HD), bf16),
        jax.ShapeDtypeStruct((N, T), bf16),
        jax.ShapeDtypeStruct((N, T), bf16),
        jax.ShapeDtypeStruct((H, T), f32),
        jax.ShapeDtypeStruct((1, H), f32),
        jax.ShapeDtypeStruct((1, H), f32),
    )
    results = pl.pallas_call(
        functools.partial(kernel, dims),
        out_shape=outs,
        in_specs=[hbm] * 8,
        out_specs=(hbm,) * 6,
        scratch_shapes=[
            *(pltpu.VMEM(o.shape, o.dtype) for o in outs),
            pltpu.VMEM((T, HD), bf16),
            pltpu.VMEM((T, HD), bf16),
            pltpu.VMEM((N, T), bf16),
            pltpu.VMEM((N, T), bf16),
            pltpu.VMEM((H, T), f32),
            pltpu.VMEM((1, H), f32),
            pltpu.VMEM((1, H), f32),
            pltpu.VMEM((1, DOCS), jnp.int32),
            pltpu.VMEM((2 * T, HD), bf16),
            pltpu.VMEM((2 * T, HD), bf16),
            pltpu.VMEM((T, HD), f32),
            pltpu.VMEM((T, HD), f32),
            pltpu.VMEM((T, HD), f32),
            pltpu.VMEM((16, HD), f32),
            pltpu.VMEM((8, HD), f32),
            pltpu.VMEM((RING, K, 2 * N, W), f32),
            pltpu.VMEM((RING, K, 2 * N, W), f32),
            pltpu.VMEM((RING, 8, W), f32),
            pltpu.VMEM((RING, 8, W), f32),
            pltpu.VMEM((K, 2, N + 8, W), f32),
            pltpu.VMEM((K, 2, N + 8, W), f32),
            pltpu.VMEM((K, 2, N + 8, W), f32),
            pltpu.VMEM((K, 2, N + 8, W), f32),
            pltpu.VMEM((K, 2, N, W), f32),
            pltpu.VMEM((RING, K, 2 * N, W), f32),
            pltpu.VMEM((RING, K, 2 * N, W), f32),
            pltpu.VMEM((2, slots, 1, 128), f32),
            dma((6 + 2 * K,)),
            dma((5 + K,)),
            *(dma((K,)) for _ in range(10)),
            dma((1,)),
            dma((1,)),
            dma((2,)),
            dma((2,)),
            pltpu.SemaphoreType.REGULAR,
        ],
        compiler_params=pltpu.CompilerParams(
            collective_id=0, has_side_effects=True, vmem_limit_bytes=60 << 20
        ),
        name="ssd_backward",
    )(
        inputs[0], grad_out[0], b_proj[0].T, c_proj[0].T, step_sizes[0],
        a_log[None], skip_gain[None], doc_lengths,
    )
    plan = [(0, slice(lo, lo + 512)) for lo in range(0, HD, 512)] + [(i, slice(None)) for i in range(1, len(outs))]
    dx, db, dc, dstep, dalog, dskip = pl.pallas_call(
        functools.partial(write_out, plan),
        out_shape=outs,
        in_specs=[hbm] * 6,
        out_specs=(hbm,) * 6,
        scratch_shapes=[*(pltpu.VMEM(o.shape, o.dtype) for o in outs), dma((len(plan),)), dma((len(plan),))],
        compiler_params=pltpu.CompilerParams(vmem_limit_bytes=60 << 20),
        name="write_out",
    )(*results)
    return dx[None], db.T[None], dc.T[None], dstep[None], dalog[0], dskip[0]


def solution(mesh):
    tokens, heads = P("dp", "ctx", None), P("dp", None, "ctx")
    n_dp, n_ctx = mesh.shape["dp"], mesh.shape["ctx"]
    n_z = min(8, n_ctx // RING)
    return jax.shard_map(
        functools.partial(per_device, n_dp, n_ctx, n_z),
        mesh=mesh,
        in_specs=(tokens, tokens, tokens, heads, P(), P(), P("dp", None), tokens),
        out_specs=(tokens, tokens, tokens, heads, P(), P()),
        check_vma=False,
    )
```

```python
import functools

import jax
import jax.numpy as jnp
from jax import lax
from jax.experimental import pallas as pl
from jax.experimental.pallas import tpu as pltpu
from jax.sharding import PartitionSpec as P

MESH = pl.DeviceIdType.MESH
f32, bf16 = jnp.float32, jnp.bfloat16

MOST_DOC = 2048
RING = 4
CHUNKS = 4
ORDER = (
    ("total", 0), ("total", 1), ("pair", 0), ("total", 2), ("pair", 1), ("total", 3), ("pair", 2), ("give", 0),
    ("pair", 3), ("give", 1), ("give", 2), ("finish", 0), ("give", 3), ("finish", 1), ("finish", 2), ("finish", 3),
)


def nn(a, b):
    return lax.dot_general(a, b, (((1,), (0,)), ((), ())), preferred_element_type=f32)


def nt(a, b):
    return lax.dot_general(a, b, (((1,), (1,)), ((), ())), preferred_element_type=f32)


def split(v, count):
    pieces = []
    for i in range(count):
        piece = v.astype(bf16)
        pieces.append(piece)
        if i + 1 < count:
            v = v - piece.astype(f32)
    return pieces


def kernel(
    dims,
    x_hbm, g_hbm, bt_hbm, ct_hbm, dt_hbm, alog_hbm, skip_hbm, len_hbm,
    dx_ref, db_ref, dc_ref, dstep_ref, dalog_ref, dskip_ref,
    x_ref, g_ref, bt_ref, ct_ref, dt_ref, alog_ref, skip_ref, len_ref,
    xh, gh, bd, z1, z2, rowv, vecs, sa, ra, st, rt, s1, r1, s2, r2, r3, sc, rc, ar,
    load, sa_send, sa_recv, s1_send, r1_recv, s2_send, r2_recv, s3_send, r3_recv, sc_send, sc_recv, st_send, rt_recv, ar_send, ar_recv, known,
):
    n_dp, n_ctx, n_z, T, H, D, N, DOCS = dims
    n_x = n_ctx // (n_z * RING)
    groups = n_ctx // RING
    W = H * D // (RING * CHUNKS)
    C = RING * W
    dp, me = lax.axis_index("dp"), lax.axis_index("ctx")
    y, group = me % RING, me // RING
    z, xhi = group % n_z, group // n_z

    y_peers = [(d, (y + d) % RING) for d in (2, 1, 3)]
    z_near = [(dp, ((group + d) % groups) * RING + y) for d in (1, groups - 1)]
    z_far = [(dp, ((group + d + groups) % groups) * RING + y) for d in (3, -3)]
    n_core = 2 - n_dp % 2
    xlo, core = dp // n_core, dp % n_core
    n_plane, n_line = RING * (n_dp // n_core) * n_x, n_z * n_core
    plane_peers, line_peers = [], []
    n_lane = n_plane // RING
    lane, n_xlo = xhi * (n_dp // n_core) + xlo, n_dp // n_core
    plane, line = lane * RING + y, z * n_core + core

    def far(step, size):
        return min(step, size - step)

    steps = [(a, b) for a in range(n_lane) for b in range(RING) if (a, b) != (0, 0)]
    for a, b in sorted(steps, key=lambda s: -far(s[0], n_lane) - far(s[1], RING)):
        other = (lane + a) % n_lane
        plane_peers.append(((other % n_xlo) * n_core + core, ((other // n_xlo) * n_z + z) * RING + (y + b) % RING))
    steps = [(a, b) for a in range(n_z) for b in range(n_core) if (a, b) != (0, 0)]
    for a, b in sorted(steps, key=lambda s: -far(s[0], n_z) - 0.5 * s[1]):
        line_peers.append((xlo * n_core + (core + b) % n_core, (xhi * n_z + (z + a) % n_z) * RING + y))

    pairs = [(len_hbm, len_ref), (dt_hbm, dt_ref), (alog_hbm, alog_ref), (bt_hbm, bt_ref), (ct_hbm, ct_ref), (skip_hbm, skip_ref)]
    small = len(pairs)
    for k in range(CHUNKS):
        at = slice(k * C, (k + 1) * C)
        pairs += [(g_hbm.at[:, at], g_ref.at[:, at]), (x_hbm.at[:, at], x_ref.at[:, at])]
    loads = [pltpu.make_async_copy(a, b, load.at[i]) for i, (a, b) in enumerate(pairs)]
    for copy in loads[: small + 2]:
        copy.start()

    x_peers, core_peers = [], []
    for a in range(1, n_lane):
        other = (lane + a) % n_lane
        x_peers.append(((other % n_xlo) * n_core + core, ((other // n_xlo) * n_z + z) * RING + y))
    for b in range(1, n_core):
        core_peers.append((xlo * n_core + (core + b) % n_core, me))
    barrier = pltpu.get_barrier_semaphore()
    greeted = [(dp, group * RING + q) for _, q in y_peers]
    greeted += z_near + z_far + x_peers + core_peers
    greeted += [(dp, (xhi * n_z + (z + d) % n_z) * RING + y) for d in range(1, n_z)]
    for target in greeted:
        pl.semaphore_signal(barrier, inc=1, device_id=target, device_id_type=MESH)
    for copy in loads[small + 2 :]:
        copy.start()

    rows = lax.broadcasted_iota(jnp.int32, (T, T), 0)
    cols = lax.broadcasted_iota(jnp.int32, (T, T), 1)
    tril = jnp.where(rows >= cols, 1.0, 0.0).astype(bf16)
    eye = jnp.where(rows == cols, 1.0, 0.0).astype(bf16)
    head_r = lax.broadcasted_iota(jnp.int32, (H, H), 0)
    head_c = lax.broadcasted_iota(jnp.int32, (H, H), 1)

    def one_hot(k, copies):
        heads = lax.broadcasted_iota(jnp.int32, (copies * H, C), 0) % H
        lanes = lax.broadcasted_iota(jnp.int32, (copies * H, C), 1) + k * C
        return jnp.where(lanes // D == heads, 1.0, 0.0).astype(bf16)

    for copy in loads[:small]:
        copy.wait()

    offset = me * T
    lengths = len_ref[...]
    doc_r = lax.broadcasted_iota(jnp.int32, (DOCS, DOCS), 0)
    doc_c = lax.broadcasted_iota(jnp.int32, (DOCS, DOCS), 1)
    length_col = jnp.sum(jnp.where(doc_r == doc_c, lengths, 0), axis=1, keepdims=True)
    start_col = jnp.sum(jnp.where(doc_c < doc_r, lengths, 0), axis=1, keepdims=True)
    start_row = jnp.sum(jnp.where(doc_r < doc_c, length_col, 0), axis=0, keepdims=True)
    place_row = lax.broadcasted_iota(jnp.int32, (DOCS, T), 1) + offset
    place_col = lax.broadcasted_iota(jnp.int32, (T, DOCS), 0) + offset
    seg_row = jnp.sum(jnp.where(start_col <= place_row, 1.0, 0.0), axis=0, keepdims=True)
    seg_col = jnp.sum(jnp.where(start_row <= place_col, 1.0, 0.0), axis=1, keepdims=True)
    before = jnp.sum(jnp.where(start_row <= offset - 1, 1.0, 0.0), axis=1, keepdims=True)
    last = jnp.sum(jnp.where(start_row <= offset + T - 1, 1.0, 0.0), axis=1, keepdims=True)
    same = seg_col == seg_row
    allowed = jnp.logical_and(rows >= cols, same)
    allowed_t = jnp.logical_and(cols >= rows, same)
    living_col = jnp.where(seg_col == before, 1.0, 0.0)
    ending_col = jnp.where(seg_col == last, 1.0, 0.0)
    living_row = jnp.where(seg_row == before, 1.0, 0.0)
    ending_row = jnp.where(seg_row == last, 1.0, 0.0)
    through_flag = jnp.where(last == before, 1.0, 0.0)

    dt = dt_ref[...]
    cum_dt, dt_t = jnp.zeros((T, H), f32), jnp.zeros((T, H), f32)
    for piece in split(dt, 3):
        cum_dt = cum_dt + nt(tril, piece)
        dt_t = dt_t + nt(eye, piece)
    rate = -jnp.exp(alog_ref[...])
    cum = cum_dt * rate
    alpha = jnp.exp(cum)
    beta = jnp.exp(-cum) * dt_t
    spread = jnp.concatenate(
        [
            jnp.concatenate(split(alpha, 3), axis=1),
            jnp.concatenate(split(beta, 3), axis=1),
        ],
        axis=0,
    )
    skip3 = jnp.concatenate(split(jnp.broadcast_to(skip_ref[...], (16, H)), 3), axis=1)

    bt, ct = bt_ref[...], ct_ref[...]
    eb_t = (bt.astype(f32) * ending_row).astype(bf16)
    lc_t = (ct.astype(f32) * living_row).astype(bf16)
    eb_t = jnp.concatenate([eb_t, eb_t], axis=1)
    lc_t = jnp.concatenate([lc_t, lc_t], axis=1)

    sent = []

    def send(src, dst, ssem, rsem, target):
        pltpu.make_async_remote_copy(
            src_ref=src, dst_ref=dst, send_sem=ssem, recv_sem=rsem, device_id=target, device_id_type=MESH
        ).start()

    def waiter(ref, sem):
        return pltpu.make_async_remote_copy(
            src_ref=ref, dst_ref=ref, send_sem=sem, recv_sem=sem, device_id=(dp, me), device_id_type=MESH
        )

    per = C // D
    row_k = lax.broadcasted_iota(jnp.int32, (8, H), 0)
    head_l = lax.broadcasted_iota(jnp.int32, (8, H), 1)
    mine = jnp.where(head_l // per == row_k, alpha[T - 1 : T] * through_flag, 0.0)
    head_s = lax.broadcasted_iota(jnp.int32, (H, C), 0)
    lane_s = lax.broadcasted_iota(jnp.int32, (H, C), 1)
    spots = jnp.where(head_s % per == lane_s // D, 1.0, 0.0).astype(bf16)
    tile = jnp.zeros((8, C), f32)
    for piece in split(mine, 3):
        tile = tile + nn(piece, spots)
    for q in range(RING):
        st[q] = tile[:, q * W : (q + 1) * W]

    def states(k):
        at = slice(k * C, (k + 1) * C)
        hot = one_hot(k, 3)
        wide = nn(spread, hot)
        alpha_w, beta_w = wide[:T], wide[T:]
        for copy in loads[small + 2 * k : small + 2 * k + 2]:
            copy.wait()
        g = g_ref[:, at].astype(f32)
        x = x_ref[:, at].astype(f32)
        g_hi, g_lo = split(g * alpha_w, 2)
        x_hi, x_lo = split(x * beta_w, 2)
        gh[0:T, at], gh[T : 2 * T, at] = g_hi, g_lo
        xh[0:T, at], xh[T : 2 * T, at] = x_hi, x_lo
        last_alpha = alpha_w[T - 1 : T]
        own_states = nn(eb_t, xh[:, at]) * last_alpha
        backs = nn(lc_t, gh[:, at])
        for q in range(RING):
            part = slice(q * W, (q + 1) * W)
            sa[q, k, 0:N, :] = own_states[:, part]
            sa[q, k, N : 2 * N, :] = backs[:, part]
        if k == 0:
            pl.semaphore_wait(barrier, len(greeted))
            for _, q in y_peers:
                send(st.at[q], rt.at[y], st_send.at[0], rt_recv.at[0], (dp, group * RING + q))
            sent.append((st.at[0 : RING - 1], st_send.at[0]))
            rt[y] = st[y]
        for _, q in y_peers:
            send(sa.at[q, k], ra.at[y, k], sa_send.at[k], sa_recv.at[k], (dp, group * RING + q))
        sent.append((sa.at[0 : RING - 1, k], sa_send.at[k]))
        ra[y, k] = sa[y, k]
        rowv[0:8, at] = nn(skip3, hot)[0:8]
        rowv[8:16, at] = jnp.broadcast_to(last_alpha, (8, C))
        vecs[:, at] = jnp.broadcast_to(jnp.sum(g * x, axis=0, keepdims=True), (8, C))
        bd[:, at] = beta_w

    def within(k):
        at = slice(k * C, (k + 1) * C)
        xp, gp = xh[:, at], gh[:, at]
        z2[:, at] = nn(s_hi, xp) + nn(s_lo, xp[:T])
        z1[:, at] = nn(t_hi, gp) + nn(t_lo, gp[:T])
        scores[0] = scores[0] + nt(gp[:T], xp)
        scores[1] = scores[1] + nt(gp[T:], xp[:T])

    for k in range(CHUNKS):
        states(k)
    for target in x_peers + core_peers:
        pl.semaphore_signal(known, inc=1, device_id=target, device_id_type=MESH)
    cum_row = jnp.zeros((H, T), f32)
    for piece in split(dt, 3):
        cum_row = cum_row + nt(piece, tril)
    b32, c32 = nt(eye, bt), nt(eye, ct)
    bb, cc = b32.astype(bf16), c32.astype(bf16)
    eb = (b32 * ending_col).astype(bf16)
    lc = (c32 * living_col).astype(bf16)
    eb = jnp.concatenate([eb, eb], axis=1)
    lc = jnp.concatenate([lc, lc], axis=1)
    s_hi, s_lo = split(jnp.where(allowed, nn(cc, bt), 0.0), 2)
    t_hi, t_lo = split(jnp.where(allowed_t, nn(bb, ct), 0.0), 2)
    s_hi = jnp.concatenate([s_hi, s_hi], axis=1)
    t_hi = jnp.concatenate([t_hi, t_hi], axis=1)
    scores = [jnp.zeros((T, 2 * T), f32), jnp.zeros((T, T), f32)]
    for k in range(CHUNKS):
        within(k)
    ds = jnp.where(allowed, scores[0][:, :T] + scores[0][:, T:] + scores[1], 0.0)
    dc, db = jnp.zeros((N, T), f32), jnp.zeros((N, T), f32)
    for piece in split(ds, 2):
        dc = dc + nt(bt, piece)
        db = db + nn(ct, piece)

    def through_of(r, k):
        return rt[r, k : k + 1, :]

    def own(r, k):
        return ra[r, k, 0:N, :]

    def pulled(r, k):
        return ra[r, k, N : 2 * N, :]

    def total(k):
        if k == 0:
            waiter(rt.at[0 : RING - 1], rt_recv.at[0]).wait_recv()
        waiter(ra.at[0 : RING - 1, k], sa_recv.at[k]).wait_recv()
        up, down = own(0, k), pulled(RING - 1, k)
        across = through_of(0, k)
        for i in range(1, RING):
            j = RING - 1 - i
            up = own(i, k) + through_of(i, k) * up
            down = pulled(j, k) + through_of(j, k) * down
            across = across * through_of(i, k)
        for side, value in ((0, up), (1, down)):
            s1[k, side, 0:N, :] = value
            s1[k, side, N : N + 8, :] = jnp.broadcast_to(across, (8, W))
            send(s1.at[k, side], r1.at[k, side], s1_send.at[k], r1_recv.at[k], z_near[side])
        sent.append((s1.at[k], s1_send.at[k]))

    def pair(k):
        waiter(r1.at[k], r1_recv.at[k]).wait_recv()
        for side in (0, 1):
            across = s1[k, side, N : N + 8, :]
            s2[k, side, 0:N, :] = s1[k, side, 0:N, :] + across[0:1] * r1[k, side, 0:N, :]
            s2[k, side, N : N + 8, :] = across * r1[k, side, N : N + 8, :]
            send(s2.at[k, side, 0:N, :], r3.at[k, side], s3_send.at[k], r3_recv.at[k], z_far[side])
            send(s2.at[k, side], r2.at[k, side], s2_send.at[k], r2_recv.at[k], z_near[side])
        sent.append((r3.at[k], s3_send.at[k]))
        sent.append((s2.at[k], s2_send.at[k]))

    def give(k):
        enters = []
        waiter(r2.at[k], r2_recv.at[k]).wait_recv()
        waiter(r3.at[k], r3_recv.at[k]).wait_recv()
        for side in (0, 1):
            enters.append(r2[k, side, 0:N, :] + r2[k, side, N : N + 1, :] * r3[k, side])
        up, down = enters
        for i in range(RING):
            j = RING - 1 - i
            sc[i, k, 0:N, :] = up
            sc[j, k, N : 2 * N, :] = down
            if i + 1 < RING:
                up = own(i, k) + through_of(i, k) * up
                down = pulled(j, k) + through_of(j, k) * down
        for _, q in y_peers:
            send(sc.at[q, k], rc.at[y, k], sc_send.at[k], sc_recv.at[k], (dp, group * RING + q))
        sent.append((sc.at[0 : RING - 1, k], sc_send.at[k]))
        rc[y, k] = sc[y, k]

    sums = [jnp.zeros((H, 2 * T), f32), jnp.zeros((H, 2 * T), f32), jnp.zeros((2 * N, 2 * T), f32), jnp.zeros((2 * N, 2 * T), f32), jnp.zeros((H, 8), f32)]

    def finish(k):
        at = slice(k * C, (k + 1) * C)
        waiter(rc.at[0 : RING - 1, k], sc_recv.at[k]).wait_recv()
        hot = one_hot(k, 1)
        state = jnp.concatenate([rc[q, k, 0:N, :] for q in range(RING)], axis=1)
        later = jnp.concatenate([rc[q, k, N : 2 * N, :] for q in range(RING)], axis=1)
        mine = jnp.concatenate([sa[q, k, 0:N, :] for q in range(RING)], axis=1)
        last_alpha = rowv[8:9, at]
        leaving = jnp.sum(later * (mine + last_alpha * through_flag * state), axis=0, keepdims=True)
        first_row = lax.broadcasted_iota(jnp.int32, (8, C), 0) == 0
        vec = jnp.where(first_row, leaving, vecs[:, at])
        hh = jnp.concatenate(split(state, 2), axis=0)
        fh = jnp.concatenate(split(later * last_alpha, 2), axis=0)
        z1_w = z1[:, at] + nn(eb, fh)
        z2_w = z2[:, at] + nn(lc, hh)
        gp, xp = gh[:, at], xh[:, at]
        p1 = z1_w * (xp[:T].astype(f32) + xp[T:].astype(f32))
        p2 = z2_w * (gp[:T].astype(f32) + gp[T:].astype(f32))
        sums[0] = sums[0] + nt(hot, jnp.concatenate(split(p1, 2), axis=0))
        sums[1] = sums[1] + nt(hot, jnp.concatenate(split(p2, 2), axis=0))
        for piece in split(vec, 3):
            sums[4] = sums[4] + nt(hot, piece)

        def remainder():
            dx_ref[:, at] = (bd[:, at] * z1_w + rowv[0:1, at] * g_ref[:, at].astype(f32)).astype(bf16)
            sums[2] = sums[2] + nt(hh, gp)
            sums[3] = sums[3] + nt(fh, xp)

        if k + 1 < CHUNKS:
            remainder()
        else:
            put_off.append(remainder)

    put_off = []
    steps = {"total": total, "pair": pair, "give": give, "finish": finish}
    for name, k in ORDER:
        steps[name](k)

    col_q = sums[0][:, :T] + sums[0][:, T:]
    row_q = sums[1][:, :T] + sums[1][:, T:]
    d_cum = row_q - col_q
    d_end, d_skip = sums[4][:, 0:1], sums[4][:, 1:2]
    rate_c = jnp.sum(jnp.where(head_r == head_c, jnp.broadcast_to(rate, (H, H)), 0.0), axis=1, keepdims=True)
    at_end = cols[:H] == T - 1
    d_alog = rate_c * jnp.sum((d_cum + jnp.where(at_end, d_end, 0.0)) * cum_row, axis=1, keepdims=True)
    part = jnp.where(rows[:H] == cols[:H], d_alog, jnp.where(rows[:H] + H == cols[:H], d_skip, 0.0))
    part = jnp.sum(part, axis=0, keepdims=True)

    stages = ((plane, n_plane, plane_peers), (line, n_line, line_peers))
    pl.semaphore_wait(known, len(x_peers) + len(core_peers))
    for s, (mine, count, peers) in enumerate(stages):
        ar[s, mine] = part
        for target in peers:
            send(ar.at[s, mine], ar.at[s, mine], ar_send.at[s], ar_recv.at[s], target)
        if s == 0:
            for work in put_off:
                work()
            acc = sums[2][:N] + sums[2][N:]
            dc_ref[...] = (dc + living_row * (acc[:, :T] + acc[:, T:])).astype(bf16)
            acc = sums[3][:N] + sums[3][N:]
            db_ref[...] = (db + ending_row * (acc[:, :T] + acc[:, T:])).astype(bf16)
            d_log = jnp.zeros((H, T), f32) + d_end
            for piece in split(d_cum, 3):
                d_log = d_log + nn(piece, tril)
            dstep_ref[...] = col_q / dt + d_log * rate_c
            for ref, sem in sent:
                waiter(ref, sem).wait_send()
        if peers:
            waiter(ar.at[s, 0 : count - 1], ar_recv.at[s]).wait_recv()
        part = ar[s, 0]
        for i in range(1, count):
            part = part + ar[s, i]
    dalog_ref[...] = part[:, :H]
    dskip_ref[...] = part[:, H : 2 * H]
    for s, (mine, count, peers) in enumerate(stages):
        if peers:
            waiter(ar.at[s, 0 : count - 1], ar_send.at[s]).wait_send()


def write_out(count, *refs):
    copies = [pltpu.make_async_copy(refs[i], refs[count + i], refs[-1].at[i]) for i in range(count)]
    for copy in copies:
        copy.start()
    for copy in copies:
        copy.wait()


def per_device(n_dp, n_ctx, n_z, inputs, b_proj, c_proj, step_sizes, a_log, skip_gain, doc_lengths, grad_out):
    T, H, N = inputs.shape[1], a_log.shape[0], b_proj.shape[2]
    D, DOCS = inputs.shape[2] // H, doc_lengths.shape[1]
    HD = H * D
    K, W = CHUNKS, HD // (RING * CHUNKS)
    assert 4 * RING * T >= MOST_DOC
    n_x = n_ctx // (n_z * RING)
    slots = max(RING * n_dp * n_x, 2 * n_z)
    dims = (n_dp, n_ctx, n_z, T, H, D, N, DOCS)
    vmem, hbm = pl.BlockSpec(memory_space=pltpu.VMEM), pl.BlockSpec(memory_space=pltpu.HBM)
    dma = pltpu.SemaphoreType.DMA
    outs = (
        jax.ShapeDtypeStruct((T, HD), bf16),
        jax.ShapeDtypeStruct((N, T), bf16),
        jax.ShapeDtypeStruct((N, T), bf16),
        jax.ShapeDtypeStruct((H, T), f32),
        jax.ShapeDtypeStruct((1, H), f32),
        jax.ShapeDtypeStruct((1, H), f32),
    )
    results = pl.pallas_call(
        functools.partial(kernel, dims),
        out_shape=outs,
        in_specs=[hbm] * 8,
        out_specs=(vmem,) * 6,
        scratch_shapes=[
            pltpu.VMEM((T, HD), bf16),
            pltpu.VMEM((T, HD), bf16),
            pltpu.VMEM((N, T), bf16),
            pltpu.VMEM((N, T), bf16),
            pltpu.VMEM((H, T), f32),
            pltpu.VMEM((1, H), f32),
            pltpu.VMEM((1, H), f32),
            pltpu.VMEM((1, DOCS), jnp.int32),
            pltpu.VMEM((2 * T, HD), bf16),
            pltpu.VMEM((2 * T, HD), bf16),
            pltpu.VMEM((T, HD), f32),
            pltpu.VMEM((T, HD), f32),
            pltpu.VMEM((T, HD), f32),
            pltpu.VMEM((16, HD), f32),
            pltpu.VMEM((8, HD), f32),
            pltpu.VMEM((RING, K, 2 * N, W), f32),
            pltpu.VMEM((RING, K, 2 * N, W), f32),
            pltpu.VMEM((RING, 8, W), f32),
            pltpu.VMEM((RING, 8, W), f32),
            pltpu.VMEM((K, 2, N + 8, W), f32),
            pltpu.VMEM((K, 2, N + 8, W), f32),
            pltpu.VMEM((K, 2, N + 8, W), f32),
            pltpu.VMEM((K, 2, N + 8, W), f32),
            pltpu.VMEM((K, 2, N, W), f32),
            pltpu.VMEM((RING, K, 2 * N, W), f32),
            pltpu.VMEM((RING, K, 2 * N, W), f32),
            pltpu.VMEM((2, slots, 1, 128), f32),
            dma((6 + 2 * K,)),
            *(dma((K,)) for _ in range(10)),
            dma((1,)),
            dma((1,)),
            dma((2,)),
            dma((2,)),
            pltpu.SemaphoreType.REGULAR,
        ],
        compiler_params=pltpu.CompilerParams(
            collective_id=0, has_side_effects=True, vmem_limit_bytes=40960 << 10
        ),
        name="ssd_backward",
    )(
        *(
            pltpu.with_memory_space_constraint(a, pltpu.HBM)
            for a in (
                inputs[0], grad_out[0], b_proj[0].T, c_proj[0].T, step_sizes[0],
                a_log[None], skip_gain[None], doc_lengths,
            )
        )
    )
    dx, db, dc, dstep, dalog, dskip = pl.pallas_call(
        functools.partial(write_out, len(outs)),
        out_shape=outs,
        in_specs=[vmem] * 6,
        out_specs=(hbm,) * 6,
        scratch_shapes=[dma((len(outs),))],
        compiler_params=pltpu.CompilerParams(vmem_limit_bytes=1 << 20),
        name="write_out",
    )(*results)
    return dx[None], db.T[None], dc.T[None], dstep[None], dalog[0], dskip[0]


def solution(mesh):
    tokens, heads = P("dp", "ctx", None), P("dp", None, "ctx")
    n_dp, n_ctx = mesh.shape["dp"], mesh.shape["ctx"]
    n_z = min(8, n_ctx // RING)
    return jax.shard_map(
        functools.partial(per_device, n_dp, n_ctx, n_z),
        mesh=mesh,
        in_specs=(tokens, tokens, tokens, heads, P(), P(), P("dp", None), tokens),
        out_specs=(tokens, tokens, tokens, heads, P(), P()),
        check_vma=False,
    )
```

```python
import functools

import jax
import jax.numpy as jnp
from jax import lax
from jax.experimental import pallas as pl
from jax.experimental.pallas import tpu as pltpu
from jax.sharding import PartitionSpec as P

MESH = pl.DeviceIdType.MESH
f32, bf16 = jnp.float32, jnp.bfloat16

MOST_DOC = 2048
RING = 4
CHUNKS = 4
ORDER = (
    ("total", 0), ("total", 1, 0), ("pair", 0, 0), ("total", 1, 1), ("pair", 0, 1), ("total", 2, 0),
    ("pair", 1, 0), ("total", 2, 1), ("pair", 1, 1), ("total", 3, 0), ("pair", 2, 0), ("total", 3, 1),
    ("pair", 2, 1), ("give", 0, 0), ("give", 0, 1), ("pair", 3, 0), ("pair", 3, 1), ("give", 1),
    ("give", 2), ("give", 3), ("finish", 0), ("finish", 1), ("finish", 2), ("finish", 3),
)


def nn(a, b):
    return lax.dot_general(a, b, (((1,), (0,)), ((), ())), preferred_element_type=f32)


def nt(a, b):
    return lax.dot_general(a, b, (((1,), (1,)), ((), ())), preferred_element_type=f32)


def split(v, count):
    pieces = []
    for i in range(count):
        piece = v.astype(bf16)
        pieces.append(piece)
        if i + 1 < count:
            v = v - piece.astype(f32)
    return pieces


def kernel(
    dims,
    x_hbm, g_hbm, bt_hbm, ct_hbm, dt_hbm, alog_hbm, skip_hbm, len_hbm,
    dx_ref, db_ref, dc_ref, dstep_ref, dalog_ref, dskip_ref,
    x_ref, g_ref, bt_ref, ct_ref, dt_ref, alog_ref, skip_ref, len_ref,
    xh, gh, bd, z1, z2, rowv, vecs, sa, ra, st, rt, s1, r1, s2, r2, r3, sc, rc, ar,
    load, sa_send, sa_recv, s1_send, r1_recv, s2_send, r2_recv, s3_send, r3_recv, sc_send, sc_recv, st_send, rt_recv, ar_send, ar_recv, known,
):
    n_dp, n_ctx, n_z, T, H, D, N, DOCS = dims
    n_x = n_ctx // (n_z * RING)
    groups = n_ctx // RING
    W = H * D // (RING * CHUNKS)
    C = RING * W
    dp, me = lax.axis_index("dp"), lax.axis_index("ctx")
    y, group = me % RING, me // RING
    z, xhi = group % n_z, group // n_z

    y_peers = [(d, (y + d) % RING) for d in (2, 1, 3)]
    z_near = [(dp, ((group + d) % groups) * RING + y) for d in (1, groups - 1)]
    z_far = [(dp, ((group + d + groups) % groups) * RING + y) for d in (3, -3)]
    n_core = 2 - n_dp % 2
    xlo, core = dp // n_core, dp % n_core
    n_plane, n_line = RING * (n_dp // n_core) * n_x, n_z * n_core
    plane_peers, line_peers = [], []
    n_lane = n_plane // RING
    lane, n_xlo = xhi * (n_dp // n_core) + xlo, n_dp // n_core
    plane, line = lane * RING + y, z * n_core + core

    def far(step, size):
        return min(step, size - step)

    steps = [(a, b) for a in range(n_lane) for b in range(RING) if (a, b) != (0, 0)]
    for a, b in sorted(steps, key=lambda s: -far(s[0], n_lane) - far(s[1], RING)):
        other = (lane + a) % n_lane
        plane_peers.append(((other % n_xlo) * n_core + core, ((other // n_xlo) * n_z + z) * RING + (y + b) % RING))
    steps = [(a, b) for a in range(n_z) for b in range(n_core) if (a, b) != (0, 0)]
    for a, b in sorted(steps, key=lambda s: -far(s[0], n_z) - 0.5 * s[1]):
        line_peers.append((xlo * n_core + (core + b) % n_core, (xhi * n_z + (z + a) % n_z) * RING + y))

    pairs = [(len_hbm, len_ref), (dt_hbm, dt_ref), (alog_hbm, alog_ref), (bt_hbm, bt_ref), (ct_hbm, ct_ref), (skip_hbm, skip_ref)]
    small = len(pairs)
    for k in range(CHUNKS):
        at = slice(k * C, (k + 1) * C)
        pairs += [(g_hbm.at[:, at], g_ref.at[:, at]), (x_hbm.at[:, at], x_ref.at[:, at])]
    loads = [pltpu.make_async_copy(a, b, load.at[i]) for i, (a, b) in enumerate(pairs)]
    for copy in loads[: small + 2]:
        copy.start()

    x_peers, core_peers = [], []
    for a in range(1, n_lane):
        other = (lane + a) % n_lane
        x_peers.append(((other % n_xlo) * n_core + core, ((other // n_xlo) * n_z + z) * RING + y))
    for b in range(1, n_core):
        core_peers.append((xlo * n_core + (core + b) % n_core, me))
    barrier = pltpu.get_barrier_semaphore()
    greeted = [(dp, group * RING + q) for _, q in y_peers]
    greeted += z_near + z_far + x_peers + core_peers
    greeted += [(dp, (xhi * n_z + (z + d) % n_z) * RING + y) for d in range(1, n_z)]
    for target in greeted:
        pl.semaphore_signal(barrier, inc=1, device_id=target, device_id_type=MESH)
    for copy in loads[small + 2 :]:
        copy.start()

    rows = lax.broadcasted_iota(jnp.int32, (T, T), 0)
    cols = lax.broadcasted_iota(jnp.int32, (T, T), 1)
    tril = jnp.where(rows >= cols, 1.0, 0.0).astype(bf16)
    eye = jnp.where(rows == cols, 1.0, 0.0).astype(bf16)
    head_r = lax.broadcasted_iota(jnp.int32, (H, H), 0)
    head_c = lax.broadcasted_iota(jnp.int32, (H, H), 1)

    def one_hot(k, copies):
        heads = lax.broadcasted_iota(jnp.int32, (copies * H, C), 0) % H
        lanes = lax.broadcasted_iota(jnp.int32, (copies * H, C), 1) + k * C
        return jnp.where(lanes // D == heads, 1.0, 0.0).astype(bf16)

    for copy in loads[:small]:
        copy.wait()

    offset = me * T
    lengths = len_ref[...]
    doc_r = lax.broadcasted_iota(jnp.int32, (DOCS, DOCS), 0)
    doc_c = lax.broadcasted_iota(jnp.int32, (DOCS, DOCS), 1)
    length_col = jnp.sum(jnp.where(doc_r == doc_c, lengths, 0), axis=1, keepdims=True)
    start_col = jnp.sum(jnp.where(doc_c < doc_r, lengths, 0), axis=1, keepdims=True)
    start_row = jnp.sum(jnp.where(doc_r < doc_c, length_col, 0), axis=0, keepdims=True)
    place_row = lax.broadcasted_iota(jnp.int32, (DOCS, T), 1) + offset
    place_col = lax.broadcasted_iota(jnp.int32, (T, DOCS), 0) + offset
    seg_row = jnp.sum(jnp.where(start_col <= place_row, 1.0, 0.0), axis=0, keepdims=True)
    seg_col = jnp.sum(jnp.where(start_row <= place_col, 1.0, 0.0), axis=1, keepdims=True)
    before = jnp.sum(jnp.where(start_row <= offset - 1, 1.0, 0.0), axis=1, keepdims=True)
    last = jnp.sum(jnp.where(start_row <= offset + T - 1, 1.0, 0.0), axis=1, keepdims=True)
    same = seg_col == seg_row
    allowed = jnp.logical_and(rows >= cols, same)
    allowed_t = jnp.logical_and(cols >= rows, same)
    living_col = jnp.where(seg_col == before, 1.0, 0.0)
    ending_col = jnp.where(seg_col == last, 1.0, 0.0)
    living_row = jnp.where(seg_row == before, 1.0, 0.0)
    ending_row = jnp.where(seg_row == last, 1.0, 0.0)
    through_flag = jnp.where(last == before, 1.0, 0.0)

    dt = dt_ref[...]
    cum_dt, dt_t = jnp.zeros((T, H), f32), jnp.zeros((T, H), f32)
    for piece in split(dt, 3):
        cum_dt = cum_dt + nt(tril, piece)
        dt_t = dt_t + nt(eye, piece)
    rate = -jnp.exp(alog_ref[...])
    cum = cum_dt * rate
    alpha = jnp.exp(cum)
    beta = jnp.exp(-cum) * dt_t
    spread = jnp.concatenate(
        [
            jnp.concatenate(split(alpha, 3), axis=1),
            jnp.concatenate(split(beta, 3), axis=1),
        ],
        axis=0,
    )
    skip3 = jnp.concatenate(split(jnp.broadcast_to(skip_ref[...], (16, H)), 3), axis=1)

    bt, ct = bt_ref[...], ct_ref[...]
    eb_t = (bt.astype(f32) * ending_row).astype(bf16)
    lc_t = (ct.astype(f32) * living_row).astype(bf16)
    eb_t = jnp.concatenate([eb_t, eb_t], axis=1)
    lc_t = jnp.concatenate([lc_t, lc_t], axis=1)

    sent = []

    def send(src, dst, ssem, rsem, target):
        pltpu.make_async_remote_copy(
            src_ref=src, dst_ref=dst, send_sem=ssem, recv_sem=rsem, device_id=target, device_id_type=MESH
        ).start()

    def waiter(ref, sem):
        return pltpu.make_async_remote_copy(
            src_ref=ref, dst_ref=ref, send_sem=sem, recv_sem=sem, device_id=(dp, me), device_id_type=MESH
        )

    per = C // D
    row_k = lax.broadcasted_iota(jnp.int32, (8, H), 0)
    head_l = lax.broadcasted_iota(jnp.int32, (8, H), 1)
    mine = jnp.where(head_l // per == row_k, alpha[T - 1 : T] * through_flag, 0.0)
    head_s = lax.broadcasted_iota(jnp.int32, (H, C), 0)
    lane_s = lax.broadcasted_iota(jnp.int32, (H, C), 1)
    spots = jnp.where(head_s % per == lane_s // D, 1.0, 0.0).astype(bf16)
    tile = jnp.zeros((8, C), f32)
    for piece in split(mine, 3):
        tile = tile + nn(piece, spots)
    for q in range(RING):
        st[q] = tile[:, q * W : (q + 1) * W]

    def states(k):
        at = slice(k * C, (k + 1) * C)
        hot = one_hot(k, 3)
        wide = nn(spread, hot)
        alpha_w, beta_w = wide[:T], wide[T:]
        for copy in loads[small + 2 * k : small + 2 * k + 2]:
            copy.wait()
        g = g_ref[:, at].astype(f32)
        x = x_ref[:, at].astype(f32)
        g_hi, g_lo = split(g * alpha_w, 2)
        x_hi, x_lo = split(x * beta_w, 2)
        gh[0:T, at], gh[T : 2 * T, at] = g_hi, g_lo
        xh[0:T, at], xh[T : 2 * T, at] = x_hi, x_lo
        last_alpha = alpha_w[T - 1 : T]
        own_states = nn(eb_t, xh[:, at]) * last_alpha
        backs = nn(lc_t, gh[:, at])
        for q in range(RING):
            part = slice(q * W, (q + 1) * W)
            sa[q, k, 0:N, :] = own_states[:, part]
            sa[q, k, N : 2 * N, :] = backs[:, part]
        if k == 0:
            pl.semaphore_wait(barrier, len(greeted))
            for _, q in y_peers:
                send(st.at[q], rt.at[y], st_send.at[0], rt_recv.at[0], (dp, group * RING + q))
            sent.append((st.at[0 : RING - 1], st_send.at[0]))
            rt[y] = st[y]
        for side in (0, 1):
            half, i = slice(side * N, side * N + N), 2 * k + side
            for _, q in y_peers:
                send(sa.at[q, k, half, :], ra.at[y, k, half, :], sa_send.at[i], sa_recv.at[i], (dp, group * RING + q))
            sent.append((sa.at[0 : RING - 1, k, half, :], sa_send.at[i]))
        ra[y, k] = sa[y, k]
        rowv[0:8, at] = nn(skip3, hot)[0:8]
        rowv[8:16, at] = jnp.broadcast_to(last_alpha, (8, C))
        vecs[:, at] = jnp.broadcast_to(jnp.sum(g * x, axis=0, keepdims=True), (8, C))
        bd[:, at] = beta_w

    def within(k):
        at = slice(k * C, (k + 1) * C)
        xp, gp = xh[:, at], gh[:, at]
        z2[:, at] = nn(s_hi, xp) + nn(s_lo, xp[:T])
        z1[:, at] = nn(t_hi, gp) + nn(t_lo, gp[:T])
        scores[0] = scores[0] + nt(gp[:T], xp)
        scores[1] = scores[1] + nt(gp[T:], xp[:T])

    for k in range(CHUNKS):
        states(k)
    for target in x_peers + core_peers:
        pl.semaphore_signal(known, inc=1, device_id=target, device_id_type=MESH)
    cum_row = jnp.zeros((H, T), f32)
    for piece in split(dt, 3):
        cum_row = cum_row + nt(piece, tril)
    b32, c32 = nt(eye, bt), nt(eye, ct)
    bb, cc = b32.astype(bf16), c32.astype(bf16)
    eb = (b32 * ending_col).astype(bf16)
    lc = (c32 * living_col).astype(bf16)
    eb = jnp.concatenate([eb, eb], axis=1)
    lc = jnp.concatenate([lc, lc], axis=1)
    s_hi, s_lo = split(jnp.where(allowed, nn(cc, bt), 0.0), 2)
    t_hi, t_lo = split(jnp.where(allowed_t, nn(bb, ct), 0.0), 2)
    s_hi = jnp.concatenate([s_hi, s_hi], axis=1)
    t_hi = jnp.concatenate([t_hi, t_hi], axis=1)
    scores = [jnp.zeros((T, 2 * T), f32), jnp.zeros((T, T), f32)]
    for k in range(CHUNKS):
        within(k)
    ds = jnp.where(allowed, scores[0][:, :T] + scores[0][:, T:] + scores[1], 0.0)
    dc, db = jnp.zeros((N, T), f32), jnp.zeros((N, T), f32)
    for piece in split(ds, 2):
        dc = dc + nt(bt, piece)
        db = db + nn(ct, piece)

    def through_of(r, k):
        return rt[r, k : k + 1, :]

    def own(r, k):
        return ra[r, k, 0:N, :]

    def pulled(r, k):
        return ra[r, k, N : 2 * N, :]

    def total(k, sides=(0, 1)):
        if k == 0 and 0 in sides:
            waiter(rt.at[0 : RING - 1], rt_recv.at[0]).wait_recv()
        across = through_of(0, k)
        for i in range(1, RING):
            across = across * through_of(i, k)
        for side in sides:
            waiter(ra.at[0 : RING - 1, k, side * N : side * N + N, :], sa_recv.at[2 * k + side]).wait_recv()
            if side == 0:
                value = own(0, k)
                for i in range(1, RING):
                    value = own(i, k) + through_of(i, k) * value
            else:
                value = pulled(RING - 1, k)
                for i in range(RING - 2, -1, -1):
                    value = pulled(i, k) + through_of(i, k) * value
            s1[k, side, 0:N, :] = value
            s1[k, side, N : N + 8, :] = jnp.broadcast_to(across, (8, W))
            i = 2 * k + side
            send(s1.at[k, side], r1.at[k, side], s1_send.at[i], r1_recv.at[i], z_near[side])
            sent.append((s1.at[k, side], s1_send.at[i]))

    def pair(k, sides=(0, 1)):
        for side in sides:
            i = 2 * k + side
            waiter(r1.at[k, side], r1_recv.at[i]).wait_recv()
            across = s1[k, side, N : N + 8, :]
            s2[k, side, 0:N, :] = s1[k, side, 0:N, :] + across[0:1] * r1[k, side, 0:N, :]
            s2[k, side, N : N + 8, :] = across * r1[k, side, N : N + 8, :]
            send(s2.at[k, side, 0:N, :], r3.at[k, side], s3_send.at[i], r3_recv.at[i], z_far[side])
            send(s2.at[k, side], r2.at[k, side], s2_send.at[i], r2_recv.at[i], z_near[side])
            sent.append((r3.at[k, side], s3_send.at[i]))
            sent.append((s2.at[k, side], s2_send.at[i]))

    def give(k, sides=(0, 1)):
        for side in sides:
            half, n = slice(side * N, side * N + N), 2 * k + side
            waiter(r2.at[k, side], r2_recv.at[n]).wait_recv()
            waiter(r3.at[k, side], r3_recv.at[n]).wait_recv()
            value = r2[k, side, 0:N, :] + r2[k, side, N : N + 1, :] * r3[k, side]
            for i in range(RING) if side == 0 else range(RING - 1, -1, -1):
                sc[i, k, half, :] = value
                value = (own(i, k) if side == 0 else pulled(i, k)) + through_of(i, k) * value
            for _, q in y_peers:
                send(sc.at[q, k, half, :], rc.at[y, k, half, :], sc_send.at[n], sc_recv.at[n], (dp, group * RING + q))
            sent.append((sc.at[0 : RING - 1, k, half, :], sc_send.at[n]))
            rc[y, k, half, :] = sc[y, k, half, :]

    sums = [jnp.zeros((H, 2 * T), f32), jnp.zeros((H, 2 * T), f32), jnp.zeros((2 * N, 2 * T), f32), jnp.zeros((2 * N, 2 * T), f32), jnp.zeros((H, 8), f32)]

    def finish(k):
        at = slice(k * C, (k + 1) * C)
        for side in (0, 1):
            waiter(rc.at[0 : RING - 1, k, side * N : side * N + N, :], sc_recv.at[2 * k + side]).wait_recv()
        hot = one_hot(k, 1)
        state = jnp.concatenate([rc[q, k, 0:N, :] for q in range(RING)], axis=1)
        later = jnp.concatenate([rc[q, k, N : 2 * N, :] for q in range(RING)], axis=1)
        mine = jnp.concatenate([sa[q, k, 0:N, :] for q in range(RING)], axis=1)
        last_alpha = rowv[8:9, at]
        leaving = jnp.sum(later * (mine + last_alpha * through_flag * state), axis=0, keepdims=True)
        first_row = lax.broadcasted_iota(jnp.int32, (8, C), 0) == 0
        vec = jnp.where(first_row, leaving, vecs[:, at])
        hh = jnp.concatenate(split(state, 2), axis=0)
        fh = jnp.concatenate(split(later * last_alpha, 2), axis=0)
        z1_w = z1[:, at] + nn(eb, fh)
        z2_w = z2[:, at] + nn(lc, hh)
        gp, xp = gh[:, at], xh[:, at]
        p1 = z1_w * (xp[:T].astype(f32) + xp[T:].astype(f32))
        p2 = z2_w * (gp[:T].astype(f32) + gp[T:].astype(f32))
        sums[0] = sums[0] + nt(hot, jnp.concatenate(split(p1, 2), axis=0))
        sums[1] = sums[1] + nt(hot, jnp.concatenate(split(p2, 2), axis=0))
        for piece in split(vec, 3):
            sums[4] = sums[4] + nt(hot, piece)

        def remainder():
            dx_ref[:, at] = (bd[:, at] * z1_w + rowv[0:1, at] * g_ref[:, at].astype(f32)).astype(bf16)
            sums[2] = sums[2] + nt(hh, gp)
            sums[3] = sums[3] + nt(fh, xp)

        if k + 1 < CHUNKS:
            remainder()
        else:
            put_off.append(remainder)

    put_off = []
    steps = {"total": total, "pair": pair, "give": give, "finish": finish}
    for name, k, *sides in ORDER:
        steps[name](k, *([sides] if sides else []))

    col_q = sums[0][:, :T] + sums[0][:, T:]
    row_q = sums[1][:, :T] + sums[1][:, T:]
    d_cum = row_q - col_q
    d_end, d_skip = sums[4][:, 0:1], sums[4][:, 1:2]
    rate_c = jnp.sum(jnp.where(head_r == head_c, jnp.broadcast_to(rate, (H, H)), 0.0), axis=1, keepdims=True)
    at_end = cols[:H] == T - 1
    d_alog = rate_c * jnp.sum((d_cum + jnp.where(at_end, d_end, 0.0)) * cum_row, axis=1, keepdims=True)
    part = jnp.where(rows[:H] == cols[:H], d_alog, jnp.where(rows[:H] + H == cols[:H], d_skip, 0.0))
    part = jnp.sum(part, axis=0, keepdims=True)

    stages = ((line, n_line, line_peers), (plane, n_plane, plane_peers))
    pl.semaphore_wait(known, len(x_peers) + len(core_peers))
    for s, (mine, count, peers) in enumerate(stages):
        ar[s, mine] = part
        for target in peers:
            send(ar.at[s, mine], ar.at[s, mine], ar_send.at[s], ar_recv.at[s], target)
        if s == 0:
            for work in put_off:
                work()
            acc = sums[2][:N] + sums[2][N:]
            dc_ref[...] = (dc + living_row * (acc[:, :T] + acc[:, T:])).astype(bf16)
            acc = sums[3][:N] + sums[3][N:]
            db_ref[...] = (db + ending_row * (acc[:, :T] + acc[:, T:])).astype(bf16)
            d_log = jnp.zeros((H, T), f32) + d_end
            for piece in split(d_cum, 3):
                d_log = d_log + nn(piece, tril)
            dstep_ref[...] = col_q / dt + d_log * rate_c
            for ref, sem in sent:
                waiter(ref, sem).wait_send()
        if peers:
            waiter(ar.at[s, 0 : count - 1], ar_recv.at[s]).wait_recv()
        part = ar[s, 0]
        for i in range(1, count):
            part = part + ar[s, i]
    dalog_ref[...] = part[:, :H]
    dskip_ref[...] = part[:, H : 2 * H]
    for s, (mine, count, peers) in enumerate(stages):
        if peers:
            waiter(ar.at[s, 0 : count - 1], ar_send.at[s]).wait_send()


def write_out(count, *refs):
    copies = [pltpu.make_async_copy(refs[i], refs[count + i], refs[-1].at[i]) for i in range(count)]
    for copy in copies:
        copy.start()
    for copy in copies:
        copy.wait()


def per_device(n_dp, n_ctx, n_z, inputs, b_proj, c_proj, step_sizes, a_log, skip_gain, doc_lengths, grad_out):
    T, H, N = inputs.shape[1], a_log.shape[0], b_proj.shape[2]
    D, DOCS = inputs.shape[2] // H, doc_lengths.shape[1]
    HD = H * D
    K, W = CHUNKS, HD // (RING * CHUNKS)
    assert 4 * RING * T >= MOST_DOC
    n_x = n_ctx // (n_z * RING)
    slots = max(RING * n_dp * n_x, 2 * n_z)
    dims = (n_dp, n_ctx, n_z, T, H, D, N, DOCS)
    vmem, hbm = pl.BlockSpec(memory_space=pltpu.VMEM), pl.BlockSpec(memory_space=pltpu.HBM)
    dma = pltpu.SemaphoreType.DMA
    outs = (
        jax.ShapeDtypeStruct((T, HD), bf16),
        jax.ShapeDtypeStruct((N, T), bf16),
        jax.ShapeDtypeStruct((N, T), bf16),
        jax.ShapeDtypeStruct((H, T), f32),
        jax.ShapeDtypeStruct((1, H), f32),
        jax.ShapeDtypeStruct((1, H), f32),
    )
    results = pl.pallas_call(
        functools.partial(kernel, dims),
        out_shape=outs,
        in_specs=[hbm] * 8,
        out_specs=(vmem,) * 6,
        scratch_shapes=[
            pltpu.VMEM((T, HD), bf16),
            pltpu.VMEM((T, HD), bf16),
            pltpu.VMEM((N, T), bf16),
            pltpu.VMEM((N, T), bf16),
            pltpu.VMEM((H, T), f32),
            pltpu.VMEM((1, H), f32),
            pltpu.VMEM((1, H), f32),
            pltpu.VMEM((1, DOCS), jnp.int32),
            pltpu.VMEM((2 * T, HD), bf16),
            pltpu.VMEM((2 * T, HD), bf16),
            pltpu.VMEM((T, HD), f32),
            pltpu.VMEM((T, HD), f32),
            pltpu.VMEM((T, HD), f32),
            pltpu.VMEM((16, HD), f32),
            pltpu.VMEM((8, HD), f32),
            pltpu.VMEM((RING, K, 2 * N, W), f32),
            pltpu.VMEM((RING, K, 2 * N, W), f32),
            pltpu.VMEM((RING, 8, W), f32),
            pltpu.VMEM((RING, 8, W), f32),
            pltpu.VMEM((K, 2, N + 8, W), f32),
            pltpu.VMEM((K, 2, N + 8, W), f32),
            pltpu.VMEM((K, 2, N + 8, W), f32),
            pltpu.VMEM((K, 2, N + 8, W), f32),
            pltpu.VMEM((K, 2, N, W), f32),
            pltpu.VMEM((RING, K, 2 * N, W), f32),
            pltpu.VMEM((RING, K, 2 * N, W), f32),
            pltpu.VMEM((2, slots, 1, 128), f32),
            dma((6 + 2 * K,)),
            *(dma((2 * K,)) for _ in range(10)),
            dma((1,)),
            dma((1,)),
            dma((2,)),
            dma((2,)),
            pltpu.SemaphoreType.REGULAR,
        ],
        compiler_params=pltpu.CompilerParams(
            collective_id=0, has_side_effects=True, vmem_limit_bytes=40960 << 10
        ),
        name="ssd_backward",
    )(
        *(
            pltpu.with_memory_space_constraint(a, pltpu.HBM)
            for a in (
                inputs[0], grad_out[0], b_proj[0].T, c_proj[0].T, step_sizes[0],
                a_log[None], skip_gain[None], doc_lengths,
            )
        )
    )
    dx, db, dc, dstep, dalog, dskip = pl.pallas_call(
        functools.partial(write_out, len(outs)),
        out_shape=outs,
        in_specs=[vmem] * 6,
        out_specs=(hbm,) * 6,
        scratch_shapes=[dma((len(outs),))],
        compiler_params=pltpu.CompilerParams(vmem_limit_bytes=1 << 20),
        name="write_out",
    )(*results)
    return dx[None], db.T[None], dc.T[None], dstep[None], dalog[0], dskip[0]


def solution(mesh):
    tokens, heads = P("dp", "ctx", None), P("dp", None, "ctx")
    n_dp, n_ctx = mesh.shape["dp"], mesh.shape["ctx"]
    n_z = min(8, n_ctx // RING)
    return jax.shard_map(
        functools.partial(per_device, n_dp, n_ctx, n_z),
        mesh=mesh,
        in_specs=(tokens, tokens, tokens, heads, P(), P(), P("dp", None), tokens),
        out_specs=(tokens, tokens, tokens, heads, P(), P()),
        check_vma=False,
    )
```

```python
import functools

import jax
import jax.numpy as jnp
from jax import lax
from jax.experimental import pallas as pl
from jax.experimental.pallas import tpu as pltpu
from jax.sharding import PartitionSpec as P

MESH = pl.DeviceIdType.MESH
f32, bf16 = jnp.float32, jnp.bfloat16

MOST_DOC = 2048
RING = 4
CHUNKS = 4
ORDER = (
    ("total", 0), ("total", 1, 0), ("pair", 0, 0), ("total", 1, 1), ("pair", 0, 1), ("total", 2, 0),
    ("pair", 1, 0), ("total", 2, 1), ("pair", 1, 1), ("total", 3, 0), ("pair", 2, 0), ("total", 3, 1),
    ("pair", 2, 1), ("give", 0, 0), ("give", 0, 1), ("pair", 3, 0), ("pair", 3, 1), ("give", 1),
    ("give", 2), ("give", 3), ("finish", 0), ("finish", 1), ("finish", 2), ("finish", 3),
)


def nn(a, b):
    return lax.dot_general(a, b, (((1,), (0,)), ((), ())), preferred_element_type=f32)


def nt(a, b):
    return lax.dot_general(a, b, (((1,), (1,)), ((), ())), preferred_element_type=f32)


def split(v, count):
    pieces = []
    for i in range(count):
        piece = v.astype(bf16)
        pieces.append(piece)
        if i + 1 < count:
            v = v - piece.astype(f32)
    return pieces


def kernel(
    dims,
    x_hbm, g_hbm, bt_hbm, ct_hbm, dt_hbm, alog_hbm, skip_hbm, len_hbm,
    dx_ref, db_ref, dc_ref, dstep_ref, dalog_ref, dskip_ref,
    x_ref, g_ref, bt_ref, ct_ref, dt_ref, alog_ref, skip_ref, len_ref,
    xh, gh, bd, z1, z2, rowv, vecs, sa, ra, st, rt, s1, r1, s2, r2, r3, sc, rc, ar,
    load, sa_send, sa_recv, s1_send, r1_recv, s2_send, r2_recv, s3_send, r3_recv, sc_send, sc_recv, st_send, rt_recv, ar_send, ar_recv, known,
):
    n_dp, n_ctx, n_z, T, H, D, N, DOCS = dims
    n_x = n_ctx // (n_z * RING)
    groups = n_ctx // RING
    W = H * D // (RING * CHUNKS)
    C = RING * W
    dp, me = lax.axis_index("dp"), lax.axis_index("ctx")
    y, group = me % RING, me // RING
    z, xhi = group % n_z, group // n_z

    y_peers = [(d, (y + d) % RING) for d in (2, 1, 3)]
    z_near = [(dp, ((group + d) % groups) * RING + y) for d in (1, groups - 1)]
    z_far = [(dp, ((group + d + groups) % groups) * RING + y) for d in (3, -3)]
    n_core = 2 - n_dp % 2
    xlo, core = dp // n_core, dp % n_core
    n_plane, n_line = RING * (n_dp // n_core) * n_x, n_z * n_core
    plane_peers, line_peers = [], []
    n_lane = n_plane // RING
    lane, n_xlo = xhi * (n_dp // n_core) + xlo, n_dp // n_core
    plane, line = lane * RING + y, z * n_core + core

    def far(step, size):
        return min(step, size - step)

    steps = [(a, b) for a in range(n_lane) for b in range(RING) if (a, b) != (0, 0)]
    for a, b in sorted(steps, key=lambda s: -far(s[0], n_lane) - far(s[1], RING)):
        other = (lane + a) % n_lane
        plane_peers.append(((other % n_xlo) * n_core + core, ((other // n_xlo) * n_z + z) * RING + (y + b) % RING))
    steps = [(a, b) for a in range(n_z) for b in range(n_core) if (a, b) != (0, 0)]
    for a, b in sorted(steps, key=lambda s: -far(s[0], n_z) - 0.5 * s[1]):
        line_peers.append((xlo * n_core + (core + b) % n_core, (xhi * n_z + (z + a) % n_z) * RING + y))

    pairs = [(len_hbm, len_ref), (dt_hbm, dt_ref), (alog_hbm, alog_ref), (bt_hbm, bt_ref), (ct_hbm, ct_ref), (skip_hbm, skip_ref)]
    small = len(pairs)
    for k in range(CHUNKS):
        at = slice(k * C, (k + 1) * C)
        pairs += [(g_hbm.at[:, at], g_ref.at[:, at]), (x_hbm.at[:, at], x_ref.at[:, at])]
    loads = [pltpu.make_async_copy(a, b, load.at[i]) for i, (a, b) in enumerate(pairs)]
    for copy in loads[: small + 2]:
        copy.start()

    x_peers, core_peers = [], []
    for a in range(1, n_lane):
        other = (lane + a) % n_lane
        x_peers.append(((other % n_xlo) * n_core + core, ((other // n_xlo) * n_z + z) * RING + y))
    for b in range(1, n_core):
        core_peers.append((xlo * n_core + (core + b) % n_core, me))
    barrier = pltpu.get_barrier_semaphore()
    greeted = [(dp, (xhi * n_z + (z + d) % n_z) * RING + y) for d in sorted(range(1, n_z), key=lambda d: -far(d, n_z))]
    greeted += z_far + z_near + [(dp, group * RING + q) for _, q in y_peers] + x_peers + core_peers
    for target in greeted:
        pl.semaphore_signal(barrier, inc=1, device_id=target, device_id_type=MESH)
    for copy in loads[small + 2 :]:
        copy.start()

    rows = lax.broadcasted_iota(jnp.int32, (T, T), 0)
    cols = lax.broadcasted_iota(jnp.int32, (T, T), 1)
    tril = jnp.where(rows >= cols, 1.0, 0.0).astype(bf16)
    eye = jnp.where(rows == cols, 1.0, 0.0).astype(bf16)
    head_r = lax.broadcasted_iota(jnp.int32, (H, H), 0)
    head_c = lax.broadcasted_iota(jnp.int32, (H, H), 1)

    def one_hot(k, copies):
        heads = lax.broadcasted_iota(jnp.int32, (copies * H, C), 0) % H
        lanes = lax.broadcasted_iota(jnp.int32, (copies * H, C), 1) + k * C
        return jnp.where(lanes // D == heads, 1.0, 0.0).astype(bf16)

    for copy in loads[:small]:
        copy.wait()

    offset = me * T
    lengths = len_ref[...]
    doc_r = lax.broadcasted_iota(jnp.int32, (DOCS, DOCS), 0)
    doc_c = lax.broadcasted_iota(jnp.int32, (DOCS, DOCS), 1)
    length_col = jnp.sum(jnp.where(doc_r == doc_c, lengths, 0), axis=1, keepdims=True)
    start_col = jnp.sum(jnp.where(doc_c < doc_r, lengths, 0), axis=1, keepdims=True)
    start_row = jnp.sum(jnp.where(doc_r < doc_c, length_col, 0), axis=0, keepdims=True)
    place_row = lax.broadcasted_iota(jnp.int32, (DOCS, T), 1) + offset
    place_col = lax.broadcasted_iota(jnp.int32, (T, DOCS), 0) + offset
    seg_row = jnp.sum(jnp.where(start_col <= place_row, 1.0, 0.0), axis=0, keepdims=True)
    seg_col = jnp.sum(jnp.where(start_row <= place_col, 1.0, 0.0), axis=1, keepdims=True)
    before = jnp.sum(jnp.where(start_row <= offset - 1, 1.0, 0.0), axis=1, keepdims=True)
    last = jnp.sum(jnp.where(start_row <= offset + T - 1, 1.0, 0.0), axis=1, keepdims=True)
    same = seg_col == seg_row
    allowed = jnp.logical_and(rows >= cols, same)
    allowed_t = jnp.logical_and(cols >= rows, same)
    living_col = jnp.where(seg_col == before, 1.0, 0.0)
    ending_col = jnp.where(seg_col == last, 1.0, 0.0)
    living_row = jnp.where(seg_row == before, 1.0, 0.0)
    ending_row = jnp.where(seg_row == last, 1.0, 0.0)
    through_flag = jnp.where(last == before, 1.0, 0.0)

    dt = dt_ref[...]
    cum_dt, dt_t = jnp.zeros((T, H), f32), jnp.zeros((T, H), f32)
    for piece in split(dt, 3):
        cum_dt = cum_dt + nt(tril, piece)
        dt_t = dt_t + nt(eye, piece)
    rate = -jnp.exp(alog_ref[...])
    cum = cum_dt * rate
    alpha = jnp.exp(cum)
    beta = jnp.exp(-cum) * dt_t
    spread = jnp.concatenate(
        [
            jnp.concatenate(split(alpha, 3), axis=1),
            jnp.concatenate(split(beta, 3), axis=1),
        ],
        axis=0,
    )
    skip3 = jnp.concatenate(split(jnp.broadcast_to(skip_ref[...], (16, H)), 3), axis=1)

    bt, ct = bt_ref[...], ct_ref[...]
    eb_t = (bt.astype(f32) * ending_row).astype(bf16)
    lc_t = (ct.astype(f32) * living_row).astype(bf16)
    eb_t = jnp.concatenate([eb_t, eb_t], axis=1)
    lc_t = jnp.concatenate([lc_t, lc_t], axis=1)

    sent = []

    def send(src, dst, ssem, rsem, target):
        pltpu.make_async_remote_copy(
            src_ref=src, dst_ref=dst, send_sem=ssem, recv_sem=rsem, device_id=target, device_id_type=MESH
        ).start()

    def waiter(ref, sem):
        return pltpu.make_async_remote_copy(
            src_ref=ref, dst_ref=ref, send_sem=sem, recv_sem=sem, device_id=(dp, me), device_id_type=MESH
        )

    per = C // D
    row_k = lax.broadcasted_iota(jnp.int32, (8, H), 0)
    head_l = lax.broadcasted_iota(jnp.int32, (8, H), 1)
    mine = jnp.where(head_l // per == row_k, alpha[T - 1 : T] * through_flag, 0.0)
    head_s = lax.broadcasted_iota(jnp.int32, (H, C), 0)
    lane_s = lax.broadcasted_iota(jnp.int32, (H, C), 1)
    spots = jnp.where(head_s % per == lane_s // D, 1.0, 0.0).astype(bf16)
    tile = jnp.zeros((8, C), f32)
    for piece in split(mine, 3):
        tile = tile + nn(piece, spots)
    for q in range(RING):
        st[q] = tile[:, q * W : (q + 1) * W]

    def states(k):
        at = slice(k * C, (k + 1) * C)
        hot = one_hot(k, 3)
        wide = nn(spread, hot)
        alpha_w, beta_w = wide[:T], wide[T:]
        for copy in loads[small + 2 * k : small + 2 * k + 2]:
            copy.wait()
        g = g_ref[:, at].astype(f32)
        x = x_ref[:, at].astype(f32)
        g_hi, g_lo = split(g * alpha_w, 2)
        x_hi, x_lo = split(x * beta_w, 2)
        gh[0:T, at], gh[T : 2 * T, at] = g_hi, g_lo
        xh[0:T, at], xh[T : 2 * T, at] = x_hi, x_lo
        last_alpha = alpha_w[T - 1 : T]
        own_states = nn(eb_t, xh[:, at]) * last_alpha
        backs = nn(lc_t, gh[:, at])
        for q in range(RING):
            part = slice(q * W, (q + 1) * W)
            sa[q, k, 0:N, :] = own_states[:, part]
            sa[q, k, N : 2 * N, :] = backs[:, part]
        if k == 0:
            pl.semaphore_wait(barrier, len(greeted))
            for _, q in y_peers:
                send(st.at[q], rt.at[y], st_send.at[0], rt_recv.at[0], (dp, group * RING + q))
            sent.append((st.at[0 : RING - 1], st_send.at[0]))
            rt[y] = st[y]
        for side in (0, 1):
            half, i = slice(side * N, side * N + N), 2 * k + side
            for _, q in y_peers:
                send(sa.at[q, k, half, :], ra.at[y, k, half, :], sa_send.at[i], sa_recv.at[i], (dp, group * RING + q))
            sent.append((sa.at[0 : RING - 1, k, half, :], sa_send.at[i]))
        ra[y, k] = sa[y, k]
        rowv[0:8, at] = nn(skip3, hot)[0:8]
        rowv[8:16, at] = jnp.broadcast_to(last_alpha, (8, C))
        vecs[:, at] = jnp.broadcast_to(jnp.sum(g * x, axis=0, keepdims=True), (8, C))
        bd[:, at] = beta_w

    def within(k):
        at = slice(k * C, (k + 1) * C)
        xp, gp = xh[:, at], gh[:, at]
        z2[:, at] = nn(s_hi, xp) + nn(s_lo, xp[:T])
        z1[:, at] = nn(t_hi, gp) + nn(t_lo, gp[:T])
        scores[0] = scores[0] + nt(gp[:T], xp)
        scores[1] = scores[1] + nt(gp[T:], xp[:T])

    for k in range(CHUNKS):
        states(k)
    for target in x_peers + core_peers:
        pl.semaphore_signal(known, inc=1, device_id=target, device_id_type=MESH)
    cum_row = jnp.zeros((H, T), f32)
    for piece in split(dt, 3):
        cum_row = cum_row + nt(piece, tril)
    b32, c32 = nt(eye, bt), nt(eye, ct)
    bb, cc = b32.astype(bf16), c32.astype(bf16)
    eb = (b32 * ending_col).astype(bf16)
    lc = (c32 * living_col).astype(bf16)
    eb = jnp.concatenate([eb, eb], axis=1)
    lc = jnp.concatenate([lc, lc], axis=1)
    s_hi, s_lo = split(jnp.where(allowed, nn(cc, bt), 0.0), 2)
    t_hi, t_lo = split(jnp.where(allowed_t, nn(bb, ct), 0.0), 2)
    s_hi = jnp.concatenate([s_hi, s_hi], axis=1)
    t_hi = jnp.concatenate([t_hi, t_hi], axis=1)
    scores = [jnp.zeros((T, 2 * T), f32), jnp.zeros((T, T), f32)]
    for k in range(CHUNKS):
        within(k)
    ds = jnp.where(allowed, scores[0][:, :T] + scores[0][:, T:] + scores[1], 0.0)
    dc, db = jnp.zeros((N, T), f32), jnp.zeros((N, T), f32)
    for piece in split(ds, 2):
        dc = dc + nt(bt, piece)
        db = db + nn(ct, piece)

    def through_of(r, k):
        return rt[r, k : k + 1, :]

    def own(r, k):
        return ra[r, k, 0:N, :]

    def pulled(r, k):
        return ra[r, k, N : 2 * N, :]

    def total(k, sides=(0, 1)):
        if k == 0 and 0 in sides:
            waiter(rt.at[0 : RING - 1], rt_recv.at[0]).wait_recv()
        across = through_of(0, k)
        for i in range(1, RING):
            across = across * through_of(i, k)
        for side in sides:
            waiter(ra.at[0 : RING - 1, k, side * N : side * N + N, :], sa_recv.at[2 * k + side]).wait_recv()
            if side == 0:
                value = own(0, k)
                for i in range(1, RING):
                    value = own(i, k) + through_of(i, k) * value
            else:
                value = pulled(RING - 1, k)
                for i in range(RING - 2, -1, -1):
                    value = pulled(i, k) + through_of(i, k) * value
            s1[k, side, 0:N, :] = value
            s1[k, side, N : N + 8, :] = jnp.broadcast_to(across, (8, W))
            i = 2 * k + side
            send(s1.at[k, side], r1.at[k, side], s1_send.at[i], r1_recv.at[i], z_near[side])
            sent.append((s1.at[k, side], s1_send.at[i]))

    def pair(k, sides=(0, 1)):
        for side in sides:
            i = 2 * k + side
            waiter(r1.at[k, side], r1_recv.at[i]).wait_recv()
            across = s1[k, side, N : N + 8, :]
            s2[k, side, 0:N, :] = s1[k, side, 0:N, :] + across[0:1] * r1[k, side, 0:N, :]
            s2[k, side, N : N + 8, :] = across * r1[k, side, N : N + 8, :]
            send(s2.at[k, side, 0:N, :], r3.at[k, side], s3_send.at[i], r3_recv.at[i], z_far[side])
            send(s2.at[k, side], r2.at[k, side], s2_send.at[i], r2_recv.at[i], z_near[side])
            sent.append((r3.at[k, side], s3_send.at[i]))
            sent.append((s2.at[k, side], s2_send.at[i]))

    def give(k, sides=(0, 1)):
        for side in sides:
            half, n = slice(side * N, side * N + N), 2 * k + side
            waiter(r2.at[k, side], r2_recv.at[n]).wait_recv()
            waiter(r3.at[k, side], r3_recv.at[n]).wait_recv()
            value = r2[k, side, 0:N, :] + r2[k, side, N : N + 1, :] * r3[k, side]
            for i in range(RING) if side == 0 else range(RING - 1, -1, -1):
                sc[i, k, half, :] = value
                value = (own(i, k) if side == 0 else pulled(i, k)) + through_of(i, k) * value
            for _, q in y_peers:
                send(sc.at[q, k, half, :], rc.at[y, k, half, :], sc_send.at[n], sc_recv.at[n], (dp, group * RING + q))
            sent.append((sc.at[0 : RING - 1, k, half, :], sc_send.at[n]))
            rc[y, k, half, :] = sc[y, k, half, :]

    sums = [jnp.zeros((H, 2 * T), f32), jnp.zeros((H, 2 * T), f32), jnp.zeros((2 * N, 2 * T), f32), jnp.zeros((2 * N, 2 * T), f32), jnp.zeros((H, 8), f32)]

    def finish(k):
        at = slice(k * C, (k + 1) * C)
        hot = one_hot(k, 1)
        waiter(rc.at[0 : RING - 1, k, 0:N, :], sc_recv.at[2 * k]).wait_recv()
        state = jnp.concatenate([rc[q, k, 0:N, :] for q in range(RING)], axis=1)
        hh = jnp.concatenate(split(state, 2), axis=0)
        gp, xp = gh[:, at], xh[:, at]
        z2_w = z2[:, at] + nn(lc, hh)
        p2 = z2_w * (gp[:T].astype(f32) + gp[T:].astype(f32))
        sums[1] = sums[1] + nt(hot, jnp.concatenate(split(p2, 2), axis=0))
        mine = jnp.concatenate([sa[q, k, 0:N, :] for q in range(RING)], axis=1)
        last_alpha = rowv[8:9, at]
        mine = mine + last_alpha * through_flag * state
        waiter(rc.at[0 : RING - 1, k, N : 2 * N, :], sc_recv.at[2 * k + 1]).wait_recv()
        later = jnp.concatenate([rc[q, k, N : 2 * N, :] for q in range(RING)], axis=1)
        leaving = jnp.sum(later * mine, axis=0, keepdims=True)
        first_row = lax.broadcasted_iota(jnp.int32, (8, C), 0) == 0
        vec = jnp.where(first_row, leaving, vecs[:, at])
        fh = jnp.concatenate(split(later * last_alpha, 2), axis=0)
        z1_w = z1[:, at] + nn(eb, fh)
        p1 = z1_w * (xp[:T].astype(f32) + xp[T:].astype(f32))
        sums[0] = sums[0] + nt(hot, jnp.concatenate(split(p1, 2), axis=0))
        for piece in split(vec, 3):
            sums[4] = sums[4] + nt(hot, piece)

        def remainder():
            dx_ref[:, at] = (bd[:, at] * z1_w + rowv[0:1, at] * g_ref[:, at].astype(f32)).astype(bf16)
            sums[2] = sums[2] + nt(hh, gp)
            sums[3] = sums[3] + nt(fh, xp)

        if k + 1 < CHUNKS:
            remainder()
        else:
            put_off.append(remainder)

    put_off = []
    steps = {"total": total, "pair": pair, "give": give, "finish": finish}
    for name, k, *sides in ORDER:
        steps[name](k, *([sides] if sides else []))

    col_q = sums[0][:, :T] + sums[0][:, T:]
    row_q = sums[1][:, :T] + sums[1][:, T:]
    d_cum = row_q - col_q
    d_end, d_skip = sums[4][:, 0:1], sums[4][:, 1:2]
    rate_c = jnp.sum(jnp.where(head_r == head_c, jnp.broadcast_to(rate, (H, H)), 0.0), axis=1, keepdims=True)
    at_end = cols[:H] == T - 1
    d_alog = rate_c * jnp.sum((d_cum + jnp.where(at_end, d_end, 0.0)) * cum_row, axis=1, keepdims=True)
    part = jnp.where(rows[:H] == cols[:H], d_alog, jnp.where(rows[:H] + H == cols[:H], d_skip, 0.0))
    part = jnp.sum(part, axis=0, keepdims=True)

    stages = ((line, n_line, line_peers), (plane, n_plane, plane_peers))
    pl.semaphore_wait(known, len(x_peers) + len(core_peers))
    for s, (mine, count, peers) in enumerate(stages):
        ar[s, mine] = part
        for target in peers:
            send(ar.at[s, mine], ar.at[s, mine], ar_send.at[s], ar_recv.at[s], target)
        if s == 0:
            for work in put_off:
                work()
            acc = sums[2][:N] + sums[2][N:]
            dc_ref[...] = (dc + living_row * (acc[:, :T] + acc[:, T:])).astype(bf16)
            acc = sums[3][:N] + sums[3][N:]
            db_ref[...] = (db + ending_row * (acc[:, :T] + acc[:, T:])).astype(bf16)
            d_log = jnp.zeros((H, T), f32) + d_end
            for piece in split(d_cum, 3):
                d_log = d_log + nn(piece, tril)
            dstep_ref[...] = col_q / dt + d_log * rate_c
            for ref, sem in sent:
                waiter(ref, sem).wait_send()
        if peers:
            waiter(ar.at[s, 0 : count - 1], ar_recv.at[s]).wait_recv()
        part = ar[s, 0]
        for i in range(1, count):
            part = part + ar[s, i]
    dalog_ref[...] = part[:, :H]
    dskip_ref[...] = part[:, H : 2 * H]
    for s, (mine, count, peers) in enumerate(stages):
        if peers:
            waiter(ar.at[s, 0 : count - 1], ar_send.at[s]).wait_send()


def write_out(count, *refs):
    copies = [pltpu.make_async_copy(refs[i], refs[count + i], refs[-1].at[i]) for i in range(count)]
    for copy in copies:
        copy.start()
    for copy in copies:
        copy.wait()


def per_device(n_dp, n_ctx, n_z, inputs, b_proj, c_proj, step_sizes, a_log, skip_gain, doc_lengths, grad_out):
    T, H, N = inputs.shape[1], a_log.shape[0], b_proj.shape[2]
    D, DOCS = inputs.shape[2] // H, doc_lengths.shape[1]
    HD = H * D
    K, W = CHUNKS, HD // (RING * CHUNKS)
    assert 4 * RING * T >= MOST_DOC
    n_x = n_ctx // (n_z * RING)
    slots = max(RING * n_dp * n_x, 2 * n_z)
    dims = (n_dp, n_ctx, n_z, T, H, D, N, DOCS)
    vmem, hbm = pl.BlockSpec(memory_space=pltpu.VMEM), pl.BlockSpec(memory_space=pltpu.HBM)
    dma = pltpu.SemaphoreType.DMA
    outs = (
        jax.ShapeDtypeStruct((T, HD), bf16),
        jax.ShapeDtypeStruct((N, T), bf16),
        jax.ShapeDtypeStruct((N, T), bf16),
        jax.ShapeDtypeStruct((H, T), f32),
        jax.ShapeDtypeStruct((1, H), f32),
        jax.ShapeDtypeStruct((1, H), f32),
    )
    results = pl.pallas_call(
        functools.partial(kernel, dims),
        out_shape=outs,
        in_specs=[hbm] * 8,
        out_specs=(vmem,) * 6,
        scratch_shapes=[
            pltpu.VMEM((T, HD), bf16),
            pltpu.VMEM((T, HD), bf16),
            pltpu.VMEM((N, T), bf16),
            pltpu.VMEM((N, T), bf16),
            pltpu.VMEM((H, T), f32),
            pltpu.VMEM((1, H), f32),
            pltpu.VMEM((1, H), f32),
            pltpu.VMEM((1, DOCS), jnp.int32),
            pltpu.VMEM((2 * T, HD), bf16),
            pltpu.VMEM((2 * T, HD), bf16),
            pltpu.VMEM((T, HD), f32),
            pltpu.VMEM((T, HD), f32),
            pltpu.VMEM((T, HD), f32),
            pltpu.VMEM((16, HD), f32),
            pltpu.VMEM((8, HD), f32),
            pltpu.VMEM((RING, K, 2 * N, W), f32),
            pltpu.VMEM((RING, K, 2 * N, W), f32),
            pltpu.VMEM((RING, 8, W), f32),
            pltpu.VMEM((RING, 8, W), f32),
            pltpu.VMEM((K, 2, N + 8, W), f32),
            pltpu.VMEM((K, 2, N + 8, W), f32),
            pltpu.VMEM((K, 2, N + 8, W), f32),
            pltpu.VMEM((K, 2, N + 8, W), f32),
            pltpu.VMEM((K, 2, N, W), f32),
            pltpu.VMEM((RING, K, 2 * N, W), f32),
            pltpu.VMEM((RING, K, 2 * N, W), f32),
            pltpu.VMEM((2, slots, 1, 128), f32),
            dma((6 + 2 * K,)),
            *(dma((2 * K,)) for _ in range(10)),
            dma((1,)),
            dma((1,)),
            dma((2,)),
            dma((2,)),
            pltpu.SemaphoreType.REGULAR,
        ],
        compiler_params=pltpu.CompilerParams(
            collective_id=0, has_side_effects=True, vmem_limit_bytes=40960 << 10
        ),
        name="ssd_backward",
    )(
        *(
            pltpu.with_memory_space_constraint(a, pltpu.HBM)
            for a in (
                inputs[0], grad_out[0], b_proj[0].T, c_proj[0].T, step_sizes[0],
                a_log[None], skip_gain[None], doc_lengths,
            )
        )
    )
    dx, db, dc, dstep, dalog, dskip = pl.pallas_call(
        functools.partial(write_out, len(outs)),
        out_shape=outs,
        in_specs=[vmem] * 6,
        out_specs=(hbm,) * 6,
        scratch_shapes=[dma((len(outs),))],
        compiler_params=pltpu.CompilerParams(vmem_limit_bytes=1 << 20),
        name="write_out",
    )(*results)
    return dx[None], db.T[None], dc.T[None], dstep[None], dalog[0], dskip[0]


def solution(mesh):
    tokens, heads = P("dp", "ctx", None), P("dp", None, "ctx")
    n_dp, n_ctx = mesh.shape["dp"], mesh.shape["ctx"]
    n_z = min(8, n_ctx // RING)
    return jax.shard_map(
        functools.partial(per_device, n_dp, n_ctx, n_z),
        mesh=mesh,
        in_specs=(tokens, tokens, tokens, heads, P(), P(), P("dp", None), tokens),
        out_specs=(tokens, tokens, tokens, heads, P(), P()),
        check_vma=False,
    )
```
